32 devices in a mesh: seq: 8 (over z, core), mlp: 4 (over y, x).
Axes of the slice: x: 2, y: 2, z: 4, core: 2. Of those that a mesh axis runs over, the one named last changes fastest.
Arguments:
- layer_input: bfloat16 [3072, 5120], P('seq')
- attention_gain: bfloat16 [5120], replicated, may hold values from 0.099609375 to 1.8984375
- feedforward_gain: bfloat16 [5120], replicated, may hold values from 0.099609375 to 1.8984375
- query_weight: bfloat16 [5120, 4096], P('seq', 'mlp'), may hold values from -0.078125 to 0.078125
- key_weight: bfloat16 [5120, 1024], P('seq'), may hold values from -0.078125 to 0.078125
- value_weight: bfloat16 [5120, 1024], P('seq'), may hold values from -0.078125 to 0.078125
- out_weight: bfloat16 [4096, 5120], P('mlp', 'seq'), may hold values from -0.09375 to 0.09375
- gate_weight: bfloat16 [5120, 6912], P('seq', 'mlp'), may hold values from -0.078125 to 0.078125
- up_weight: bfloat16 [5120, 6912], P('seq', 'mlp'), may hold values from -0.078125 to 0.078125
- down_weight: bfloat16 [6912, 5120], P('mlp', 'seq'), may hold values from -0.078125 to 0.078125
- query_bias: bfloat16 [4096], P('mlp'), may hold values from -5 to 5
- key_bias: bfloat16 [1024], replicated, may hold values from -250 to 250
- value_bias: bfloat16 [1024], replicated, may hold values from -5 to 5
- doc_lengths: int32 [4], replicated, may hold values from 1 to 1536, 3072 in all
- piece_order: int32 [16], replicated, may hold values from 0 to 15, each once
- cache_page: int32 [16], replicated, may hold values from 0 to 15, each once
Outputs:
- layer_output: bfloat16 [3072, 5120], P(('seq', 'mlp'))
- kv_cache: bfloat16 [3072, 2048], P('seq', 'mlp')
The draws below stay inside these ranges and needn't reach their ends.
Inputs may be any that keep to these rules, and one draw needn't show every extreme that they name: `doc_lengths`: the lengths sum to 3072, the longest is exactly 1536. `piece_order`: each piece number appears once. `cache_page`: each page number appears once.
All inputs are finite; a program needn't handle non-finite values.
Results may differ from the reference program's by a relative error of at most 0.0096.
Values may be sent and summed in bfloat16 or wider, within the bound.
No kernel may reach another device: no remote copies, remote signals or barrier semaphores. Data moves between devices by JAX's collectives and lax.ppermute only.
A program may use at most 192 MiB of HBM per device.

```python
import math
import jax
import jax.numpy as jnp
import numpy as np
from jax import lax

D = 5120
QH = 32
KVH = 8
HD = 128
FF = 6912
TOK_SEQ = 384
PIECES_DEV = 2
TOKENS = 3072
NPIECE = 16
PROMPT_MAX = 1536
NDOCS = 4
N_MLP = 4


def draw_layer_input(key, part):
    row_key, col_key, body_key = jax.random.split(key, 3)
    col_scale = jnp.exp(jax.random.uniform(col_key, (1, D), jnp.float32, math.log(0.3), math.log(3.0)))
    row_scale = jnp.exp(jax.random.uniform(row_key, (TOKENS, 1), jnp.float32, math.log(0.5), math.log(5.0)))
    base_vals = jax.random.normal(body_key, (TOKENS, D), jnp.float32)
    return (base_vals * row_scale * col_scale).astype(jnp.bfloat16)


def draw_key_bias(key, part):
    noise_key = jax.random.fold_in(key, 0)
    noise_vals = jnp.clip(jax.random.normal(noise_key, (KVH, 2, HD // 2), jnp.float32), -6.0, 6.0)
    return noise_vals.reshape(KVH * HD).astype(jnp.bfloat16)


def block_levels(rng, shape, cuts, least, largest):
    def one(dim, blocks):
        steps = jax.random.uniform(jax.random.fold_in(jax.random.fold_in(rng, 6), dim), (blocks,), jnp.float32, least / len(cuts), largest / len(cuts))
        return jnp.repeat(jnp.exp(steps), shape[dim] // blocks).reshape((-1,) + (1,) * (len(shape) - dim - 1))

    gain = one(*cuts[0])
    for cut in cuts[1:]:
        gain = gain * one(*cut)
    return gain


def split_up(number_of, total, bound, lean):
    portions = [(1 << 20) // math.isqrt(rank ** lean) + 1 for rank in range(2, number_of + 1)]
    rest, given = total - bound - (number_of - 1), [1] * (number_of - 1)
    while rest > 0:
        candidates = [i for i in range(number_of - 1) if given[i] < bound]
        whole, remaining = sum([portions[i] for i in candidates]), rest
        for i in candidates:
            addition = min(bound - given[i], max(1, remaining * portions[i] // whole), rest)
            given[i] = given[i] + addition
            rest = rest - addition
    return np.array([bound] + given)


def ragged(rng, number_of, total, reach, slope):
    if number_of == 2:
        one = jax.random.randint(rng, (), max(1, total - reach), min(reach, total - 1) + 1)
        return jnp.stack([one, total - one])
    sizes = jnp.asarray(split_up(number_of, total, reach, slope), jnp.int32)
    couples = (number_of - 1) // 2
    donor, taker = sizes[1:1 + 2 * couples:2], sizes[2:2 + 2 * couples:2]
    room = jnp.minimum(donor - 1, reach - taker)
    moved = jax.random.randint(jax.random.fold_in(rng, 1), (couples,), 0, 1 << 20) % (room + 1)
    sizes = sizes.at[1:1 + 2 * couples:2].set(donor - moved).at[2:2 + 2 * couples:2].set(taker + moved)
    return sizes[jax.random.permutation(jax.random.fold_in(rng, 2), number_of)]


def normal_values(own_key, shape, deviation, bound, cuts=(), kind=jnp.bfloat16):
    values = deviation * jax.random.normal(own_key, shape, jnp.float32)
    if cuts:
        values = values * block_levels(own_key, shape, cuts, -0.22, 0.18)
    return jnp.clip(values, -bound, bound).astype(kind)


def setup_inputs(seed: int = 0) -> dict:
    key_of = jax.random.split(jax.random.key(seed), 17)
    return {
        "layer_input": draw_layer_input(jax.random.fold_in(key_of[16], 71), 0),
        "attention_gain": jnp.clip(1.0 + 0.18 * jax.random.normal(key_of[1], (D,), jnp.float32), 0.099609375, 1.8984375).astype(jnp.bfloat16),
        "feedforward_gain": jnp.clip(1.0 + 0.18 * jax.random.normal(key_of[2], (D,), jnp.float32), 0.099609375, 1.8984375).astype(jnp.bfloat16),
        "query_weight": normal_values(key_of[3], (D, QH * HD), D ** -0.5, 0.078125, ((0, 8), (1, 4))),
        "key_weight": normal_values(key_of[4], (D, KVH * HD), D ** -0.5, 0.078125, ((0, 8),)),
        "value_weight": normal_values(key_of[5], (D, KVH * HD), D ** -0.5, 0.078125, ((0, 8),)),
        "out_weight": normal_values(key_of[6], (QH * HD, D), (QH * HD) ** -0.5, 0.09375, ((0, 4), (1, 8))),
        "gate_weight": normal_values(key_of[7], (D, FF), D ** -0.5, 0.078125, ((0, 8), (1, 4))),
        "up_weight": normal_values(key_of[8], (D, FF), D ** -0.5, 0.078125, ((0, 8), (1, 4))),
        "down_weight": normal_values(key_of[9], (FF, D), FF ** -0.5, 0.078125, ((0, 4), (1, 8))),
        "query_bias": normal_values(key_of[10], (QH * HD,), 1.0, 5.0, ((0, 4),)),
        "key_bias": draw_key_bias(jax.random.fold_in(key_of[16], 71), 0),
        "value_bias": normal_values(key_of[12], (KVH * HD,), 1.0, 5.0),
        "doc_lengths": ragged(key_of[13], NDOCS, TOKENS, PROMPT_MAX, 2).astype(jnp.int32),
        "piece_order": jax.random.permutation(key_of[14], NPIECE).astype(jnp.int32),
        "cache_page": jax.random.permutation(key_of[15], NPIECE).astype(jnp.int32),
    }


rope_base = 1000000.0
norm_eps = 1e-06
far_below = -1e+30

def rms_scale(values, gain_vec):
    mean_sq = lax.optimization_barrier(jnp.mean(values * values, axis=-1, keepdims=True))
    return values * lax.rsqrt(mean_sq + norm_eps) * gain_vec.astype(jnp.float32)

def rope_tables(position, head_dim):
    half_dim = head_dim // 2
    inverse_freq = jnp.power(jnp.float32(rope_base), -2.0 * jnp.arange(half_dim, dtype=jnp.float32) / head_dim)
    angles = position.astype(jnp.float32)[:, None] * inverse_freq[None, :]
    return (jnp.cos(angles), jnp.sin(angles))

def rotate(values, cosine, sine_part, head_count):
    row_count = values.shape[0]
    halves = values.reshape(row_count, head_count, 2, -1)
    lower_half = halves[:, :, 0, :]
    upper_half = halves[:, :, 1, :]
    cos_wide = cosine[:, None, :]
    sin_wide = sine_part[:, None, :]
    new_lower = lower_half * cos_wide - upper_half * sin_wide
    new_upper = upper_half * cos_wide + lower_half * sin_wide
    return jnp.stack([new_lower, new_upper], axis=2).reshape(row_count, -1)

def lookup(small_table, indices):
    matches = indices[:, None] == jnp.arange(small_table.shape[0], dtype=jnp.int32)[None, :]
    return lax.optimization_barrier(jnp.sum(jnp.where(matches, small_table[None, :], 0), axis=1)).astype(jnp.int32)

def stream_segment(doc_lengths, piece_order, row_ids, piece_len):
    stream = lookup(piece_order, row_ids // piece_len) * piece_len + row_ids % piece_len
    doc_ends = jnp.cumsum(doc_lengths).astype(jnp.int32)
    segment = lax.optimization_barrier(jnp.sum((stream[:, None] >= doc_ends[None, :]).astype(jnp.int32), axis=1)).astype(jnp.int32)
    return (stream, segment)

def stream_layout(doc_lengths, piece_order, row_ids, piece_len):
    stream, segment = stream_segment(doc_lengths, piece_order, row_ids, piece_len)
    doc_ends = jnp.cumsum(doc_lengths).astype(jnp.int32)
    doc_first = lookup((doc_ends - doc_lengths).astype(jnp.int32), segment)
    return (stream, segment, (stream - doc_first).astype(jnp.int32))

def reference(layer_input, attention_gain, feedforward_gain, query_weight, key_weight, value_weight, out_weight, gate_weight, up_weight, down_weight, query_bias, key_bias, value_bias, doc_lengths, piece_order, cache_page):
    tokens = layer_input.shape[0]
    piece_len = TOK_SEQ // PIECES_DEV
    row_ids = jnp.arange(tokens, dtype=jnp.int32)
    stream, segment, position = stream_layout(doc_lengths, piece_order, row_ids, piece_len)
    cosine, sine_part = rope_tables(position, HD)
    residual = layer_input.astype(jnp.float32)
    normed = rms_scale(residual, attention_gain).astype(jnp.bfloat16)
    query = jnp.dot(normed, query_weight, preferred_element_type=jnp.float32) + query_bias.astype(jnp.float32)
    key_act = jnp.dot(normed, key_weight, preferred_element_type=jnp.float32) + key_bias.astype(jnp.float32)
    value_act = jnp.dot(normed, value_weight, preferred_element_type=jnp.float32) + value_bias.astype(jnp.float32)
    query_rot = rotate(query, cosine, sine_part, QH).astype(jnp.bfloat16)
    key_rot = rotate(key_act, cosine, sine_part, KVH).astype(jnp.bfloat16)
    value_b = value_act.astype(jnp.bfloat16)
    per_group = QH // KVH
    query_heads = query_rot.reshape(tokens, QH, HD).transpose(1, 0, 2)
    key_heads = key_rot.reshape(tokens, KVH, HD).transpose(1, 0, 2)
    value_heads = value_b.reshape(tokens, KVH, HD).transpose(1, 0, 2)
    allowed = (segment[:, None] == segment[None, :]) & (stream[None, :] <= stream[:, None])

    def one_head(head_idx):
        query_one = query_heads[head_idx]
        key_one = key_heads[head_idx // per_group]
        value_one = value_heads[head_idx // per_group]
        scores = jnp.dot(query_one, key_one.T, preferred_element_type=jnp.float32) / math.sqrt(HD)
        row_top = lax.optimization_barrier(jnp.max(jnp.where(allowed, scores, far_below), axis=1, keepdims=True))
        weights = jnp.where(allowed, jnp.exp(scores - row_top), 0.0)
        row_total = lax.optimization_barrier(jnp.sum(weights, axis=1, keepdims=True))
        mixed_one = jnp.dot(weights.astype(jnp.bfloat16), value_one, preferred_element_type=jnp.float32) / row_total
        return mixed_one.astype(jnp.bfloat16)
    head_out = lax.map(one_head, jnp.arange(QH, dtype=jnp.int32))
    mixed = head_out.transpose(1, 0, 2).reshape(tokens, QH * HD)
    head_share = QH * HD // N_MLP
    attn_sum = jnp.zeros((tokens, D), jnp.float32)
    for group_idx in range(N_MLP):
        group_part = jnp.dot(mixed[:, group_idx * head_share:(group_idx + 1) * head_share], out_weight[group_idx * head_share:(group_idx + 1) * head_share], preferred_element_type=jnp.float32)
        attn_sum = attn_sum + group_part.astype(jnp.bfloat16).astype(jnp.float32)
    residual = residual + attn_sum
    normed2 = rms_scale(residual, feedforward_gain).astype(jnp.bfloat16)
    gate_act = jnp.dot(normed2, gate_weight, preferred_element_type=jnp.float32)
    up_act = jnp.dot(normed2, up_weight, preferred_element_type=jnp.float32)
    hidden_units = (jax.nn.silu(gate_act) * up_act).astype(jnp.bfloat16)
    unit_share = FF // N_MLP
    down_sum = jnp.zeros((tokens, D), jnp.float32)
    for group_idx in range(N_MLP):
        group_part = jnp.dot(hidden_units[:, group_idx * unit_share:(group_idx + 1) * unit_share], down_weight[group_idx * unit_share:(group_idx + 1) * unit_share], preferred_element_type=jnp.float32)
        down_sum = down_sum + group_part.astype(jnp.bfloat16).astype(jnp.float32)
    layer_output = (residual + down_sum).astype(jnp.bfloat16)
    joined = jnp.stack([key_rot.reshape(tokens, KVH, HD), value_b.reshape(tokens, KVH, HD)], axis=2).reshape(tokens, 2 * KVH * HD)
    piece_total = tokens // piece_len
    pieces = jnp.arange(piece_total, dtype=jnp.int32)
    stream_of_page = jnp.zeros((piece_total,), jnp.int32).at[cache_page].set(pieces)
    slot_of_stream = jnp.zeros((piece_total,), jnp.int32).at[piece_order].set(pieces)
    source_piece = slot_of_stream[stream_of_page]
    kv_cache = joined.reshape(piece_total, piece_len, 2 * KVH * HD)[source_piece].reshape(tokens, 2 * KVH * HD)
    return (layer_output, kv_cache)
```

```python
import math

import jax
import jax.numpy as jnp
from jax import lax
from jax.experimental import pallas as pl
from jax.experimental.pallas import tpu as pltpu
from jax.sharding import PartitionSpec as P

KVH = 8
HD = 128
PIECES_DEV = 2
CORES = 2

rope_base = 1000000.0
norm_eps = 1e-06
far_below = -1e30
start_top = -1e29
F32 = jnp.float32
BF16 = jnp.bfloat16


def rope_tables(position, head_dim):
    half_dim = head_dim // 2
    inverse_freq = jnp.power(
        jnp.float32(rope_base), -2.0 * jnp.arange(half_dim, dtype=jnp.float32) / head_dim
    )
    angles = position.astype(jnp.float32)[:, None] * inverse_freq[None, :]
    return (jnp.cos(angles), jnp.sin(angles))


def rotate(values, cosine, sine_part, head_count):
    row_count = values.shape[0]
    halves = values.reshape(row_count, head_count, 2, -1)
    lower_half = halves[:, :, 0, :]
    upper_half = halves[:, :, 1, :]
    cos_wide = cosine[:, None, :]
    sin_wide = sine_part[:, None, :]
    new_lower = lower_half * cos_wide - upper_half * sin_wide
    new_upper = upper_half * cos_wide + lower_half * sin_wide
    return jnp.stack([new_lower, new_upper], axis=2).reshape(row_count, -1)


def lookup(small_table, indices):
    matches = indices[:, None] == jnp.arange(small_table.shape[0], dtype=jnp.int32)[None, :]
    return jnp.sum(jnp.where(matches, small_table[None, :], 0), axis=1)


def attend_kernel(count, active, piece_stream, q_ref, k_ref, v_ref, lo_ref, hi_ref, o_ref, acc_ref):
    chunk = pl.program_id(1)
    piece_len = k_ref.shape[0] // piece_stream.shape[0]
    rows = q_ref.shape[1]
    per_kv = q_ref.shape[2] // HD
    scale = 1.0 / math.sqrt(HD)
    q = jnp.concatenate([q_ref[0, :, i * HD : (i + 1) * HD] for i in range(per_kv)], axis=0)
    lo = lo_ref[0]
    hi = hi_ref[0]
    acc_ref[...] = jnp.zeros_like(acc_ref)

    def step(i, carry):
        top, total = carry
        piece = active[chunk, i]
        first = pl.multiple_of(piece * piece_len, piece_len)
        k = k_ref[pl.ds(first, piece_len), :]
        v = v_ref[pl.ds(first, piece_len), :]
        s = lax.dot_general(k, q, (((1,), (1,)), ((), ())), preferred_element_type=F32) * scale
        stream = piece_stream[piece] * piece_len + lax.broadcasted_iota(jnp.int32, s.shape, 0)
        s = jnp.where((stream >= lo) & (stream <= hi), s, far_below)
        new_top = jnp.maximum(top, jnp.max(s, axis=0, keepdims=True))
        w = jnp.exp(s - new_top)
        fade = jnp.exp(top - new_top)
        total = total * fade + jnp.sum(w, axis=0, keepdims=True)
        part = lax.dot_general(v, w.astype(BF16), (((0,), (0,)), ((), ())), preferred_element_type=F32)
        acc_ref[...] = acc_ref[...] * fade + part
        return (new_top, total)

    top = jnp.full((1, q.shape[0]), start_top, F32)
    total = jnp.zeros((1, q.shape[0]), F32)
    top, total = lax.fori_loop(0, count[chunk], step, (top, total))
    out = (acc_ref[...] / total).T.astype(BF16)
    for i in range(per_kv):
        o_ref[0, :, i * HD : (i + 1) * HD] = out[i * rows : (i + 1) * rows]


def attend(query, kv_rows, lo, hi, piece_stream, kv_heads):
    chunks, rows, width = query.shape
    per_kv = width // (kv_heads * HD)
    keys = kv_rows.shape[0]
    pieces = piece_stream.shape[0]
    piece_len = keys // pieces
    first = piece_stream[None, None, :] * piece_len
    touch = jnp.any(
        (lo[:, :, None] <= first + piece_len - 1) & (hi[:, :, None] >= first), axis=1
    ).astype(jnp.int32)
    place = jnp.cumsum(touch, axis=1) - 1
    ids = jnp.arange(pieces, dtype=jnp.int32)
    active = jnp.sum(
        jnp.where((touch[:, :, None] > 0) & (place[:, :, None] == ids), ids[None, :, None], 0), axis=1
    ).astype(jnp.int32)
    count = jnp.sum(touch, axis=1).astype(jnp.int32)
    lo_wide = jnp.tile(lo, (1, per_kv))[:, None, :]
    hi_wide = jnp.tile(hi, (1, per_kv))[:, None, :]
    return pl.pallas_call(
        attend_kernel,
        grid_spec=pltpu.PrefetchScalarGridSpec(
            num_scalar_prefetch=3,
            grid=(kv_heads, chunks),
            in_specs=[
                pl.BlockSpec((1, rows, per_kv * HD), lambda g, h, *_: (h, 0, g)),
                pl.BlockSpec((keys, HD), lambda g, h, *_: (0, 2 * g)),
                pl.BlockSpec((keys, HD), lambda g, h, *_: (0, 2 * g + 1)),
                pl.BlockSpec((1, 1, rows * per_kv), lambda g, h, *_: (h, 0, 0)),
                pl.BlockSpec((1, 1, rows * per_kv), lambda g, h, *_: (h, 0, 0)),
            ],
            out_specs=pl.BlockSpec((1, rows, per_kv * HD), lambda g, h, *_: (h, 0, g)),
            scratch_shapes=[pltpu.VMEM((HD, rows * per_kv), F32)],
        ),
        out_shape=jax.ShapeDtypeStruct(query.shape, BF16),
        compiler_params=pltpu.CompilerParams(vmem_limit_bytes=32 * 2**20),
    )(count, active, piece_stream, query, kv_rows, kv_rows, lo_wide, hi_wide)


def shards(
    layer_input,
    attention_gain,
    feedforward_gain,
    query_weight,
    key_weight,
    value_weight,
    out_weight,
    gate_weight,
    up_weight,
    down_weight,
    query_bias,
    key_bias,
    value_bias,
    doc_lengths,
    piece_order,
    cache_page,
):
    seq_count = lax.axis_size("seq")
    mlp_count = lax.axis_size("mlp")
    seq_rank = lax.axis_index("seq")
    mlp_rank = lax.axis_index("mlp")
    planes = seq_count // CORES
    plane = seq_rank // CORES
    core = seq_rank % CORES
    rows, width = layer_input.shape
    dz = width // planes
    ds = width // seq_count
    share = rows // mlp_count
    chunks = 2 if share % 32 == 0 else 1
    sub = share // chunks
    crows = mlp_count * sub
    piece_len = rows // PIECES_DEV

    def move(x, pairs):
        return lax.ppermute(
            x, "seq", [(a * CORES + e, b * CORES + e) for a, b in pairs for e in range(CORES)]
        )

    def sibling(x):
        return lax.ppermute(
            x, "seq", [(a * CORES + e, a * CORES + 1 - e) for a in range(planes) for e in range(CORES)]
        )

    def line_gather(x):
        ups, downs = [x], [x]
        for t in range(1, planes):
            ups.append(move(ups[-1], [(i, i + 1) for i in range(t - 1, planes - 1)]))
            downs.append(move(downs[-1], [(i, i - 1) for i in range(1, planes - t + 1)]))
        return [x] + [ups[k] + downs[planes - k] for k in range(1, planes)]

    def line_scatter(parts):
        up = down = None
        for t in range(1, planes):
            send_up, send_down = parts[t], parts[planes - t]
            if up is not None:
                send_up = (send_up.astype(F32) + up.astype(F32)).astype(BF16)
                send_down = (send_down.astype(F32) + down.astype(F32)).astype(BF16)
            up = move(send_up, [(i, i + 1) for i in range(0, min(t, planes - 1))])
            down = move(send_down, [(i, i - 1) for i in range(max(1, planes - t), planes)])
        return parts[0].astype(F32) + up.astype(F32) + down.astype(F32)

    def swap_halves(x):
        return jnp.where(core == 0, x, jnp.concatenate([x[..., ds:], x[..., :ds]], axis=-1))

    kv_cols = max(HD, KVH * HD // mlp_count)
    kv_first = mlp_rank * KVH // mlp_count * HD
    qkv_weight = jnp.concatenate(
        [
            lax.dynamic_slice_in_dim(key_weight, kv_first, kv_cols, 1),
            lax.dynamic_slice_in_dim(value_weight, kv_first, kv_cols, 1),
            query_weight,
        ],
        axis=1,
    )
    qkv_bias = jnp.concatenate(
        [
            lax.dynamic_slice_in_dim(key_bias, kv_first, kv_cols, 0),
            lax.dynamic_slice_in_dim(value_bias, kv_first, kv_cols, 0),
            query_bias,
        ]
    ).astype(F32)
    qkv_weight = lax.all_gather(qkv_weight, "seq", axis=0, tiled=True)

    units = gate_weight.shape[1]
    whole = units // HD * HD
    glu_own = jnp.concatenate(
        [gate_weight[:, :whole], up_weight[:, :whole], gate_weight[:, whole:], up_weight[:, whole:]],
        axis=1,
    )
    glu_weight = jnp.concatenate([glu_own, sibling(glu_own)], axis=0)
    out_wide = jnp.concatenate([out_weight, sibling(out_weight)], axis=1)
    down_wide = jnp.concatenate([down_weight, sibling(down_weight)], axis=1)

    def regroup(x):
        return jnp.swapaxes(x.reshape((mlp_count, chunks, sub) + x.shape[1:]), 0, 1).reshape(x.shape)

    def ungroup(x):
        return jnp.swapaxes(x.reshape((chunks, mlp_count, sub) + x.shape[1:]), 0, 1).reshape(x.shape)

    own_share = lax.dynamic_slice_in_dim(layer_input, mlp_rank * share, share, 0)
    lane_parts = []
    for k in range(planes):
        part = lax.dynamic_slice_in_dim(own_share, (plane + k) % planes * dz, dz, 1)
        if k:
            part = move(part, [(i, (i + k) % planes) for i in range(planes)])
        lane_parts.append(part)
    lane_input = swap_halves(jnp.stack(lane_parts, axis=0))
    lane_input = lane_input.reshape(planes, chunks, sub, dz)
    gain_lane = swap_halves(lax.dynamic_slice_in_dim(feedforward_gain, plane * dz, dz, 0)).astype(F32)

    row_ids = seq_rank * rows + regroup(jnp.arange(rows, dtype=jnp.int32))
    stream = lookup(piece_order, row_ids // piece_len) * piece_len + row_ids % piece_len
    doc_ends = jnp.cumsum(doc_lengths)
    segment = jnp.sum((stream[:, None] >= doc_ends[None, :]).astype(jnp.int32), axis=1)
    doc_first = lookup(doc_ends - doc_lengths, segment)
    cosine, sine_part = rope_tables(stream - doc_first, HD)

    x = regroup(layer_input).astype(F32)
    mean_sq = jnp.mean(x * x, axis=-1, keepdims=True)
    normed = (x * lax.rsqrt(mean_sq + norm_eps) * attention_gain.astype(F32)).astype(BF16)
    qkv = jnp.dot(normed, qkv_weight, preferred_element_type=F32) + qkv_bias
    kv_heads = kv_cols // HD
    query_heads = query_weight.shape[1] // HD
    key_rot = rotate(qkv[:, :kv_cols], cosine, sine_part, kv_heads).astype(BF16)
    value_b = qkv[:, kv_cols : 2 * kv_cols].astype(BF16)
    query_rot = rotate(qkv[:, 2 * kv_cols :], cosine, sine_part, query_heads).astype(BF16)
    joined = jnp.stack(
        [key_rot.reshape(rows, kv_heads, HD), value_b.reshape(rows, kv_heads, HD)], axis=2
    ).reshape(rows, 2 * kv_cols)
    kv_rows = lax.all_gather(ungroup(joined), "seq", axis=0, tiled=True)

    own_cols = KVH * HD // mlp_count
    cache_width = 2 * own_cols
    offset = mlp_rank % max(1, HD // own_cols) * cache_width
    pieces = jnp.arange(piece_order.shape[0], dtype=jnp.int32)
    pages = []
    for p in range(PIECES_DEV):
        stream_piece = jnp.sum(jnp.where(cache_page == seq_rank * PIECES_DEV + p, pieces, 0))
        source = jnp.sum(jnp.where(piece_order == stream_piece, pieces, 0))
        pages.append(lax.dynamic_slice(kv_rows, (source * piece_len, offset), (piece_len, cache_width)))
    kv_cache = jnp.concatenate(pages, axis=0)

    mixed = attend(
        query_rot.reshape(chunks, crows, query_heads * HD),
        kv_rows,
        doc_first.reshape(chunks, crows),
        stream.reshape(chunks, crows),
        piece_order,
        kv_heads,
    )

    def by_share(slots):
        return jnp.stack([v.reshape(mlp_count, sub, -1) for v in slots], axis=1).reshape(
            mlp_count * planes * sub, -1
        )

    finals = []
    for h in range(chunks):
        heads = by_share(line_gather(mixed[h]))
        attn = jnp.dot(heads, out_wide, preferred_element_type=F32).astype(BF16)
        attn = lax.psum_scatter(attn, "mlp", scatter_dimension=0, tiled=True)
        residual = lane_input[:, h].astype(F32).reshape(planes * sub, dz) + attn.astype(F32)
        square = jnp.sum(residual * residual, axis=-1).reshape(planes, sub)
        lane = lax.all_gather((residual * gain_lane).astype(BF16), "mlp", axis=0, tiled=True)
        square = sum(
            [square[0]]
            + [move(square[k], [(i, (i - k) % planes) for i in range(planes)]) for k in range(1, planes)]
        )
        square = lax.all_gather(square, "mlp", axis=0, tiled=True)
        scale = lax.rsqrt(square / width + norm_eps)[:, None]
        part = jnp.dot(lane, glu_weight, preferred_element_type=F32).astype(BF16)
        part = part.reshape(mlp_count, planes, sub, 2 * units)
        act = line_scatter([part[:, k].reshape(crows, 2 * units) for k in range(planes)]) * scale
        hidden = jax.nn.silu(act[:, :whole]) * act[:, whole : 2 * whole]
        if units > whole:
            last = act[:, 2 * whole :]
            edge = units - whole
            hidden = jnp.concatenate(
                [hidden, jax.nn.silu(last[:, :edge]) * last[:, edge:]], axis=1
            )
        hidden = by_share(line_gather(hidden.astype(BF16)))
        down = jnp.dot(hidden, down_wide, preferred_element_type=F32).astype(BF16)
        down = lax.psum_scatter(down, "mlp", scatter_dimension=0, tiled=True)
        final = (residual + down.astype(F32)).astype(BF16).reshape(planes, sub, dz)
        finals.append(
            jnp.stack(
                [final[0]]
                + [move(final[k], [(i, (i - k) % planes) for i in range(planes)]) for k in range(1, planes)]
            )
        )
    final = swap_halves(jnp.concatenate(finals, axis=1))
    final = lax.dynamic_slice_in_dim(
        jnp.concatenate([final, final], axis=0), (planes - plane) % planes, planes, 0
    )
    layer_output = jnp.swapaxes(final, 0, 1).reshape(share, width)
    return (layer_output, kv_cache)


def solution(mesh):
    placed = (
        P("seq", None),
        P(),
        P(),
        P("seq", "mlp"),
        P("seq", None),
        P("seq", None),
        P("mlp", "seq"),
        P("seq", "mlp"),
        P("seq", "mlp"),
        P("mlp", "seq"),
        P("mlp"),
        P(),
        P(),
        P(),
        P(),
        P(),
    )
    return jax.shard_map(
        shards,
        mesh=mesh,
        in_specs=placed,
        out_specs=(P(("seq", "mlp"), None), P("seq", "mlp")),
        check_vma=False,
    )
```

```python
import math

import jax
import jax.numpy as jnp
from jax import lax
from jax.experimental import pallas as pl
from jax.experimental.pallas import tpu as pltpu
from jax.sharding import PartitionSpec as P

KVH = 8
HD = 128
PIECES_DEV = 2
CORES = 2

rope_base = 1000000.0
norm_eps = 1e-06
far_below = -1e30
start_top = -1e29
F32 = jnp.float32
BF16 = jnp.bfloat16


def rope_tables(position, head_dim):
    half_dim = head_dim // 2
    inverse_freq = jnp.power(
        jnp.float32(rope_base), -2.0 * jnp.arange(half_dim, dtype=jnp.float32) / head_dim
    )
    angles = position.astype(jnp.float32)[:, None] * inverse_freq[None, :]
    return (jnp.cos(angles), jnp.sin(angles))


def rotate(values, cosine, sine_part, head_count):
    row_count = values.shape[0]
    halves = values.reshape(row_count, head_count, 2, -1)
    lower_half = halves[:, :, 0, :]
    upper_half = halves[:, :, 1, :]
    cos_wide = cosine[:, None, :]
    sin_wide = sine_part[:, None, :]
    new_lower = lower_half * cos_wide - upper_half * sin_wide
    new_upper = upper_half * cos_wide + lower_half * sin_wide
    return jnp.stack([new_lower, new_upper], axis=2).reshape(row_count, -1)


def lookup(small_table, indices):
    matches = indices[:, None] == jnp.arange(small_table.shape[0], dtype=jnp.int32)[None, :]
    return jnp.sum(jnp.where(matches, small_table[None, :], 0), axis=1)


def attend_kernel(count, active, piece_stream, q_ref, k_ref, v_ref, lo_ref, hi_ref, o_ref, acc_ref):
    chunk = pl.program_id(1)
    piece_len = k_ref.shape[0] // piece_stream.shape[0]
    rows = q_ref.shape[1]
    per_kv = q_ref.shape[2] // HD
    scale = 1.0 / math.sqrt(HD)
    q = jnp.concatenate([q_ref[0, :, i * HD : (i + 1) * HD] for i in range(per_kv)], axis=0)
    lo = lo_ref[0]
    hi = hi_ref[0]
    acc_ref[...] = jnp.zeros_like(acc_ref)

    def step(i, carry):
        top, total = carry
        piece = active[chunk, i]
        first = pl.multiple_of(piece * piece_len, piece_len)
        k = k_ref[pl.ds(first, piece_len), :]
        v = v_ref[pl.ds(first, piece_len), :]
        s = lax.dot_general(k, q, (((1,), (1,)), ((), ())), preferred_element_type=F32) * scale
        stream = piece_stream[piece] * piece_len + lax.broadcasted_iota(jnp.int32, s.shape, 0)
        s = jnp.where((stream >= lo) & (stream <= hi), s, far_below)
        new_top = jnp.maximum(top, jnp.max(s, axis=0, keepdims=True))
        w = jnp.exp(s - new_top)
        fade = jnp.exp(top - new_top)
        total = total * fade + jnp.sum(w, axis=0, keepdims=True)
        part = lax.dot_general(v, w.astype(BF16), (((0,), (0,)), ((), ())), preferred_element_type=F32)
        acc_ref[...] = acc_ref[...] * fade + part
        return (new_top, total)

    top = jnp.full((1, q.shape[0]), start_top, F32)
    total = jnp.zeros((1, q.shape[0]), F32)
    top, total = lax.fori_loop(0, count[chunk], step, (top, total))
    out = (acc_ref[...] / total).T.astype(BF16)
    for i in range(per_kv):
        o_ref[0, :, i * HD : (i + 1) * HD] = out[i * rows : (i + 1) * rows]


def attend(query, kv_rows, lo, hi, piece_stream, kv_heads):
    chunks, rows, width = query.shape
    per_kv = width // (kv_heads * HD)
    keys = kv_rows.shape[0]
    pieces = piece_stream.shape[0]
    piece_len = keys // pieces
    first = piece_stream[None, None, :] * piece_len
    touch = jnp.any(
        (lo[:, :, None] <= first + piece_len - 1) & (hi[:, :, None] >= first), axis=1
    ).astype(jnp.int32)
    place = jnp.cumsum(touch, axis=1) - 1
    ids = jnp.arange(pieces, dtype=jnp.int32)
    active = jnp.sum(
        jnp.where((touch[:, :, None] > 0) & (place[:, :, None] == ids), ids[None, :, None], 0), axis=1
    ).astype(jnp.int32)
    count = jnp.sum(touch, axis=1).astype(jnp.int32)
    lo_wide = jnp.tile(lo, (1, per_kv))[:, None, :]
    hi_wide = jnp.tile(hi, (1, per_kv))[:, None, :]
    return pl.pallas_call(
        attend_kernel,
        grid_spec=pltpu.PrefetchScalarGridSpec(
            num_scalar_prefetch=3,
            grid=(kv_heads, chunks),
            in_specs=[
                pl.BlockSpec((1, rows, per_kv * HD), lambda g, h, *_: (h, 0, g)),
                pl.BlockSpec((keys, HD), lambda g, h, *_: (0, 2 * g)),
                pl.BlockSpec((keys, HD), lambda g, h, *_: (0, 2 * g + 1)),
                pl.BlockSpec((1, 1, rows * per_kv), lambda g, h, *_: (h, 0, 0)),
                pl.BlockSpec((1, 1, rows * per_kv), lambda g, h, *_: (h, 0, 0)),
            ],
            out_specs=pl.BlockSpec((1, rows, per_kv * HD), lambda g, h, *_: (h, 0, g)),
            scratch_shapes=[pltpu.VMEM((HD, rows * per_kv), F32)],
        ),
        out_shape=jax.ShapeDtypeStruct(query.shape, BF16),
        compiler_params=pltpu.CompilerParams(vmem_limit_bytes=32 * 2**20),
    )(count, active, piece_stream, query, kv_rows, kv_rows, lo_wide, hi_wide)


def shards(
    layer_input,
    attention_gain,
    feedforward_gain,
    query_weight,
    key_weight,
    value_weight,
    out_weight,
    gate_weight,
    up_weight,
    down_weight,
    query_bias,
    key_bias,
    value_bias,
    doc_lengths,
    piece_order,
    cache_page,
):
    seq_count = lax.axis_size("seq")
    mlp_count = lax.axis_size("mlp")
    seq_rank = lax.axis_index("seq")
    mlp_rank = lax.axis_index("mlp")
    planes = seq_count // CORES
    plane = seq_rank // CORES
    core = seq_rank % CORES
    rows, width = layer_input.shape
    dz = width // planes
    ds = width // seq_count
    share = rows // mlp_count
    chunks = 2 if share % 32 == 0 else 1
    sub = share // chunks
    crows = mlp_count * sub
    piece_len = rows // PIECES_DEV
    bits = mlp_count.bit_length() - 1

    def move(x, pairs):
        return lax.ppermute(
            x, "seq", [(a * CORES + e, b * CORES + e) for a, b in pairs for e in range(CORES)]
        )

    def sibling(x):
        return lax.ppermute(
            x, "seq", [(a * CORES + e, a * CORES + 1 - e) for a in range(planes) for e in range(CORES)]
        )

    def partner(x, bit):
        return lax.ppermute(x, "mlp", [(a, a ^ bit) for a in range(mlp_count)])

    def after(x, dep):
        return lax.optimization_barrier((x, dep))

    def add(a, b):
        return (a.astype(F32) + b.astype(F32)).astype(BF16)

    def gather_step(state, t):
        ups, downs = state
        ups.append(move(ups[-1], [(i, i + 1) for i in range(t - 1, planes - 1)]))
        downs.append(move(downs[-1], [(i, i - 1) for i in range(1, planes - t + 1)]))

    def gather_slots(state):
        ups, downs = state
        return [ups[0]] + [ups[k] + downs[planes - k] for k in range(1, planes)]

    def line_gather(x):
        state = ([x], [x])
        for t in range(1, planes):
            gather_step(state, t)
        return gather_slots(state)

    def scatter_step(parts, carried, t):
        send_up, send_down = parts[t], parts[planes - t]
        if carried is not None:
            send_up, send_down = add(send_up, carried[0]), add(send_down, carried[1])
        up = move(send_up, [(i, i + 1) for i in range(0, min(t, planes - 1))])
        down = move(send_down, [(i, i - 1) for i in range(max(1, planes - t), planes)])
        return (up, down)

    half = max(1, planes // 2)
    orders = [list(range(bits)), [(b + bits // 2) % bits for b in range(bits)]]

    def mlp_scatter(x):
        out = []
        for part, order in zip((x[:half], x[half:]), orders):
            slots = {j: part[:, j] for j in range(mlp_count)}
            for b in order:
                bit = 1 << b
                sent = [j for j in sorted(slots) if j & bit]
                got = partner(jnp.stack([slots[j].astype(BF16) for j in sent], axis=0), bit)
                slots = {
                    j ^ bit: slots[j ^ bit].astype(F32) + got[i].astype(F32)
                    for i, j in enumerate(sent)
                }
            out.append(slots[0])
        return jnp.concatenate(out, axis=0)

    def mlp_gather(x):
        out = []
        for part, order in zip((x[:half], x[half:]), orders):
            slots = {0: part}
            for b in reversed(order):
                bit = 1 << b
                have = sorted(slots)
                got = partner(jnp.stack([slots[j] for j in have], axis=0), bit)
                for i, j in enumerate(have):
                    slots[j | bit] = got[i]
            out.append(jnp.stack([slots[j] for j in range(mlp_count)], axis=1))
        return jnp.concatenate(out, axis=0)

    def swap_halves(x):
        return jnp.where(core == 0, x, jnp.concatenate([x[..., ds:], x[..., :ds]], axis=-1))

    kv_cols = max(HD, KVH * HD // mlp_count)
    kv_first = mlp_rank * KVH // mlp_count * HD
    kv_weight = jnp.concatenate(
        [
            lax.dynamic_slice_in_dim(key_weight, kv_first, kv_cols, 1),
            lax.dynamic_slice_in_dim(value_weight, kv_first, kv_cols, 1),
        ],
        axis=1,
    )
    kv_bias = jnp.concatenate(
        [
            lax.dynamic_slice_in_dim(key_bias, kv_first, kv_cols, 0),
            lax.dynamic_slice_in_dim(value_bias, kv_first, kv_cols, 0),
        ]
    ).astype(F32)
    kv_state = ([kv_weight], [kv_weight])
    for t in range(1, planes - 1):
        gather_step(kv_state, t)
    query_weight, (kv_state[0][-1], kv_state[1][-1]) = after(
        query_weight, (kv_state[0][-1], kv_state[1][-1])
    )
    gather_step(kv_state, planes - 1)
    q_state = ([query_weight], [query_weight])
    for t in range(1, planes):
        gather_step(q_state, t)

    relative = [mlp_rank ^ j for j in range(mlp_count)]

    def regroup(x):
        parts = x.reshape((mlp_count, share) + x.shape[1:])
        parts = jnp.stack([lax.dynamic_index_in_dim(parts, r, 0, False) for r in relative], axis=0)
        parts = parts.reshape((mlp_count, chunks, sub) + x.shape[1:])
        return jnp.swapaxes(parts, 0, 1).reshape(x.shape)

    def ungroup(x):
        parts = jnp.swapaxes(x.reshape((chunks, mlp_count, sub) + x.shape[1:]), 0, 1)
        parts = jnp.stack([lax.dynamic_index_in_dim(parts, r, 0, False) for r in relative], axis=0)
        return parts.reshape(x.shape)

    x = regroup(layer_input).astype(F32)
    mean_sq = jnp.mean(x * x, axis=-1, keepdims=True)
    normed = (x * lax.rsqrt(mean_sq + norm_eps) * attention_gain.astype(F32)).astype(BF16)
    even = jnp.concatenate([normed[:, CORES * z * ds : (CORES * z + 1) * ds] for z in range(planes)], axis=1)
    odd = jnp.concatenate([normed[:, (CORES * z + 1) * ds : CORES * (z + 1) * ds] for z in range(planes)], axis=1)
    mine = jnp.where(core == 0, even, odd)
    theirs = sibling(jnp.where(core == 0, odd, even))
    both = jnp.concatenate([mine, theirs], axis=0)
    lanes = [lax.dynamic_slice_in_dim(both, (plane - k) % planes * ds, ds, 1) for k in range(planes)]

    units = gate_weight.shape[1]
    whole = units // HD * HD
    glu_own = jnp.concatenate(
        [gate_weight[:, :whole], up_weight[:, :whole], gate_weight[:, whole:], up_weight[:, whole:]],
        axis=1,
    )
    glu_own = lax.optimization_barrier(glu_own)
    glu_weight = jnp.concatenate([glu_own, sibling(glu_own)], axis=0)
    out_wide = jnp.concatenate([out_weight, sibling(out_weight)], axis=1)
    down_wide = jnp.concatenate([down_weight, sibling(down_weight)], axis=1)

    own_share = lax.dynamic_slice_in_dim(layer_input, mlp_rank * share, share, 0)
    lane_parts = []
    for k in range(planes):
        part = lax.dynamic_slice_in_dim(own_share, (plane + k) % planes * dz, dz, 1)
        if k:
            part = move(part, [(i, (i + k) % planes) for i in range(planes)])
        lane_parts.append(part)
    lane_input = swap_halves(jnp.stack(lane_parts, axis=0))
    lane_input = lane_input.reshape(planes, chunks, sub, dz)
    gain_lane = swap_halves(lax.dynamic_slice_in_dim(feedforward_gain, plane * dz, dz, 0)).astype(F32)
    lanes, glu_weight, out_wide, down_wide, lane_input = lax.optimization_barrier(
        (lanes, glu_weight, out_wide, down_wide, lane_input)
    )

    row_ids = seq_rank * rows + regroup(jnp.arange(rows, dtype=jnp.int32))
    stream = lookup(piece_order, row_ids // piece_len) * piece_len + row_ids % piece_len
    doc_ends = jnp.cumsum(doc_lengths)
    segment = jnp.sum((stream[:, None] >= doc_ends[None, :]).astype(jnp.int32), axis=1)
    doc_first = lookup(doc_ends - doc_lengths, segment)
    cosine, sine_part = rope_tables(stream - doc_first, HD)

    def project(state, bias):
        total = None
        for lane, weight in zip(lanes, gather_slots(state)):
            part = jnp.dot(lane, lax.optimization_barrier(weight), preferred_element_type=F32)
            total = part if total is None else total + part
        return total[:rows] + sibling(total[rows:]) + bias

    kv_heads = kv_cols // HD
    query_heads = query_weight.shape[1] // HD
    kv = project(kv_state, kv_bias)
    key_rot = rotate(kv[:, :kv_cols], cosine, sine_part, kv_heads).astype(BF16)
    value_b = kv[:, kv_cols:].astype(BF16)
    joined = jnp.stack(
        [key_rot.reshape(rows, kv_heads, HD), value_b.reshape(rows, kv_heads, HD)], axis=2
    ).reshape(rows, 2 * kv_cols)
    core_rows = jnp.concatenate(line_gather(ungroup(joined)), axis=0)
    kv_rows = jnp.concatenate([core_rows, sibling(core_rows)], axis=0)
    offsets = (plane - jnp.arange(planes, dtype=jnp.int32)) % planes
    slots = jnp.concatenate([offsets * CORES + core, offsets * CORES + 1 - core])
    slots = (slots[:, None] * PIECES_DEV + jnp.arange(PIECES_DEV, dtype=jnp.int32)).reshape(-1)
    piece_stream = lookup(piece_order, slots)

    own_cols = KVH * HD // mlp_count
    cache_width = 2 * own_cols
    offset = mlp_rank % max(1, HD // own_cols) * cache_width
    pieces = jnp.arange(piece_order.shape[0], dtype=jnp.int32)
    pages = []
    for p in range(PIECES_DEV):
        stream_piece = jnp.sum(jnp.where(cache_page == seq_rank * PIECES_DEV + p, pieces, 0))
        source = jnp.sum(jnp.where(piece_stream == stream_piece, pieces, 0))
        pages.append(lax.dynamic_slice(kv_rows, (source * piece_len, offset), (piece_len, cache_width)))
    kv_cache = jnp.concatenate(pages, axis=0)

    query = project(q_state, query_bias.astype(F32))
    query_rot = rotate(query, cosine, sine_part, query_heads).astype(BF16)
    mixed = attend(
        query_rot.reshape(chunks, crows, query_heads * HD),
        kv_rows,
        doc_first.reshape(chunks, crows),
        stream.reshape(chunks, crows),
        piece_stream,
        kv_heads,
    )

    mixed_states = []
    dep = None
    for h in range(chunks):
        first = mixed[h]
        if dep is not None:
            first, dep = after(first, dep)
            mixed_states[-1][0][-1], mixed_states[-1][1][-1] = dep
            gather_step(mixed_states[-1], planes - 1)
        state = ([first], [first])
        for t in range(1, planes - 1):
            gather_step(state, t)
        dep = (state[0][-1], state[1][-1])
        mixed_states.append(state)
    gather_step(mixed_states[-1], planes - 1)

    residuals, scales, parts = [], [], []
    for h in range(chunks):
        heads = jnp.concatenate(gather_slots(mixed_states[h]), axis=0)
        attn = jnp.dot(heads, out_wide, preferred_element_type=F32).astype(BF16)
        attn = mlp_scatter(attn.reshape(planes, mlp_count, sub, dz))
        residual = lane_input[:, h].astype(F32) + attn
        square = jnp.sum(residual * residual, axis=-1)
        lane = mlp_gather((residual * gain_lane).astype(BF16))
        square = sum(
            [square[0]]
            + [move(square[k], [(i, (i - k) % planes) for i in range(planes)]) for k in range(1, planes)]
        )
        found = {0: square}
        for b in range(bits):
            bit = 1 << b
            have = sorted(found)
            got = partner(jnp.stack([found[j] for j in have], axis=0), bit)
            for i, j in enumerate(have):
                found[j | bit] = got[i]
        square = jnp.stack([found[j] for j in range(mlp_count)], axis=0).reshape(crows, 1)
        scales.append(lax.rsqrt(square / width + norm_eps))
        part = jnp.dot(lane.reshape(planes * crows, dz), glu_weight, preferred_element_type=F32)
        parts.append(part.astype(BF16).reshape(planes, crows, 2 * units))
        residuals.append(residual)

    carried = [None] * chunks
    for h in range(chunks):
        for t in range(1, planes):
            if t == planes - 1 and h + 1 < chunks:
                parts[h + 1], carried[h] = after(parts[h + 1], carried[h])
            carried[h] = scatter_step(parts[h], carried[h], t)

    finals = []
    for h in range(chunks):
        act = parts[h][0].astype(F32) + carried[h][0].astype(F32) + carried[h][1].astype(F32)
        act = act * scales[h]
        hidden = jax.nn.silu(act[:, :whole]) * act[:, whole : 2 * whole]
        if units > whole:
            last = act[:, 2 * whole :]
            edge = units - whole
            hidden = jnp.concatenate(
                [hidden, jax.nn.silu(last[:, :edge]) * last[:, edge:]], axis=1
            )
        hidden = jnp.concatenate(line_gather(hidden.astype(BF16)), axis=0)
        down = jnp.dot(hidden, down_wide, preferred_element_type=F32).astype(BF16)
        down = mlp_scatter(down.reshape(planes, mlp_count, sub, dz))
        final = (residuals[h] + down).astype(BF16)
        finals.append(
            jnp.stack(
                [final[0]]
                + [move(final[k], [(i, (i - k) % planes) for i in range(planes)]) for k in range(1, planes)]
            )
        )
    final = swap_halves(jnp.concatenate(finals, axis=1))
    final = lax.dynamic_slice_in_dim(
        jnp.concatenate([final, final], axis=0), (planes - plane) % planes, planes, 0
    )
    layer_output = jnp.swapaxes(final, 0, 1).reshape(share, width)
    return (layer_output, kv_cache)


def solution(mesh):
    placed = (
        P("seq", None),
        P(),
        P(),
        P("seq", "mlp"),
        P("seq", None),
        P("seq", None),
        P("mlp", "seq"),
        P("seq", "mlp"),
        P("seq", "mlp"),
        P("mlp", "seq"),
        P("mlp"),
        P(),
        P(),
        P(),
        P(),
        P(),
    )
    return jax.shard_map(
        shards,
        mesh=mesh,
        in_specs=placed,
        out_specs=(P(("seq", "mlp"), None), P("seq", "mlp")),
        check_vma=False,
    )
```

```python
import math

import jax
import jax.numpy as jnp
from jax import lax
from jax.experimental import pallas as pl
from jax.experimental.pallas import tpu as pltpu
from jax.sharding import PartitionSpec as P

KVH = 8
HD = 128
PIECES_DEV = 2
CORES = 2

rope_base = 1000000.0
norm_eps = 1e-06
far_below = -1e30
start_top = -1e29
F32 = jnp.float32
BF16 = jnp.bfloat16


def rope_tables(position, head_dim):
    half_dim = head_dim // 2
    inverse_freq = jnp.power(
        jnp.float32(rope_base), -2.0 * jnp.arange(half_dim, dtype=jnp.float32) / head_dim
    )
    angles = position.astype(jnp.float32)[:, None] * inverse_freq[None, :]
    return (jnp.cos(angles), jnp.sin(angles))


def rotate(values, cosine, sine_part, head_count):
    row_count = values.shape[0]
    halves = values.reshape(row_count, head_count, 2, -1)
    lower_half = halves[:, :, 0, :]
    upper_half = halves[:, :, 1, :]
    cos_wide = cosine[:, None, :]
    sin_wide = sine_part[:, None, :]
    new_lower = lower_half * cos_wide - upper_half * sin_wide
    new_upper = upper_half * cos_wide + lower_half * sin_wide
    return jnp.stack([new_lower, new_upper], axis=2).reshape(row_count, -1)


def lookup(small_table, indices):
    matches = indices[:, None] == jnp.arange(small_table.shape[0], dtype=jnp.int32)[None, :]
    return jnp.sum(jnp.where(matches, small_table[None, :], 0), axis=1)


def attend_kernel(count, active, piece_stream, q_ref, k_ref, v_ref, lo_ref, hi_ref, o_ref, acc_ref):
    chunk = pl.program_id(1)
    piece_len = k_ref.shape[0] // piece_stream.shape[0]
    rows = q_ref.shape[1]
    per_kv = q_ref.shape[2] // HD
    scale = 1.0 / math.sqrt(HD)
    q = jnp.concatenate([q_ref[0, :, i * HD : (i + 1) * HD] for i in range(per_kv)], axis=0)
    lo = lo_ref[0]
    hi = hi_ref[0]
    acc_ref[...] = jnp.zeros_like(acc_ref)

    def step(i, carry):
        top, total = carry
        piece = active[chunk, i]
        first = pl.multiple_of(piece * piece_len, piece_len)
        k = k_ref[pl.ds(first, piece_len), :]
        v = v_ref[pl.ds(first, piece_len), :]
        s = lax.dot_general(k, q, (((1,), (1,)), ((), ())), preferred_element_type=F32) * scale
        stream = piece_stream[piece] * piece_len + lax.broadcasted_iota(jnp.int32, s.shape, 0)
        s = jnp.where((stream >= lo) & (stream <= hi), s, far_below)
        new_top = jnp.maximum(top, jnp.max(s, axis=0, keepdims=True))
        w = jnp.exp(s - new_top)
        fade = jnp.exp(top - new_top)
        total = total * fade + jnp.sum(w, axis=0, keepdims=True)
        part = lax.dot_general(v, w.astype(BF16), (((0,), (0,)), ((), ())), preferred_element_type=F32)
        acc_ref[...] = acc_ref[...] * fade + part
        return (new_top, total)

    top = jnp.full((1, q.shape[0]), start_top, F32)
    total = jnp.zeros((1, q.shape[0]), F32)
    top, total = lax.fori_loop(0, count[chunk], step, (top, total))
    out = (acc_ref[...] / total).T.astype(BF16)
    for i in range(per_kv):
        o_ref[0, :, i * HD : (i + 1) * HD] = out[i * rows : (i + 1) * rows]


def attend(query, kv_rows, lo, hi, piece_stream, kv_heads):
    chunks, rows, width = query.shape
    per_kv = width // (kv_heads * HD)
    keys = kv_rows.shape[0]
    pieces = piece_stream.shape[0]
    piece_len = keys // pieces
    first = piece_stream[None, None, :] * piece_len
    touch = jnp.any(
        (lo[:, :, None] <= first + piece_len - 1) & (hi[:, :, None] >= first), axis=1
    ).astype(jnp.int32)
    place = jnp.cumsum(touch, axis=1) - 1
    ids = jnp.arange(pieces, dtype=jnp.int32)
    active = jnp.sum(
        jnp.where((touch[:, :, None] > 0) & (place[:, :, None] == ids), ids[None, :, None], 0), axis=1
    ).astype(jnp.int32)
    count = jnp.sum(touch, axis=1).astype(jnp.int32)
    lo_wide = jnp.tile(lo, (1, per_kv))[:, None, :]
    hi_wide = jnp.tile(hi, (1, per_kv))[:, None, :]
    return pl.pallas_call(
        attend_kernel,
        grid_spec=pltpu.PrefetchScalarGridSpec(
            num_scalar_prefetch=3,
            grid=(kv_heads, chunks),
            in_specs=[
                pl.BlockSpec((1, rows, per_kv * HD), lambda g, h, *_: (h, 0, g)),
                pl.BlockSpec((keys, HD), lambda g, h, *_: (0, 2 * g)),
                pl.BlockSpec((keys, HD), lambda g, h, *_: (0, 2 * g + 1)),
                pl.BlockSpec((1, 1, rows * per_kv), lambda g, h, *_: (h, 0, 0)),
                pl.BlockSpec((1, 1, rows * per_kv), lambda g, h, *_: (h, 0, 0)),
            ],
            out_specs=pl.BlockSpec((1, rows, per_kv * HD), lambda g, h, *_: (h, 0, g)),
            scratch_shapes=[pltpu.VMEM((HD, rows * per_kv), F32)],
        ),
        out_shape=jax.ShapeDtypeStruct(query.shape, BF16),
        compiler_params=pltpu.CompilerParams(vmem_limit_bytes=32 * 2**20),
    )(count, active, piece_stream, query, kv_rows, kv_rows, lo_wide, hi_wide)


def shards(
    layer_input,
    attention_gain,
    feedforward_gain,
    query_weight,
    key_weight,
    value_weight,
    out_weight,
    gate_weight,
    up_weight,
    down_weight,
    query_bias,
    key_bias,
    value_bias,
    doc_lengths,
    piece_order,
    cache_page,
):
    seq_count = lax.axis_size("seq")
    mlp_count = lax.axis_size("mlp")
    seq_rank = lax.axis_index("seq")
    mlp_rank = lax.axis_index("mlp")
    planes = seq_count // CORES
    plane = seq_rank // CORES
    core = seq_rank % CORES
    rows, width = layer_input.shape
    dz = width // planes
    ds = width // seq_count
    share = rows // mlp_count
    chunks = 2 if share % 32 == 0 else 1
    sub = share // chunks
    crows = mlp_count * sub
    piece_len = rows // PIECES_DEV
    bits = mlp_count.bit_length() - 1

    def move(x, pairs):
        return lax.ppermute(
            x, "seq", [(a * CORES + e, b * CORES + e) for a, b in pairs for e in range(CORES)]
        )

    def sibling(x):
        return lax.ppermute(
            x, "seq", [(a * CORES + e, a * CORES + 1 - e) for a in range(planes) for e in range(CORES)]
        )

    def partner(x, bit):
        return lax.ppermute(x, "mlp", [(a, a ^ bit) for a in range(mlp_count)])

    def after(x, dep):
        return lax.optimization_barrier((x, dep))

    def add(a, b):
        return (a.astype(F32) + b.astype(F32)).astype(BF16)

    def gather_step(state, t):
        ups, downs = state
        ups.append(move(ups[-1], [(i, i + 1) for i in range(t - 1, planes - 1)]))
        downs.append(move(downs[-1], [(i, i - 1) for i in range(1, planes - t + 1)]))

    def gather_slots(state):
        ups, downs = state
        return [ups[0]] + [ups[k] + downs[planes - k] for k in range(1, planes)]

    def line_gather(x):
        state = ([x], [x])
        for t in range(1, planes):
            gather_step(state, t)
        return gather_slots(state)

    def scatter_step(parts, carried, t):
        send_up, send_down = parts[t], parts[planes - t]
        if carried is not None:
            send_up, send_down = add(send_up, carried[0]), add(send_down, carried[1])
        up = move(send_up, [(i, i + 1) for i in range(0, min(t, planes - 1))])
        down = move(send_down, [(i, i - 1) for i in range(max(1, planes - t), planes)])
        return (up, down)

    half = max(1, planes // 2)
    orders = [list(range(bits)), [(b + bits // 2) % bits for b in range(bits)]]

    def mlp_scatter(x):
        out = []
        for part, order in zip((x[:half], x[half:]), orders):
            slots = {j: part[:, j] for j in range(mlp_count)}
            for b in order:
                bit = 1 << b
                sent = [j for j in sorted(slots) if j & bit]
                got = partner(jnp.stack([slots[j].astype(BF16) for j in sent], axis=0), bit)
                slots = {
                    j ^ bit: slots[j ^ bit].astype(F32) + got[i].astype(F32)
                    for i, j in enumerate(sent)
                }
            out.append(slots[0])
        return jnp.concatenate(out, axis=0)

    def mlp_gather(x):
        out = []
        for part, order in zip((x[:half], x[half:]), orders):
            slots = {0: part}
            for b in reversed(order):
                bit = 1 << b
                have = sorted(slots)
                got = partner(jnp.stack([slots[j] for j in have], axis=0), bit)
                for i, j in enumerate(have):
                    slots[j | bit] = got[i]
            out.append(jnp.stack([slots[j] for j in range(mlp_count)], axis=1))
        return jnp.concatenate(out, axis=0)

    lines = [[z * CORES + e for z in range(planes)] for e in range(CORES)]

    def line_collect(x):
        return lax.all_gather(x, "seq", axis=0, tiled=True, axis_index_groups=lines)

    def swap_halves(x):
        return jnp.where(core == 0, x, jnp.concatenate([x[..., ds:], x[..., :ds]], axis=-1))

    kv_cols = max(HD, KVH * HD // mlp_count)
    kv_first = mlp_rank * KVH // mlp_count * HD
    kv_weight = jnp.concatenate(
        [
            lax.dynamic_slice_in_dim(key_weight, kv_first, kv_cols, 1),
            lax.dynamic_slice_in_dim(value_weight, kv_first, kv_cols, 1),
        ],
        axis=1,
    )
    kv_bias = jnp.concatenate(
        [
            lax.dynamic_slice_in_dim(key_bias, kv_first, kv_cols, 0),
            lax.dynamic_slice_in_dim(value_bias, kv_first, kv_cols, 0),
        ]
    ).astype(F32)
    kv_weight = line_collect(kv_weight)
    q_weight = line_collect(query_weight)

    relative = [mlp_rank ^ j for j in range(mlp_count)]

    def regroup(x):
        parts = x.reshape((mlp_count, share) + x.shape[1:])
        parts = jnp.stack([lax.dynamic_index_in_dim(parts, r, 0, False) for r in relative], axis=0)
        parts = parts.reshape((mlp_count, chunks, sub) + x.shape[1:])
        return jnp.swapaxes(parts, 0, 1).reshape(x.shape)

    def ungroup(x):
        parts = jnp.swapaxes(x.reshape((chunks, mlp_count, sub) + x.shape[1:]), 0, 1)
        parts = jnp.stack([lax.dynamic_index_in_dim(parts, r, 0, False) for r in relative], axis=0)
        return parts.reshape(x.shape)

    x = regroup(layer_input).astype(F32)
    mean_sq = jnp.mean(x * x, axis=-1, keepdims=True)
    normed = (x * lax.rsqrt(mean_sq + norm_eps) * attention_gain.astype(F32)).astype(BF16)
    even = jnp.concatenate([normed[:, CORES * z * ds : (CORES * z + 1) * ds] for z in range(planes)], axis=1)
    odd = jnp.concatenate([normed[:, (CORES * z + 1) * ds : CORES * (z + 1) * ds] for z in range(planes)], axis=1)
    mine = jnp.where(core == 0, even, odd)
    theirs = sibling(jnp.where(core == 0, odd, even))
    both = jnp.concatenate([mine, theirs], axis=0)

    units = gate_weight.shape[1]
    whole = units // HD * HD
    glu_own = jnp.concatenate(
        [gate_weight[:, :whole], up_weight[:, :whole], gate_weight[:, whole:], up_weight[:, whole:]],
        axis=1,
    )
    glu_own = lax.optimization_barrier(glu_own)
    glu_weight = jnp.concatenate(
        [
            jnp.pad(jnp.concatenate([glu_own, sibling(glu_own)], axis=0), ((0, 0), (0, HD))),
            jnp.pad(jnp.eye(HD, dtype=BF16), ((0, 0), (2 * units, 0))),
        ],
        axis=0,
    )
    out_wide = jnp.concatenate([out_weight, sibling(out_weight)], axis=1)
    down_wide = jnp.concatenate([down_weight, sibling(down_weight)], axis=1)

    both, glu_weight, out_wide, down_wide = lax.optimization_barrier(
        (both, glu_weight, out_wide, down_wide)
    )

    row_ids = seq_rank * rows + regroup(jnp.arange(rows, dtype=jnp.int32))
    stream = lookup(piece_order, row_ids // piece_len) * piece_len + row_ids % piece_len
    doc_ends = jnp.cumsum(doc_lengths)
    segment = jnp.sum((stream[:, None] >= doc_ends[None, :]).astype(jnp.int32), axis=1)
    doc_first = lookup(doc_ends - doc_lengths, segment)
    cosine, sine_part = rope_tables(stream - doc_first, HD)

    def project(weight, bias):
        total = jnp.dot(both, weight, preferred_element_type=F32)
        return total[:rows] + sibling(total[rows:]) + bias

    kv_heads = kv_cols // HD
    query_heads = query_weight.shape[1] // HD
    kv = project(kv_weight, kv_bias)
    key_rot = rotate(kv[:, :kv_cols], cosine, sine_part, kv_heads).astype(BF16)
    value_b = kv[:, kv_cols:].astype(BF16)
    joined = jnp.stack(
        [key_rot.reshape(rows, kv_heads, HD), value_b.reshape(rows, kv_heads, HD)], axis=2
    ).reshape(rows, 2 * kv_cols)
    core_rows = jnp.concatenate(line_gather(ungroup(joined)), axis=0)
    layer_input, core_rows = after(layer_input, core_rows)
    own_share = lax.dynamic_slice_in_dim(layer_input, mlp_rank * share, share, 0)
    lane_parts = []
    for k in range(planes):
        part = lax.dynamic_slice_in_dim(own_share, (plane + k) % planes * dz, dz, 1)
        if k:
            part = move(part, [(i, (i + k) % planes) for i in range(planes)])
        lane_parts.append(part)
    lane_input = swap_halves(jnp.stack(lane_parts, axis=0))
    lane_input = lane_input.reshape(planes, chunks, sub, dz)
    gain_lane = swap_halves(lax.dynamic_slice_in_dim(feedforward_gain, plane * dz, dz, 0)).astype(F32)
    kv_rows = jnp.concatenate([core_rows, sibling(core_rows)], axis=0)
    offsets = (plane - jnp.arange(planes, dtype=jnp.int32)) % planes
    slots = jnp.concatenate([offsets * CORES + core, offsets * CORES + 1 - core])
    slots = (slots[:, None] * PIECES_DEV + jnp.arange(PIECES_DEV, dtype=jnp.int32)).reshape(-1)
    piece_stream = lookup(piece_order, slots)

    own_cols = KVH * HD // mlp_count
    cache_width = 2 * own_cols
    offset = mlp_rank % max(1, HD // own_cols) * cache_width
    pieces = jnp.arange(piece_order.shape[0], dtype=jnp.int32)
    pages = []
    for p in range(PIECES_DEV):
        stream_piece = jnp.sum(jnp.where(cache_page == seq_rank * PIECES_DEV + p, pieces, 0))
        source = jnp.sum(jnp.where(piece_stream == stream_piece, pieces, 0))
        pages.append(lax.dynamic_slice(kv_rows, (source * piece_len, offset), (piece_len, cache_width)))
    kv_cache = jnp.concatenate(pages, axis=0)

    query = project(q_weight, query_bias.astype(F32))
    query_rot = rotate(query, cosine, sine_part, query_heads).astype(BF16)
    mixed = attend(
        query_rot.reshape(chunks, crows, query_heads * HD),
        kv_rows,
        doc_first.reshape(chunks, crows),
        stream.reshape(chunks, crows),
        piece_stream,
        kv_heads,
    )

    collected = [line_collect(mixed[h]) for h in range(chunks)]
    residuals, parts = [], []
    for h in range(chunks):
        heads = jnp.concatenate(
            [
                lax.dynamic_slice_in_dim(collected[h], (plane - k) % planes * crows, crows, 0)
                for k in range(planes)
            ],
            axis=0,
        )
        attn = jnp.dot(heads, out_wide, preferred_element_type=F32).astype(BF16)
        attn = mlp_scatter(attn.reshape(planes, mlp_count, sub, dz))
        residual = lane_input[:, h].astype(F32) + attn
        square = residual * residual
        square = sum(square[..., i : i + HD] for i in range(0, dz, HD))
        lane = jnp.concatenate([(residual * gain_lane).astype(BF16), square.astype(BF16)], axis=-1)
        lane = mlp_gather(lane).reshape(planes * crows, dz + HD)
        part = jnp.dot(lane, glu_weight, preferred_element_type=F32)
        parts.append(part.astype(BF16).reshape(planes, crows, 2 * units + HD))
        residuals.append(residual)

    carried = [None] * chunks
    for h in range(chunks):
        for t in range(1, planes):
            if t == planes - 1 and h + 1 < chunks:
                parts[h + 1], carried[h] = after(parts[h + 1], carried[h])
            carried[h] = scatter_step(parts[h], carried[h], t)

    finals = []
    for h in range(chunks):
        act = parts[h][0].astype(F32) + carried[h][0].astype(F32) + carried[h][1].astype(F32)
        square = jnp.sum(act[:, 2 * units :], axis=1, keepdims=True)
        act = act * lax.rsqrt(square / width + norm_eps)
        hidden = jax.nn.silu(act[:, :whole]) * act[:, whole : 2 * whole]
        if units > whole:
            last = act[:, 2 * whole : 2 * units]
            edge = units - whole
            hidden = jnp.concatenate(
                [hidden, jax.nn.silu(last[:, :edge]) * last[:, edge:]], axis=1
            )
        hidden = jnp.concatenate(line_gather(hidden.astype(BF16)), axis=0)
        down = jnp.dot(hidden, down_wide, preferred_element_type=F32).astype(BF16)
        down = mlp_scatter(down.reshape(planes, mlp_count, sub, dz))
        final = (residuals[h] + down).astype(BF16)
        finals.append(
            jnp.stack(
                [final[0]]
                + [move(final[k], [(i, (i - k) % planes) for i in range(planes)]) for k in range(1, planes)]
            )
        )
    final = swap_halves(jnp.concatenate(finals, axis=1))
    final = lax.dynamic_slice_in_dim(
        jnp.concatenate([final, final], axis=0), (planes - plane) % planes, planes, 0
    )
    layer_output = jnp.swapaxes(final, 0, 1).reshape(share, width)
    return (layer_output, kv_cache)


def solution(mesh):
    placed = (
        P("seq", None),
        P(),
        P(),
        P("seq", "mlp"),
        P("seq", None),
        P("seq", None),
        P("mlp", "seq"),
        P("seq", "mlp"),
        P("seq", "mlp"),
        P("mlp", "seq"),
        P("mlp"),
        P(),
        P(),
        P(),
        P(),
        P(),
    )
    return jax.shard_map(
        shards,
        mesh=mesh,
        in_specs=placed,
        out_specs=(P(("seq", "mlp"), None), P("seq", "mlp")),
        check_vma=False,
    )
```

```python
import math

import jax
import jax.numpy as jnp
from jax import lax
from jax.experimental import pallas as pl
from jax.experimental.pallas import tpu as pltpu
from jax.sharding import PartitionSpec as P

KVH = 8
HD = 128
PIECES_DEV = 2
CORES = 2

rope_base = 1000000.0
norm_eps = 1e-06
far_below = -1e30
start_top = -1e29
F32 = jnp.float32
BF16 = jnp.bfloat16


def rope_tables(position, head_dim):
    half_dim = head_dim // 2
    inverse_freq = jnp.power(
        jnp.float32(rope_base), -2.0 * jnp.arange(half_dim, dtype=jnp.float32) / head_dim
    )
    angles = position.astype(jnp.float32)[:, None] * inverse_freq[None, :]
    cosine, sine = jnp.cos(angles), jnp.sin(angles)
    return (jnp.concatenate([cosine, cosine], axis=1), jnp.concatenate([-sine, sine], axis=1))


def rotate_wide(values, cosine, sine):
    return values * cosine + pltpu.roll(values, HD // 2, 1) * sine


def lookup(small_table, indices):
    matches = indices[:, None] == jnp.arange(small_table.shape[0], dtype=jnp.int32)[None, :]
    return jnp.sum(jnp.where(matches, small_table[None, :], 0), axis=1)


def attend_kernel(
    count, active, piece_stream, own_ref, sib_ref, bias_ref, cos_ref, sin_ref, k_ref, v_ref, lo_ref, hi_ref, o_ref, acc_ref
):
    slot = pl.program_id(1)
    piece_len = k_ref.shape[0] // piece_stream.shape[0]
    rows, wide = own_ref.shape
    per_kv = wide // HD
    scale = 1.0 / math.sqrt(HD)
    cosine, sine = cos_ref[...], sin_ref[...]
    query = own_ref[...] + sib_ref[...] + bias_ref[...]
    q = jnp.concatenate(
        [
            rotate_wide(query[:, i * HD : (i + 1) * HD], cosine, sine).astype(BF16)
            for i in range(per_kv)
        ],
        axis=0,
    )
    lo = lo_ref[0]
    hi = hi_ref[0]
    acc_ref[...] = jnp.zeros_like(acc_ref)

    def step(i, carry):
        top, total = carry
        piece = active[slot, i]
        first = pl.multiple_of(piece * piece_len, piece_len)
        k = k_ref[pl.ds(first, piece_len), :]
        v = v_ref[pl.ds(first, piece_len), :]
        s = lax.dot_general(k, q, (((1,), (1,)), ((), ())), preferred_element_type=F32) * scale
        stream = piece_stream[piece] * piece_len + lax.broadcasted_iota(jnp.int32, s.shape, 0)
        s = jnp.where((stream >= lo) & (stream <= hi), s, far_below)
        new_top = jnp.maximum(top, jnp.max(s, axis=0, keepdims=True))
        w = jnp.exp(s - new_top)
        fade = jnp.exp(top - new_top)
        total = total * fade + jnp.sum(w, axis=0, keepdims=True)
        part = lax.dot_general(v, w.astype(BF16), (((0,), (0,)), ((), ())), preferred_element_type=F32)
        acc_ref[...] = acc_ref[...] * fade + part
        return (new_top, total)

    top = jnp.full((1, q.shape[0]), start_top, F32)
    total = jnp.zeros((1, q.shape[0]), F32)
    top, total = lax.fori_loop(0, count[slot], step, (top, total))
    out = (acc_ref[...] / total).T.astype(BF16)
    for i in range(per_kv):
        o_ref[:, i * HD : (i + 1) * HD] = out[i * rows : (i + 1) * rows]


def attend(query, query_sib, bias, cosine, sine, kv_rows, lo, hi, piece_stream, kv_heads):
    rows, width = query_sib.shape
    slots = PIECES_DEV
    lo, hi = lo.reshape(slots, -1), hi.reshape(slots, -1)
    per_kv = width // (kv_heads * HD)
    keys = kv_rows.shape[0]
    pieces = piece_stream.shape[0]
    piece_len = keys // pieces
    first = piece_stream[None, None, :] * piece_len
    touch = jnp.any(
        (lo[:, :, None] <= first + piece_len - 1) & (hi[:, :, None] >= first), axis=1
    ).astype(jnp.int32)
    place = jnp.cumsum(touch, axis=1) - 1
    ids = jnp.arange(pieces, dtype=jnp.int32)
    active = jnp.sum(
        jnp.where((touch[:, :, None] > 0) & (place[:, :, None] == ids), ids[None, :, None], 0), axis=1
    ).astype(jnp.int32)
    count = jnp.sum(touch, axis=1).astype(jnp.int32)
    lo_wide = jnp.tile(lo, (1, per_kv))[:, None, :]
    hi_wide = jnp.tile(hi, (1, per_kv))[:, None, :]
    tile = (piece_len, per_kv * HD)
    return pl.pallas_call(
        attend_kernel,
        grid_spec=pltpu.PrefetchScalarGridSpec(
            num_scalar_prefetch=3,
            grid=(kv_heads, slots),
            in_specs=[
                pl.BlockSpec(tile, lambda g, h, *_: (h, g)),
                pl.BlockSpec(tile, lambda g, h, *_: (h, g)),
                pl.BlockSpec((1, per_kv * HD), lambda g, h, *_: (0, g)),
                pl.BlockSpec((piece_len, HD), lambda g, h, *_: (h, 0)),
                pl.BlockSpec((piece_len, HD), lambda g, h, *_: (h, 0)),
                pl.BlockSpec((keys, HD), lambda g, h, *_: (0, 2 * g)),
                pl.BlockSpec((keys, HD), lambda g, h, *_: (0, 2 * g + 1)),
                pl.BlockSpec((1, 1, piece_len * per_kv), lambda g, h, *_: (h, 0, 0)),
                pl.BlockSpec((1, 1, piece_len * per_kv), lambda g, h, *_: (h, 0, 0)),
            ],
            out_specs=pl.BlockSpec(tile, lambda g, h, *_: (h, g)),
            scratch_shapes=[pltpu.VMEM((HD, piece_len * per_kv), F32)],
        ),
        out_shape=jax.ShapeDtypeStruct((rows, width), BF16),
        compiler_params=pltpu.CompilerParams(vmem_limit_bytes=32 * 2**20),
    )(count, active, piece_stream, query, query_sib, bias, cosine, sine, kv_rows, kv_rows, lo_wide, hi_wide)


def join_kernel(own_ref, sib_ref, bias_ref, cos_ref, sin_ref, o_ref):
    rows, wide = o_ref.shape
    heads = wide // (2 * HD)
    cosine, sine = cos_ref[...], sin_ref[...]
    kv = own_ref[:rows, :] + sib_ref[...] + bias_ref[...]
    for g in range(heads):
        key = rotate_wide(kv[:, g * HD : (g + 1) * HD], cosine, sine)
        o_ref[:, 2 * g * HD : (2 * g + 1) * HD] = key.astype(BF16)
        value = kv[:, (heads + g) * HD : (heads + g + 1) * HD]
        o_ref[:, (2 * g + 1) * HD : (2 * g + 2) * HD] = value.astype(BF16)


def shards(
    layer_input,
    attention_gain,
    feedforward_gain,
    query_weight,
    key_weight,
    value_weight,
    out_weight,
    gate_weight,
    up_weight,
    down_weight,
    query_bias,
    key_bias,
    value_bias,
    doc_lengths,
    piece_order,
    cache_page,
):
    seq_count = lax.axis_size("seq")
    mlp_count = lax.axis_size("mlp")
    seq_rank = lax.axis_index("seq")
    mlp_rank = lax.axis_index("mlp")
    planes = seq_count // CORES
    plane = seq_rank // CORES
    core = seq_rank % CORES
    rows, width = layer_input.shape
    dz = width // planes
    ds = width // seq_count
    share = rows // mlp_count
    chunks = 2 if share % 32 == 0 else 1
    sub = share // chunks
    crows = mlp_count * sub
    piece_len = rows // PIECES_DEV
    bits = mlp_count.bit_length() - 1

    def move(x, pairs):
        return lax.ppermute(
            x, "seq", [(a * CORES + e, b * CORES + e) for a, b in pairs for e in range(CORES)]
        )

    def sibling(x):
        return lax.ppermute(
            x, "seq", [(a * CORES + e, a * CORES + 1 - e) for a in range(planes) for e in range(CORES)]
        )

    def partner(x, bit):
        return lax.ppermute(x, "mlp", [(a, a ^ bit) for a in range(mlp_count)])

    def after(x, dep):
        return lax.optimization_barrier((x, dep))

    def add(a, b):
        return (a.astype(F32) + b.astype(F32)).astype(BF16)

    def gather_step(state, t):
        ups, downs = state
        ups.append(move(ups[-1], [(i, i + 1) for i in range(t - 1, planes - 1)]))
        downs.append(move(downs[-1], [(i, i - 1) for i in range(1, planes - t + 1)]))

    def gather_slots(state):
        ups, downs = state
        return [ups[0]] + [ups[k] + downs[planes - k] for k in range(1, planes)]

    def line_gather(x):
        state = ([x], [x])
        for t in range(1, planes):
            gather_step(state, t)
        return gather_slots(state)

    def scatter_step(parts, carried, t):
        send_up, send_down = parts[t], parts[planes - t]
        if carried is not None:
            send_up, send_down = add(send_up, carried[0]), add(send_down, carried[1])
        up = move(send_up, [(i, i + 1) for i in range(0, min(t, planes - 1))])
        down = move(send_down, [(i, i - 1) for i in range(max(1, planes - t), planes)])
        return (up, down)

    half = max(1, planes // 2)
    orders = [list(range(bits)), [(b + bits // 2) % bits for b in range(bits)]]

    def mlp_scatter(x):
        out = []
        for part, order in zip((x[:half], x[half:]), orders):
            slots = {j: part[:, j] for j in range(mlp_count)}
            for b in order:
                bit = 1 << b
                sent = [j for j in sorted(slots) if j & bit]
                got = partner(jnp.stack([slots[j].astype(BF16) for j in sent], axis=0), bit)
                slots = {
                    j ^ bit: slots[j ^ bit].astype(F32) + got[i].astype(F32)
                    for i, j in enumerate(sent)
                }
            out.append(slots[0])
        return jnp.concatenate(out, axis=0)

    def mlp_gather(x):
        out = []
        for part, order in zip((x[:half], x[half:]), orders):
            slots = {0: part}
            for b in reversed(order):
                bit = 1 << b
                have = sorted(slots)
                got = partner(jnp.stack([slots[j] for j in have], axis=0), bit)
                for i, j in enumerate(have):
                    slots[j | bit] = got[i]
            out.append(jnp.stack([slots[j] for j in range(mlp_count)], axis=1))
        return jnp.concatenate(out, axis=0)

    lines = [[z * CORES + e for z in range(planes)] for e in range(CORES)]

    def line_collect(x):
        return lax.all_gather(x, "seq", axis=0, tiled=True, axis_index_groups=lines)

    def swap_halves(x):
        return jnp.where(core == 0, x, jnp.concatenate([x[..., ds:], x[..., :ds]], axis=-1))

    kv_cols = max(HD, KVH * HD // mlp_count)
    kv_first = mlp_rank * KVH // mlp_count * HD
    kv_weight = jnp.concatenate(
        [
            lax.dynamic_slice_in_dim(key_weight, kv_first, kv_cols, 1),
            lax.dynamic_slice_in_dim(value_weight, kv_first, kv_cols, 1),
        ],
        axis=1,
    )
    kv_bias = jnp.concatenate(
        [
            lax.dynamic_slice_in_dim(key_bias, kv_first, kv_cols, 0),
            lax.dynamic_slice_in_dim(value_bias, kv_first, kv_cols, 0),
        ]
    ).astype(F32)
    kv_weight, (gate_weight, up_weight, out_weight, down_weight, layer_input) = after(
        kv_weight, (gate_weight, up_weight, out_weight, down_weight, layer_input)
    )
    kv_weight = line_collect(kv_weight)
    q_weight = line_collect(query_weight)

    x = layer_input.astype(F32)
    mean_sq = jnp.mean(x * x, axis=-1, keepdims=True)
    normed = (x * lax.rsqrt(mean_sq + norm_eps) * attention_gain.astype(F32)).astype(BF16)
    even = jnp.concatenate([normed[:, CORES * z * ds : (CORES * z + 1) * ds] for z in range(planes)], axis=1)
    odd = jnp.concatenate([normed[:, (CORES * z + 1) * ds : CORES * (z + 1) * ds] for z in range(planes)], axis=1)
    mine = jnp.where(core == 0, even, odd)
    theirs = sibling(jnp.where(core == 0, odd, even))
    both = jnp.concatenate([mine, theirs], axis=0)

    units = gate_weight.shape[1]
    whole = units // HD * HD
    glu_own = jnp.concatenate(
        [gate_weight[:, :whole], up_weight[:, :whole], gate_weight[:, whole:], up_weight[:, whole:]],
        axis=1,
    )
    glu_own = lax.optimization_barrier(glu_own)
    glu_weight = jnp.concatenate(
        [
            jnp.pad(jnp.concatenate([glu_own, sibling(glu_own)], axis=0), ((0, 0), (0, HD))),
            jnp.pad(jnp.eye(HD, dtype=BF16), ((0, 0), (2 * units, 0))),
        ],
        axis=0,
    )
    out_wide = jnp.concatenate([out_weight, sibling(out_weight)], axis=1)
    down_wide = jnp.concatenate([down_weight, sibling(down_weight)], axis=1)

    both, glu_weight, out_wide, down_wide = lax.optimization_barrier(
        (both, glu_weight, out_wide, down_wide)
    )

    row_ids = seq_rank * rows + jnp.arange(rows, dtype=jnp.int32)
    stream = lookup(piece_order, row_ids // piece_len) * piece_len + row_ids % piece_len
    doc_ends = jnp.cumsum(doc_lengths)
    segment = jnp.sum((stream[:, None] >= doc_ends[None, :]).astype(jnp.int32), axis=1)
    doc_first = lookup(doc_ends - doc_lengths, segment)
    cosine, sine = rope_tables(stream - doc_first, HD)

    kv_heads = kv_cols // HD
    kv = jnp.dot(both, kv_weight, preferred_element_type=F32)
    joined = pl.pallas_call(
        join_kernel, out_shape=jax.ShapeDtypeStruct((rows, 2 * kv_cols), BF16)
    )(kv, sibling(kv[rows:]), kv_bias[None, :], cosine, sine)
    core_rows = jnp.concatenate(line_gather(joined), axis=0)
    kv_rows = jnp.concatenate([core_rows, sibling(core_rows)], axis=0)
    offsets = (plane - jnp.arange(planes, dtype=jnp.int32)) % planes
    slots = jnp.concatenate([offsets * CORES + core, offsets * CORES + 1 - core])
    slots = (slots[:, None] * PIECES_DEV + jnp.arange(PIECES_DEV, dtype=jnp.int32)).reshape(-1)
    piece_stream = lookup(piece_order, slots)

    own_cols = KVH * HD // mlp_count
    cache_width = 2 * own_cols
    offset = mlp_rank % max(1, HD // own_cols) * cache_width
    pieces = jnp.arange(piece_order.shape[0], dtype=jnp.int32)
    pages = []
    for p in range(PIECES_DEV):
        stream_piece = jnp.sum(jnp.where(cache_page == seq_rank * PIECES_DEV + p, pieces, 0))
        source = jnp.sum(jnp.where(piece_stream == stream_piece, pieces, 0))
        pages.append(lax.dynamic_slice(kv_rows, (source * piece_len, offset), (piece_len, cache_width)))
    kv_cache = jnp.concatenate(pages, axis=0)

    layer_input, q_weight = after(layer_input, q_weight)
    own_share = lax.dynamic_slice_in_dim(layer_input, mlp_rank * share, share, 0)
    lane_parts = []
    for k in range(planes):
        part = lax.dynamic_slice_in_dim(own_share, (plane + k) % planes * dz, dz, 1)
        if k:
            part = move(part, [(i, (i + k) % planes) for i in range(planes)])
        lane_parts.append(part)
    lane_input = swap_halves(jnp.stack(lane_parts, axis=0))
    lane_input = lane_input.reshape(planes, chunks, sub, dz)
    gain_lane = swap_halves(lax.dynamic_slice_in_dim(feedforward_gain, plane * dz, dz, 0)).astype(F32)
    query = jnp.dot(both, q_weight, preferred_element_type=F32)
    query_sib, lane_input = after(sibling(query[rows:]), lane_input)
    mixed = attend(
        query, query_sib, query_bias.astype(F32)[None, :], cosine, sine, kv_rows, doc_first, stream, piece_stream, kv_heads
    )
    chunked = [
        jnp.concatenate(
            [
                lax.dynamic_slice_in_dim(mixed, (mlp_rank ^ j) * share + h * sub, sub, 0)
                for j in range(mlp_count)
            ],
            axis=0,
        )
        for h in range(chunks)
    ]

    collected = [line_collect(v) for v in chunked]

    def attn_sum(h):
        heads = jnp.concatenate(
            [
                lax.dynamic_slice_in_dim(collected[h], (plane - k) % planes * crows, crows, 0)
                for k in range(planes)
            ],
            axis=0,
        )
        attn = jnp.dot(heads, out_wide, preferred_element_type=F32).astype(BF16)
        attn = mlp_scatter(attn.reshape(planes, mlp_count, sub, dz))
        return lane_input[:, h].astype(F32) + attn

    def contract(residual):
        square = residual * residual
        square = sum(square[..., i : i + HD] for i in range(0, dz, HD))
        lane = jnp.concatenate([(residual * gain_lane).astype(BF16), square.astype(BF16)], axis=-1)
        lane = mlp_gather(lane).reshape(planes * crows, dz + HD)
        part = jnp.dot(lane, glu_weight, preferred_element_type=F32)
        return part.astype(BF16).reshape(planes, crows, 2 * units + HD)

    def activate(part, carried):
        act = part[0].astype(F32) + carried[0].astype(F32) + carried[1].astype(F32)
        square = jnp.sum(act[:, 2 * units :], axis=1, keepdims=True)
        act = act * lax.rsqrt(square / width + norm_eps)
        hidden = jax.nn.silu(act[:, :whole]) * act[:, whole : 2 * whole]
        if units > whole:
            last = act[:, 2 * whole : 2 * units]
            edge = units - whole
            hidden = jnp.concatenate(
                [hidden, jax.nn.silu(last[:, :edge]) * last[:, edge:]], axis=1
            )
        return hidden.astype(BF16)

    steps = planes - 1
    delay = max(1, steps - 1)
    residuals, parts = [None] * chunks, [None] * chunks
    carried, states = [None] * chunks, [None] * chunks
    residuals[0] = attn_sum(0)
    parts[0] = contract(residuals[0])
    if chunks > 1:
        parts[0], collected[1] = after(parts[0], collected[1])
    for g in range(1, 2 * steps + (chunks - 1) * delay + 1):
        for h in range(chunks):
            t = g - h * delay
            if 1 <= t <= steps:
                carried[h] = scatter_step(parts[h], carried[h], t)
            elif steps < t <= 2 * steps:
                if t == steps + 1:
                    hidden = activate(parts[h], carried[h])
                    states[h] = ([hidden], [hidden])
                gather_step(states[h], t - steps)
        if chunks > 1:
            flight = []
            for h in range(chunks):
                t = g - h * delay
                if 1 <= t <= steps:
                    flight.append(carried[h])
                elif steps < t <= 2 * steps:
                    flight.append((states[h][0][-1], states[h][1][-1]))
            if g == 1:
                residuals[1] = attn_sum(1)
                flight.append(residuals[1])
            if g == delay:
                parts[1] = contract(residuals[1])
                flight.append(parts[1])
            flight = list(lax.optimization_barrier(tuple(flight)))
            if g == delay:
                parts[1] = flight.pop()
            if g == 1:
                residuals[1] = flight.pop()
            for h in range(chunks):
                t = g - h * delay
                if 1 <= t <= steps:
                    carried[h] = flight.pop(0)
                elif steps < t <= 2 * steps:
                    states[h][0][-1], states[h][1][-1] = flight.pop(0)

    finals = []
    for h in range(chunks):
        hidden = jnp.concatenate(gather_slots(states[h]), axis=0)
        down = jnp.dot(hidden, down_wide, preferred_element_type=F32).astype(BF16)
        down = mlp_scatter(down.reshape(planes, mlp_count, sub, dz))
        final = (residuals[h] + down).astype(BF16)
        finals.append(
            jnp.stack(
                [final[0]]
                + [move(final[k], [(i, (i - k) % planes) for i in range(planes)]) for k in range(1, planes)]
            )
        )
    final = swap_halves(jnp.concatenate(finals, axis=1))
    final = lax.dynamic_slice_in_dim(
        jnp.concatenate([final, final], axis=0), (planes - plane) % planes, planes, 0
    )
    layer_output = jnp.swapaxes(final, 0, 1).reshape(share, width)
    return (layer_output, kv_cache)


def solution(mesh):
    placed = (
        P("seq", None),
        P(),
        P(),
        P("seq", "mlp"),
        P("seq", None),
        P("seq", None),
        P("mlp", "seq"),
        P("seq", "mlp"),
        P("seq", "mlp"),
        P("mlp", "seq"),
        P("mlp"),
        P(),
        P(),
        P(),
        P(),
        P(),
    )
    return jax.shard_map(
        shards,
        mesh=mesh,
        in_specs=placed,
        out_specs=(P(("seq", "mlp"), None), P("seq", "mlp")),
        check_vma=False,
    )
```

```python
import math

import jax
import jax.numpy as jnp
from jax import lax
from jax.experimental import pallas as pl
from jax.experimental.pallas import tpu as pltpu
from jax.sharding import PartitionSpec as P

KVH = 8
HD = 128
PIECES_DEV = 2
CORES = 2

rope_base = 1000000.0
norm_eps = 1e-06
far_below = -1e30
start_top = -1e29
F32 = jnp.float32
BF16 = jnp.bfloat16


def rope_tables(position, head_dim):
    half_dim = head_dim // 2
    inverse_freq = jnp.power(
        jnp.float32(rope_base), -2.0 * jnp.arange(half_dim, dtype=jnp.float32) / head_dim
    )
    angles = position.astype(jnp.float32)[:, None] * inverse_freq[None, :]
    cosine, sine = jnp.cos(angles), jnp.sin(angles)
    return (jnp.concatenate([cosine, cosine], axis=1), jnp.concatenate([-sine, sine], axis=1))


def rotate_wide(values, cosine, sine):
    return values * cosine + pltpu.roll(values, HD // 2, 1) * sine


def lookup(small_table, indices):
    matches = indices[:, None] == jnp.arange(small_table.shape[0], dtype=jnp.int32)[None, :]
    return jnp.sum(jnp.where(matches, small_table[None, :], 0), axis=1)


def attend_kernel(
    count, active, piece_stream, own_ref, sib_ref, bias_ref, cos_ref, sin_ref, k_ref, v_ref, lo_ref, hi_ref, o_ref, acc_ref
):
    slot = pl.program_id(1)
    piece_len = k_ref.shape[0] // piece_stream.shape[0]
    rows, wide = own_ref.shape
    per_kv = wide // HD
    scale = 1.0 / math.sqrt(HD)
    cosine, sine = cos_ref[...], sin_ref[...]
    query = own_ref[...] + sib_ref[...] + bias_ref[...]
    q = jnp.concatenate(
        [
            rotate_wide(query[:, i * HD : (i + 1) * HD], cosine, sine).astype(BF16)
            for i in range(per_kv)
        ],
        axis=0,
    )
    lo = lo_ref[0]
    hi = hi_ref[0]
    acc_ref[...] = jnp.zeros_like(acc_ref)

    def step(i, carry):
        top, total = carry
        piece = active[slot, i]
        first = pl.multiple_of(piece * piece_len, piece_len)
        k = k_ref[pl.ds(first, piece_len), :]
        v = v_ref[pl.ds(first, piece_len), :]
        s = lax.dot_general(k, q, (((1,), (1,)), ((), ())), preferred_element_type=F32) * scale
        stream = piece_stream[piece] * piece_len + lax.broadcasted_iota(jnp.int32, s.shape, 0)
        s = jnp.where((stream >= lo) & (stream <= hi), s, far_below)
        new_top = jnp.maximum(top, jnp.max(s, axis=0, keepdims=True))
        w = jnp.exp(s - new_top)
        fade = jnp.exp(top - new_top)
        total = total * fade + jnp.sum(w, axis=0, keepdims=True)
        part = lax.dot_general(v, w.astype(BF16), (((0,), (0,)), ((), ())), preferred_element_type=F32)
        acc_ref[...] = acc_ref[...] * fade + part
        return (new_top, total)

    top = jnp.full((1, q.shape[0]), start_top, F32)
    total = jnp.zeros((1, q.shape[0]), F32)
    top, total = lax.fori_loop(0, count[slot], step, (top, total))
    out = (acc_ref[...] / total).T.astype(BF16)
    for i in range(per_kv):
        o_ref[:, i * HD : (i + 1) * HD] = out[i * rows : (i + 1) * rows]


def attend(query, query_sib, bias, cosine, sine, kv_rows, lo, hi, piece_stream, kv_heads):
    rows, width = query_sib.shape
    slots = PIECES_DEV
    lo, hi = lo.reshape(slots, -1), hi.reshape(slots, -1)
    per_kv = width // (kv_heads * HD)
    keys = kv_rows.shape[0]
    pieces = piece_stream.shape[0]
    piece_len = keys // pieces
    first = piece_stream[None, None, :] * piece_len
    touch = jnp.any(
        (lo[:, :, None] <= first + piece_len - 1) & (hi[:, :, None] >= first), axis=1
    ).astype(jnp.int32)
    place = jnp.cumsum(touch, axis=1) - 1
    ids = jnp.arange(pieces, dtype=jnp.int32)
    active = jnp.sum(
        jnp.where((touch[:, :, None] > 0) & (place[:, :, None] == ids), ids[None, :, None], 0), axis=1
    ).astype(jnp.int32)
    count = jnp.sum(touch, axis=1).astype(jnp.int32)
    lo_wide = jnp.tile(lo, (1, per_kv))[:, None, :]
    hi_wide = jnp.tile(hi, (1, per_kv))[:, None, :]
    tile = (piece_len, per_kv * HD)
    return pl.pallas_call(
        attend_kernel,
        grid_spec=pltpu.PrefetchScalarGridSpec(
            num_scalar_prefetch=3,
            grid=(kv_heads, slots),
            in_specs=[
                pl.BlockSpec(tile, lambda g, h, *_: (h, g)),
                pl.BlockSpec(tile, lambda g, h, *_: (h, g)),
                pl.BlockSpec((1, per_kv * HD), lambda g, h, *_: (0, g)),
                pl.BlockSpec((piece_len, HD), lambda g, h, *_: (h, 0)),
                pl.BlockSpec((piece_len, HD), lambda g, h, *_: (h, 0)),
                pl.BlockSpec((keys, HD), lambda g, h, *_: (0, 2 * g)),
                pl.BlockSpec((keys, HD), lambda g, h, *_: (0, 2 * g + 1)),
                pl.BlockSpec((1, 1, piece_len * per_kv), lambda g, h, *_: (h, 0, 0)),
                pl.BlockSpec((1, 1, piece_len * per_kv), lambda g, h, *_: (h, 0, 0)),
            ],
            out_specs=pl.BlockSpec(tile, lambda g, h, *_: (h, g)),
            scratch_shapes=[pltpu.VMEM((HD, piece_len * per_kv), F32)],
        ),
        out_shape=jax.ShapeDtypeStruct((rows, width), BF16),
        compiler_params=pltpu.CompilerParams(vmem_limit_bytes=32 * 2**20),
    )(count, active, piece_stream, query, query_sib, bias, cosine, sine, kv_rows, kv_rows, lo_wide, hi_wide)


def product_kernel(x_ref, w_ref, o_ref):
    o_ref[...] = jnp.dot(x_ref[...], w_ref[...], preferred_element_type=F32).astype(o_ref.dtype)


def product(x, w, out_type):
    rows, inner = x.shape
    cols = w.shape[1]
    tile = next((t for t in (512, 384, 256) if cols % t == 0), cols)
    return pl.pallas_call(
        product_kernel,
        grid=(cols // tile,),
        in_specs=[
            pl.BlockSpec((rows, inner), lambda n: (0, 0)),
            pl.BlockSpec((inner, tile), lambda n: (0, n)),
        ],
        out_specs=pl.BlockSpec((rows, tile), lambda n: (0, n)),
        out_shape=jax.ShapeDtypeStruct((rows, cols), out_type),
        cost_estimate=pl.CostEstimate(flops=0, transcendentals=0, bytes_accessed=0),
        compiler_params=pltpu.CompilerParams(vmem_limit_bytes=48 * 2**20),
    )(x, w)


def join_kernel(own_ref, sib_ref, bias_ref, cos_ref, sin_ref, o_ref):
    rows, wide = o_ref.shape
    heads = wide // (2 * HD)
    cosine, sine = cos_ref[...], sin_ref[...]
    kv = own_ref[:rows, :] + sib_ref[...] + bias_ref[...]
    for g in range(heads):
        key = rotate_wide(kv[:, g * HD : (g + 1) * HD], cosine, sine)
        o_ref[:, 2 * g * HD : (2 * g + 1) * HD] = key.astype(BF16)
        value = kv[:, (heads + g) * HD : (heads + g + 1) * HD]
        o_ref[:, (2 * g + 1) * HD : (2 * g + 2) * HD] = value.astype(BF16)


def shards(
    layer_input,
    attention_gain,
    feedforward_gain,
    query_weight,
    key_weight,
    value_weight,
    out_weight,
    gate_weight,
    up_weight,
    down_weight,
    query_bias,
    key_bias,
    value_bias,
    doc_lengths,
    piece_order,
    cache_page,
):
    seq_count = lax.axis_size("seq")
    mlp_count = lax.axis_size("mlp")
    seq_rank = lax.axis_index("seq")
    mlp_rank = lax.axis_index("mlp")
    planes = seq_count // CORES
    plane = seq_rank // CORES
    core = seq_rank % CORES
    rows, width = layer_input.shape
    dz = width // planes
    ds = width // seq_count
    share = rows // mlp_count
    chunks = 2 if share % 32 == 0 else 1
    sub = share // chunks
    crows = mlp_count * sub
    piece_len = rows // PIECES_DEV
    bits = mlp_count.bit_length() - 1

    def move(x, pairs):
        return lax.ppermute(
            x, "seq", [(a * CORES + e, b * CORES + e) for a, b in pairs for e in range(CORES)]
        )

    def sibling(x):
        return lax.ppermute(
            x, "seq", [(a * CORES + e, a * CORES + 1 - e) for a in range(planes) for e in range(CORES)]
        )

    def partner(x, bit):
        return lax.ppermute(x, "mlp", [(a, a ^ bit) for a in range(mlp_count)])

    def after(x, dep):
        return lax.optimization_barrier((x, dep))

    def add(a, b):
        return (a.astype(F32) + b.astype(F32)).astype(BF16)

    def gather_step(state, t):
        ups, downs = state
        ups.append(move(ups[-1], [(i, i + 1) for i in range(t - 1, planes - 1)]))
        downs.append(move(downs[-1], [(i, i - 1) for i in range(1, planes - t + 1)]))

    def gather_slots(state):
        ups, downs = state
        return [ups[0]] + [ups[k] + downs[planes - k] for k in range(1, planes)]

    def line_gather(x):
        state = ([x], [x])
        for t in range(1, planes):
            gather_step(state, t)
        return gather_slots(state)

    def scatter_step(parts, carried, t, held=()):
        send_up, send_down = parts[t], parts[planes - t]
        if carried is not None:
            send_up, send_down = add(send_up, carried[0]), add(send_down, carried[1])
        send_up, send_down, held = lax.optimization_barrier((send_up, send_down, held))
        up = move(send_up, [(i, i + 1) for i in range(0, min(t, planes - 1))])
        down = move(send_down, [(i, i - 1) for i in range(max(1, planes - t), planes)])
        return (up, down), held

    half = max(1, planes // 2)
    orders = [list(range(bits)), [(b + bits // 2) % bits for b in range(bits)]]

    def mlp_scatter(x):
        out = []
        for part, order in zip((x[:half], x[half:]), orders):
            slots = {j: part[:, j] for j in range(mlp_count)}
            for b in order:
                bit = 1 << b
                sent = [j for j in sorted(slots) if j & bit]
                got = partner(jnp.stack([slots[j].astype(BF16) for j in sent], axis=0), bit)
                slots = {
                    j ^ bit: slots[j ^ bit].astype(F32) + got[i].astype(F32)
                    for i, j in enumerate(sent)
                }
            out.append(slots[0])
        return jnp.concatenate(out, axis=0)

    def mlp_gather(x):
        out = []
        for part, order in zip((x[:half], x[half:]), orders):
            slots = {0: part}
            for b in reversed(order):
                bit = 1 << b
                have = sorted(slots)
                got = partner(jnp.stack([slots[j] for j in have], axis=0), bit)
                for i, j in enumerate(have):
                    slots[j | bit] = got[i]
            out.append(jnp.stack([slots[j] for j in range(mlp_count)], axis=1))
        return out

    lines = [[z * CORES + e for z in range(planes)] for e in range(CORES)]

    def line_collect(x):
        return lax.all_gather(x, "seq", axis=0, tiled=True, axis_index_groups=lines)

    def swap_halves(x):
        return jnp.where(core == 0, x, jnp.concatenate([x[..., ds:], x[..., :ds]], axis=-1))

    order = []
    for k in range(1, planes // 2 + 1):
        order += [k] if 2 * k == planes else [k, planes - k]
    order.append(0)
    own_share = lax.dynamic_slice_in_dim(layer_input, mlp_rank * share, share, 0)
    lane_parts = []
    for k in order:
        part = lax.dynamic_slice_in_dim(own_share, (plane + k) % planes * dz, dz, 1)
        if k:
            part = move(part, [(i, (i + k) % planes) for i in range(planes)])
        lane_parts.append(part)

    kv_cols = max(HD, KVH * HD // mlp_count)
    kv_first = mlp_rank * KVH // mlp_count * HD
    kv_weight = jnp.concatenate(
        [
            lax.dynamic_slice_in_dim(key_weight, kv_first, kv_cols, 1),
            lax.dynamic_slice_in_dim(value_weight, kv_first, kv_cols, 1),
        ],
        axis=1,
    )
    kv_bias = jnp.concatenate(
        [
            lax.dynamic_slice_in_dim(key_bias, kv_first, kv_cols, 0),
            lax.dynamic_slice_in_dim(value_bias, kv_first, kv_cols, 0),
        ]
    ).astype(F32)
    kv_weight, (gate_weight, up_weight, out_weight, down_weight, layer_input) = after(
        kv_weight, (gate_weight, up_weight, out_weight, down_weight, layer_input)
    )
    kv_weight = line_collect(kv_weight)
    q_weight = line_collect(query_weight)

    x = layer_input.astype(F32)
    mean_sq = jnp.mean(x * x, axis=-1, keepdims=True)
    normed = (x * lax.rsqrt(mean_sq + norm_eps) * attention_gain.astype(F32)).astype(BF16)
    even = jnp.concatenate([normed[:, CORES * z * ds : (CORES * z + 1) * ds] for z in range(planes)], axis=1)
    odd = jnp.concatenate([normed[:, (CORES * z + 1) * ds : CORES * (z + 1) * ds] for z in range(planes)], axis=1)
    mine = jnp.where(core == 0, even, odd)
    theirs = sibling(jnp.where(core == 0, odd, even))
    both = jnp.concatenate([mine, theirs], axis=0)

    units = gate_weight.shape[1]
    whole = units // HD * HD
    glu_own = jnp.concatenate(
        [gate_weight[:, :whole], up_weight[:, :whole], gate_weight[:, whole:], up_weight[:, whole:]],
        axis=1,
    )
    glu_own = lax.optimization_barrier(glu_own)
    glu_weight = jnp.concatenate(
        [
            jnp.pad(jnp.concatenate([glu_own, sibling(glu_own)], axis=0), ((0, 0), (0, HD))),
            jnp.pad(jnp.eye(HD, dtype=BF16), ((0, 0), (2 * units, 0))),
        ],
        axis=0,
    )
    out_wide = jnp.concatenate([out_weight, sibling(out_weight)], axis=1)
    down_wide = jnp.concatenate([down_weight, sibling(down_weight)], axis=1)

    lane_input = swap_halves(jnp.stack(lane_parts, axis=0)).reshape(planes, chunks, sub, dz)
    gain_lane = swap_halves(lax.dynamic_slice_in_dim(feedforward_gain, plane * dz, dz, 0)).astype(F32)
    both, glu_weight, out_wide, down_wide, lane_input = lax.optimization_barrier(
        (both, glu_weight, out_wide, down_wide, lane_input)
    )

    row_ids = seq_rank * rows + jnp.arange(rows, dtype=jnp.int32)
    stream = lookup(piece_order, row_ids // piece_len) * piece_len + row_ids % piece_len
    doc_ends = jnp.cumsum(doc_lengths)
    segment = jnp.sum((stream[:, None] >= doc_ends[None, :]).astype(jnp.int32), axis=1)
    doc_first = lookup(doc_ends - doc_lengths, segment)
    cosine, sine = rope_tables(stream - doc_first, HD)

    kv_heads = kv_cols // HD
    kv = product(both, kv_weight, F32)
    joined = pl.pallas_call(
        join_kernel, out_shape=jax.ShapeDtypeStruct((rows, 2 * kv_cols), BF16)
    )(kv, sibling(kv[rows:]), kv_bias[None, :], cosine, sine)
    core_rows = jnp.concatenate(line_gather(joined), axis=0)
    kv_rows = jnp.concatenate([core_rows, sibling(core_rows)], axis=0)
    offsets = (plane - jnp.arange(planes, dtype=jnp.int32)) % planes
    slots = jnp.concatenate([offsets * CORES + core, offsets * CORES + 1 - core])
    slots = (slots[:, None] * PIECES_DEV + jnp.arange(PIECES_DEV, dtype=jnp.int32)).reshape(-1)
    piece_stream = lookup(piece_order, slots)

    own_cols = KVH * HD // mlp_count
    cache_width = 2 * own_cols
    offset = mlp_rank % max(1, HD // own_cols) * cache_width
    pieces = jnp.arange(piece_order.shape[0], dtype=jnp.int32)
    pages = []
    for p in range(PIECES_DEV):
        stream_piece = jnp.sum(jnp.where(cache_page == seq_rank * PIECES_DEV + p, pieces, 0))
        source = jnp.sum(jnp.where(piece_stream == stream_piece, pieces, 0))
        pages.append(lax.dynamic_slice(kv_rows, (source * piece_len, offset), (piece_len, cache_width)))
    kv_cache = jnp.concatenate(pages, axis=0)

    query = product(both, q_weight, F32)
    query_sib = sibling(query[rows:])
    mixed = attend(
        query, query_sib, query_bias.astype(F32)[None, :], cosine, sine, kv_rows, doc_first, stream, piece_stream, kv_heads
    )
    chunked = [
        jnp.concatenate(
            [
                lax.dynamic_slice_in_dim(mixed, (mlp_rank ^ j) * share + h * sub, sub, 0)
                for j in range(mlp_count)
            ],
            axis=0,
        )
        for h in range(chunks)
    ]

    collected = [line_collect(v) for v in chunked]

    def attn_sum(h):
        heads = jnp.concatenate(
            [
                lax.dynamic_slice_in_dim(collected[h], (plane - k) % planes * crows, crows, 0)
                for k in order
            ],
            axis=0,
        )
        attn = product(heads, out_wide, BF16)
        attn = mlp_scatter(attn.reshape(planes, mlp_count, sub, dz))
        return lane_input[:, h].astype(F32) + attn

    def spread(residual):
        square = residual * residual
        square = sum(square[..., i : i + HD] for i in range(0, dz, HD))
        lane = jnp.concatenate([(residual * gain_lane).astype(BF16), square.astype(BF16)], axis=-1)
        return mlp_gather(lane)

    def contract_half(lane):
        part = product(lane.reshape(-1, dz + HD), glu_weight, BF16).reshape(-1, crows, 2 * units + HD)
        return [part[i] for i in range(part.shape[0])]

    def contract(lanes):
        first = contract_half(lanes[0])
        last, first[0] = after(lanes[1], first[0])
        return dict(zip(order, first + contract_half(last)))

    def activate(part, carried):
        act = part[0].astype(F32) + carried[0].astype(F32) + carried[1].astype(F32)
        square = jnp.sum(act[:, 2 * units :], axis=1, keepdims=True)
        act = act * lax.rsqrt(square / width + norm_eps)
        hidden = jax.nn.silu(act[:, :whole]) * act[:, whole : 2 * whole]
        if units > whole:
            last = act[:, 2 * whole : 2 * units]
            edge = units - whole
            hidden = jnp.concatenate(
                [hidden, jax.nn.silu(last[:, :edge]) * last[:, edge:]], axis=1
            )
        return hidden.astype(BF16)

    def deliver(h, down):
        final = (residuals[h] + down).astype(BF16)
        found = {
            k: move(final[i], [(p, (p - k) % planes) for p in range(planes)]) if k else final[i]
            for i, k in enumerate(order)
        }
        return jnp.stack([found[k] for k in range(planes)])

    def project_down(state):
        slots = gather_slots(state)
        hidden = jnp.concatenate([slots[k] for k in order], axis=0)
        down = product(hidden, down_wide, BF16)
        return mlp_scatter(down.reshape(planes, mlp_count, sub, dz))

    steps = planes - 1
    residuals = [attn_sum(0)]
    lanes = spread(residuals[0])
    first = contract_half(lanes[0])
    carried, last = scatter_step(dict(zip(order, first)), None, 1, lanes[1])
    parts = dict(zip(order, first + contract_half(last)))
    queued = None
    for t in range(1, steps + 1):
        if t > 1:
            carried, queued = scatter_step(parts, carried, t, queued)
        if chunks > 1:
            if t == 1:
                collected[1], carried = after(collected[1], carried)
            if t == min(2, steps):
                residuals.append(attn_sum(1))
                queued, carried = after(residuals[1], carried)
            if t == steps:
                queued = contract(spread(queued))
    finals = []
    for h in range(chunks):
        following = queued if h + 1 < chunks else None
        ahead = None
        if following is not None:
            ahead, carried = scatter_step(following, None, 1, carried)
        hidden = activate(parts, carried)
        state = ([hidden], [hidden])
        if following is None:
            for t in range(1, steps + 1):
                gather_step(state, t)
            finals.append(deliver(h, project_down(state)))
            continue
        gather_step(state, 1)
        gather_step(state, 2)
        for t in range(2, steps + 1):
            ahead, (state[0][-1], state[1][-1]) = after(ahead, (state[0][-1], state[1][-1]))
            ahead, (state[0][-1], state[1][-1]) = scatter_step(
                following, ahead, t, (state[0][-1], state[1][-1])
            )
            if t < steps:
                gather_step(state, t + 1)
        down = project_down(state)
        down, carried = after(down, ahead)
        parts = following
        finals.append(deliver(h, down))
    final = swap_halves(jnp.concatenate(finals, axis=1))
    final = lax.dynamic_slice_in_dim(
        jnp.concatenate([final, final], axis=0), (planes - plane) % planes, planes, 0
    )
    layer_output = jnp.swapaxes(final, 0, 1).reshape(share, width)
    return (layer_output, kv_cache)


def solution(mesh):
    placed = (
        P("seq", None),
        P(),
        P(),
        P("seq", "mlp"),
        P("seq", None),
        P("seq", None),
        P("mlp", "seq"),
        P("seq", "mlp"),
        P("seq", "mlp"),
        P("mlp", "seq"),
        P("mlp"),
        P(),
        P(),
        P(),
        P(),
        P(),
    )
    return jax.shard_map(
        shards,
        mesh=mesh,
        in_specs=placed,
        out_specs=(P(("seq", "mlp"), None), P("seq", "mlp")),
        check_vma=False,
    )
```

```python
import math

import jax
import jax.numpy as jnp
from jax import lax
from jax.experimental import pallas as pl
from jax.experimental.pallas import tpu as pltpu
from jax.sharding import PartitionSpec as P

KVH = 8
HD = 128
PIECES_DEV = 2
CORES = 2

rope_base = 1000000.0
norm_eps = 1e-06
far_below = -1e30
start_top = -1e29
F32 = jnp.float32
BF16 = jnp.bfloat16


def rope_tables(position, head_dim):
    half_dim = head_dim // 2
    inverse_freq = jnp.power(
        jnp.float32(rope_base), -2.0 * jnp.arange(half_dim, dtype=jnp.float32) / head_dim
    )
    angles = position.astype(jnp.float32)[:, None] * inverse_freq[None, :]
    cosine, sine = jnp.cos(angles), jnp.sin(angles)
    return (jnp.concatenate([cosine, cosine], axis=1), jnp.concatenate([-sine, sine], axis=1))


def rotate_wide(values, cosine, sine):
    return values * cosine + pltpu.roll(values, HD // 2, 1) * sine


def lookup(small_table, indices):
    matches = indices[:, None] == jnp.arange(small_table.shape[0], dtype=jnp.int32)[None, :]
    return jnp.sum(jnp.where(matches, small_table[None, :], 0), axis=1)


def attend_kernel(
    count, active, piece_stream, own_ref, sib_ref, bias_ref, cos_ref, sin_ref, k_ref, v_ref, lo_ref, hi_ref, o_ref, acc_ref
):
    slot = pl.program_id(1)
    piece_len = k_ref.shape[0] // piece_stream.shape[0]
    rows, wide = own_ref.shape
    per_kv = wide // HD
    scale = 1.0 / math.sqrt(HD)
    cosine, sine = cos_ref[...], sin_ref[...]
    query = own_ref[...] + sib_ref[...] + bias_ref[...]
    q = jnp.concatenate(
        [
            rotate_wide(query[:, i * HD : (i + 1) * HD], cosine, sine).astype(BF16)
            for i in range(per_kv)
        ],
        axis=0,
    )
    lo = lo_ref[0]
    hi = hi_ref[0]
    acc_ref[...] = jnp.zeros_like(acc_ref)

    def step(i, carry):
        top, total = carry
        piece = active[slot, i]
        first = pl.multiple_of(piece * piece_len, piece_len)
        k = k_ref[pl.ds(first, piece_len), :]
        v = v_ref[pl.ds(first, piece_len), :]
        s = lax.dot_general(k, q, (((1,), (1,)), ((), ())), preferred_element_type=F32) * scale
        stream = piece_stream[piece] * piece_len + lax.broadcasted_iota(jnp.int32, s.shape, 0)
        s = jnp.where((stream >= lo) & (stream <= hi), s, far_below)
        new_top = jnp.maximum(top, jnp.max(s, axis=0, keepdims=True))
        w = jnp.exp(s - new_top)
        fade = jnp.exp(top - new_top)
        total = total * fade + jnp.sum(w, axis=0, keepdims=True)
        part = lax.dot_general(v, w.astype(BF16), (((0,), (0,)), ((), ())), preferred_element_type=F32)
        acc_ref[...] = acc_ref[...] * fade + part
        return (new_top, total)

    top = jnp.full((1, q.shape[0]), start_top, F32)
    total = jnp.zeros((1, q.shape[0]), F32)
    top, total = lax.fori_loop(0, count[slot], step, (top, total))
    out = (acc_ref[...] / total).T.astype(BF16)
    for i in range(per_kv):
        o_ref[:, i * HD : (i + 1) * HD] = out[i * rows : (i + 1) * rows]


def attend(query, query_sib, bias, cosine, sine, kv_rows, lo, hi, piece_stream, kv_heads):
    rows, width = query_sib.shape
    slots = PIECES_DEV
    lo, hi = lo.reshape(slots, -1), hi.reshape(slots, -1)
    per_kv = width // (kv_heads * HD)
    keys = kv_rows.shape[0]
    pieces = piece_stream.shape[0]
    piece_len = keys // pieces
    first = piece_stream[None, None, :] * piece_len
    touch = jnp.any(
        (lo[:, :, None] <= first + piece_len - 1) & (hi[:, :, None] >= first), axis=1
    ).astype(jnp.int32)
    place = jnp.cumsum(touch, axis=1) - 1
    ids = jnp.arange(pieces, dtype=jnp.int32)
    active = jnp.sum(
        jnp.where((touch[:, :, None] > 0) & (place[:, :, None] == ids), ids[None, :, None], 0), axis=1
    ).astype(jnp.int32)
    count = jnp.sum(touch, axis=1).astype(jnp.int32)
    lo_wide = jnp.tile(lo, (1, per_kv))[:, None, :]
    hi_wide = jnp.tile(hi, (1, per_kv))[:, None, :]
    tile = (piece_len, per_kv * HD)
    return pl.pallas_call(
        attend_kernel,
        grid_spec=pltpu.PrefetchScalarGridSpec(
            num_scalar_prefetch=3,
            grid=(kv_heads, slots),
            in_specs=[
                pl.BlockSpec(tile, lambda g, h, *_: (h, g)),
                pl.BlockSpec(tile, lambda g, h, *_: (h, g)),
                pl.BlockSpec((1, per_kv * HD), lambda g, h, *_: (0, g)),
                pl.BlockSpec((piece_len, HD), lambda g, h, *_: (h, 0)),
                pl.BlockSpec((piece_len, HD), lambda g, h, *_: (h, 0)),
                pl.BlockSpec((keys, HD), lambda g, h, *_: (0, 2 * g)),
                pl.BlockSpec((keys, HD), lambda g, h, *_: (0, 2 * g + 1)),
                pl.BlockSpec((1, 1, piece_len * per_kv), lambda g, h, *_: (h, 0, 0)),
                pl.BlockSpec((1, 1, piece_len * per_kv), lambda g, h, *_: (h, 0, 0)),
            ],
            out_specs=pl.BlockSpec(tile, lambda g, h, *_: (h, g)),
            scratch_shapes=[pltpu.VMEM((HD, piece_len * per_kv), F32)],
        ),
        out_shape=jax.ShapeDtypeStruct((rows, width), BF16),
        compiler_params=pltpu.CompilerParams(vmem_limit_bytes=32 * 2**20),
    )(count, active, piece_stream, query, query_sib, bias, cosine, sine, kv_rows, kv_rows, lo_wide, hi_wide)


def product_kernel(x_ref, w_ref, o_ref):
    o_ref[...] = jnp.dot(x_ref[...], w_ref[...], preferred_element_type=F32).astype(o_ref.dtype)


def product(x, w, out_type):
    rows, inner = x.shape
    cols = w.shape[1]
    tile = next((t for t in (512, 384, 256) if cols % t == 0), cols)
    return pl.pallas_call(
        product_kernel,
        grid=(cols // tile,),
        in_specs=[
            pl.BlockSpec((rows, inner), lambda n: (0, 0)),
            pl.BlockSpec((inner, tile), lambda n: (0, n)),
        ],
        out_specs=pl.BlockSpec((rows, tile), lambda n: (0, n)),
        out_shape=jax.ShapeDtypeStruct((rows, cols), out_type),
        cost_estimate=pl.CostEstimate(flops=0, transcendentals=0, bytes_accessed=0),
        compiler_params=pltpu.CompilerParams(vmem_limit_bytes=48 * 2**20),
    )(x, w)


def join_kernel(own_ref, sib_ref, bias_ref, cos_ref, sin_ref, o_ref):
    rows, wide = o_ref.shape
    heads = wide // (2 * HD)
    cosine, sine = cos_ref[...], sin_ref[...]
    kv = own_ref[:rows, :] + sib_ref[...] + bias_ref[...]
    for g in range(heads):
        key = rotate_wide(kv[:, g * HD : (g + 1) * HD], cosine, sine)
        o_ref[:, 2 * g * HD : (2 * g + 1) * HD] = key.astype(BF16)
        value = kv[:, (heads + g) * HD : (heads + g + 1) * HD]
        o_ref[:, (2 * g + 1) * HD : (2 * g + 2) * HD] = value.astype(BF16)


def shards(
    layer_input,
    attention_gain,
    feedforward_gain,
    query_weight,
    key_weight,
    value_weight,
    out_weight,
    gate_weight,
    up_weight,
    down_weight,
    query_bias,
    key_bias,
    value_bias,
    doc_lengths,
    piece_order,
    cache_page,
):
    seq_count = lax.axis_size("seq")
    mlp_count = lax.axis_size("mlp")
    seq_rank = lax.axis_index("seq")
    mlp_rank = lax.axis_index("mlp")
    planes = seq_count // CORES
    plane = seq_rank // CORES
    core = seq_rank % CORES
    rows, width = layer_input.shape
    dz = width // planes
    ds = width // seq_count
    share = rows // mlp_count
    chunks = 2 if share % 32 == 0 and planes > 3 else 1
    sub = share // chunks
    crows = mlp_count * sub
    piece_len = rows // PIECES_DEV
    bits = mlp_count.bit_length() - 1

    def move(x, pairs):
        return lax.ppermute(
            x, "seq", [(a * CORES + e, b * CORES + e) for a, b in pairs for e in range(CORES)]
        )

    def sibling(x):
        return lax.ppermute(
            x, "seq", [(a * CORES + e, a * CORES + 1 - e) for a in range(planes) for e in range(CORES)]
        )

    def partner(x, bit):
        return lax.ppermute(x, "mlp", [(a, a ^ bit) for a in range(mlp_count)])

    def after(x, dep):
        return lax.optimization_barrier((x, dep))

    def add(a, b):
        return (a.astype(F32) + b.astype(F32)).astype(BF16)

    def gather_step(state, t):
        ups, downs = state
        ups.append(move(ups[-1], [(i, i + 1) for i in range(t - 1, planes - 1)]))
        downs.append(move(downs[-1], [(i, i - 1) for i in range(1, planes - t + 1)]))

    def gather_slots(state):
        ups, downs = state
        return [ups[0]] + [ups[k] + downs[planes - k] for k in range(1, planes)]

    def line_gather(x):
        state = ([x], [x])
        for t in range(1, planes):
            gather_step(state, t)
        return gather_slots(state)

    def scatter_step(parts, carried, t, held=()):
        send_up, send_down = parts[t], parts[planes - t]
        if carried is not None:
            send_up, send_down = add(send_up, carried[0]), add(send_down, carried[1])
        send_up, send_down, held = lax.optimization_barrier((send_up, send_down, held))
        up = move(send_up, [(i, i + 1) for i in range(0, min(t, planes - 1))])
        down = move(send_down, [(i, i - 1) for i in range(max(1, planes - t), planes)])
        return (up, down), held

    half = max(1, planes // 2)
    orders = [list(range(bits)), [(b + bits // 2) % bits for b in range(bits)]]

    def sum_begin(x):
        return [{j: part[:, j] for j in range(mlp_count)} for part in (x[:half], x[half:])]

    def sum_sent(states, n):
        return [[j for j in sorted(v) if j & (1 << o[n])] for v, o in zip(states, orders)]

    def sum_launch(states, n):
        sends = [
            jnp.stack([v[j].astype(BF16) for j in w], axis=0) for v, w in zip(states, sum_sent(states, n))
        ]
        sends = lax.optimization_barrier(sends)
        return [partner(send, 1 << o[n]) for send, o in zip(sends, orders)]

    def sum_land(states, n, gots):
        return [
            {j ^ (1 << o[n]): v[j ^ (1 << o[n])].astype(F32) + got[i].astype(F32) for i, j in enumerate(w)}
            for v, w, o, got in zip(states, sum_sent(states, n), orders, gots)
        ]

    def sum_stage(states, n):
        return sum_land(states, n, sum_launch(states, n))

    def sum_end(states):
        return jnp.concatenate([v[0] for v in states], axis=0)

    def spread_begin(x):
        return [{0: x[:half]}, {0: x[half:]}]

    def spread_launch(states, n):
        sends = [jnp.stack([v[j] for j in sorted(v)], axis=0) for v in states]
        sends = lax.optimization_barrier(sends)
        return [partner(send, 1 << o[bits - 1 - n]) for send, o in zip(sends, orders)]

    def spread_land(states, n, gots):
        return [
            v | {j | (1 << o[bits - 1 - n]): got[i] for i, j in enumerate(sorted(v))}
            for v, o, got in zip(states, orders, gots)
        ]

    def spread_stage(states, n):
        return spread_land(states, n, spread_launch(states, n))

    def spread_end(states):
        return [jnp.stack([v[j] for j in range(mlp_count)], axis=1) for v in states]

    lines = [[z * CORES + e for z in range(planes)] for e in range(CORES)]

    def line_collect(x):
        return lax.all_gather(x, "seq", axis=0, tiled=True, axis_index_groups=lines)

    def swap_halves(x):
        return jnp.where(core == 0, x, jnp.concatenate([x[..., ds:], x[..., :ds]], axis=-1))

    order = []
    for k in range(1, planes // 2 + 1):
        order += [k] if 2 * k == planes else [k, planes - k]
    order.append(0)

    kv_cols = max(HD, KVH * HD // mlp_count)
    kv_first = mlp_rank * KVH // mlp_count * HD
    kv_weight = jnp.concatenate(
        [
            lax.dynamic_slice_in_dim(key_weight, kv_first, kv_cols, 1),
            lax.dynamic_slice_in_dim(value_weight, kv_first, kv_cols, 1),
        ],
        axis=1,
    )
    kv_bias = jnp.concatenate(
        [
            lax.dynamic_slice_in_dim(key_bias, kv_first, kv_cols, 0),
            lax.dynamic_slice_in_dim(value_bias, kv_first, kv_cols, 0),
        ]
    ).astype(F32)
    kv_weight, (gate_weight, up_weight, out_weight, down_weight, layer_input) = after(
        kv_weight, (gate_weight, up_weight, out_weight, down_weight, layer_input)
    )
    kv_weight = line_collect(kv_weight)
    q_weight = line_collect(query_weight)

    x = layer_input.astype(F32)
    mean_sq = jnp.mean(x * x, axis=-1, keepdims=True)
    normed = (x * lax.rsqrt(mean_sq + norm_eps) * attention_gain.astype(F32)).astype(BF16)
    even = jnp.concatenate([normed[:, CORES * z * ds : (CORES * z + 1) * ds] for z in range(planes)], axis=1)
    odd = jnp.concatenate([normed[:, (CORES * z + 1) * ds : CORES * (z + 1) * ds] for z in range(planes)], axis=1)
    mine = jnp.where(core == 0, even, odd)
    theirs = sibling(jnp.where(core == 0, odd, even))
    both = jnp.concatenate([mine, theirs], axis=0)

    units = gate_weight.shape[1]
    whole = units // HD * HD
    glu_own = jnp.concatenate(
        [gate_weight[:, :whole], up_weight[:, :whole], gate_weight[:, whole:], up_weight[:, whole:]],
        axis=1,
    )
    glu_own = lax.optimization_barrier(glu_own)
    glu_weight = jnp.concatenate(
        [
            jnp.pad(jnp.concatenate([glu_own, sibling(glu_own)], axis=0), ((0, 0), (0, HD))),
            jnp.pad(jnp.eye(HD, dtype=BF16), ((0, 0), (2 * units, 0))),
        ],
        axis=0,
    )
    out_wide = jnp.concatenate([out_weight, sibling(out_weight)], axis=1)
    down_wide = jnp.concatenate([down_weight, sibling(down_weight)], axis=1)

    own_share = lax.dynamic_slice_in_dim(layer_input, mlp_rank * share, share, 0)
    lane_sends = [lax.dynamic_slice_in_dim(own_share, (plane + k) % planes * dz, dz, 1) for k in order]
    gain_lane = swap_halves(lax.dynamic_slice_in_dim(feedforward_gain, plane * dz, dz, 0)).astype(F32)
    both, glu_weight, out_wide, down_wide, lane_sends = lax.optimization_barrier(
        (both, glu_weight, out_wide, down_wide, lane_sends)
    )

    row_ids = seq_rank * rows + jnp.arange(rows, dtype=jnp.int32)
    stream = lookup(piece_order, row_ids // piece_len) * piece_len + row_ids % piece_len
    doc_ends = jnp.cumsum(doc_lengths)
    segment = jnp.sum((stream[:, None] >= doc_ends[None, :]).astype(jnp.int32), axis=1)
    doc_first = lookup(doc_ends - doc_lengths, segment)
    cosine, sine = rope_tables(stream - doc_first, HD)

    kv_heads = kv_cols // HD
    kv = product(both, kv_weight, F32)
    joined = pl.pallas_call(
        join_kernel, out_shape=jax.ShapeDtypeStruct((rows, 2 * kv_cols), BF16)
    )(kv, sibling(kv[rows:]), kv_bias[None, :], cosine, sine)
    core_rows = jnp.concatenate(line_gather(joined), axis=0)
    kv_rows = jnp.concatenate([core_rows, sibling(core_rows)], axis=0)
    offsets = (plane - jnp.arange(planes, dtype=jnp.int32)) % planes
    slots = jnp.concatenate([offsets * CORES + core, offsets * CORES + 1 - core])
    slots = (slots[:, None] * PIECES_DEV + jnp.arange(PIECES_DEV, dtype=jnp.int32)).reshape(-1)
    piece_stream = lookup(piece_order, slots)

    own_cols = KVH * HD // mlp_count
    cache_width = 2 * own_cols
    offset = mlp_rank % max(1, HD // own_cols) * cache_width
    pieces = jnp.arange(piece_order.shape[0], dtype=jnp.int32)
    pages = []
    for p in range(PIECES_DEV):
        stream_piece = jnp.sum(jnp.where(cache_page == seq_rank * PIECES_DEV + p, pieces, 0))
        source = jnp.sum(jnp.where(piece_stream == stream_piece, pieces, 0))
        pages.append(lax.dynamic_slice(kv_rows, (source * piece_len, offset), (piece_len, cache_width)))
    kv_cache = jnp.concatenate(pages, axis=0)

    lane_sends, q_weight = after(lane_sends, q_weight)
    lane_parts = [
        move(v, [(i, (i + k) % planes) for i in range(planes)]) if k else v
        for k, v in zip(order, lane_sends)
    ]
    query = product(both, q_weight, F32)
    query_sib, lane_parts = after(sibling(query[rows:]), lane_parts)
    lane_input = swap_halves(jnp.stack(lane_parts, axis=0)).reshape(planes, chunks, sub, dz)
    mixed = attend(
        query, query_sib, query_bias.astype(F32)[None, :], cosine, sine, kv_rows, doc_first, stream, piece_stream, kv_heads
    )
    chunked = [
        jnp.concatenate(
            [
                lax.dynamic_slice_in_dim(mixed, (mlp_rank ^ j) * share + h * sub, sub, 0)
                for j in range(mlp_count)
            ],
            axis=0,
        )
        for h in range(chunks)
    ]

    collected = [line_collect(v) for v in chunked]

    def attn_terms(h):
        heads = jnp.concatenate(
            [
                lax.dynamic_slice_in_dim(collected[h], (plane - k) % planes * crows, crows, 0)
                for k in order
            ],
            axis=0,
        )
        return sum_begin(product(heads, out_wide, BF16).reshape(planes, mlp_count, sub, dz))

    def attn_end(h, states):
        return lane_input[:, h].astype(F32) + sum_end(states)

    def lane_terms(residual):
        square = residual * residual
        square = sum(square[..., i : i + HD] for i in range(0, dz, HD))
        lane = jnp.concatenate([(residual * gain_lane).astype(BF16), square.astype(BF16)], axis=-1)
        return spread_begin(lane)

    def contract_half(lane):
        part = product(lane.reshape(-1, dz + HD), glu_weight, BF16).reshape(-1, crows, 2 * units + HD)
        return [part[i] for i in range(part.shape[0])]

    def contract(lanes):
        first = contract_half(lanes[0])
        last, first[0] = after(lanes[1], first[0])
        return dict(zip(order, first + contract_half(last)))

    def activate(part, carried):
        act = part[0].astype(F32) + carried[0].astype(F32) + carried[1].astype(F32)
        square = jnp.sum(act[:, 2 * units :], axis=1, keepdims=True)
        act = act * lax.rsqrt(square / width + norm_eps)
        hidden = jax.nn.silu(act[:, :whole]) * act[:, whole : 2 * whole]
        if units > whole:
            last = act[:, 2 * whole : 2 * units]
            edge = units - whole
            hidden = jnp.concatenate(
                [hidden, jax.nn.silu(last[:, :edge]) * last[:, edge:]], axis=1
            )
        return hidden.astype(BF16)

    def deliver(h, down):
        final = (residuals[h] + down).astype(BF16)
        found = {
            k: move(final[i], [(p, (p - k) % planes) for p in range(planes)]) if k else final[i]
            for i, k in enumerate(order)
        }
        return jnp.stack([found[k] for k in range(planes)])

    def down_terms(state):
        slots = gather_slots(state)
        hidden = jnp.concatenate([slots[k] for k in order], axis=0)
        return sum_begin(product(hidden, down_wide, BF16).reshape(planes, mlp_count, sub, dz))

    steps = planes - 1
    states = attn_terms(0)
    for n in range(bits):
        states = sum_stage(states, n)
    residuals = [attn_end(0, states)]
    states = lane_terms(residuals[0])
    for n in range(bits):
        states = spread_stage(states, n)
    lanes = lax.optimization_barrier(spread_end(states))
    first = contract_half(lanes[0])
    carried, last = scatter_step(dict(zip(order, first)), None, 1, lanes[1])
    parts = dict(zip(order, first + contract_half(last)))
    following = None
    if chunks > 1:
        collected[1], parts[0] = after(collected[1], parts[0])
        states = attn_terms(1)
        gots = sum_launch(states, 0)
    for t in range(2, steps + 1):
        if chunks > 1 and t == 2:
            carried, gots = scatter_step(parts, carried, t, gots)
            states = sum_land(states, 0, gots)
            for n in range(1, bits):
                states = sum_stage(states, n)
            residuals.append(attn_end(1, states))
            states = lane_terms(residuals[1])
            gots = spread_launch(states, 0)
        elif chunks > 1 and t == 3:
            carried, gots = scatter_step(parts, carried, t, gots)
            states = spread_land(states, 0, gots)
            for n in range(1, bits):
                states = spread_stage(states, n)
            following = contract(spread_end(states))
        else:
            carried, _ = scatter_step(parts, carried, t)
    finals = []
    if following is not None:
        ahead, carried = scatter_step(following, None, 1, carried)
        hidden = activate(parts, carried)
        state = ([hidden], [hidden])
        gather_step(state, 1)
        gather_step(state, 2)
        for t in range(2, steps + 1):
            ahead, (state[0][-1], state[1][-1]) = scatter_step(
                following, ahead, t, (state[0][-1], state[1][-1])
            )
            if t < steps:
                gather_step(state, t + 1)
        states = down_terms(state)
        gots = sum_launch(states, 0)
        hidden = activate(following, ahead)
        state = ([hidden], [hidden])
        for t in range(1, steps + 1):
            gather_step(state, t)
            if t <= bits:
                (state[0][-1], state[1][-1]), gots = after((state[0][-1], state[1][-1]), gots)
                states = sum_land(states, t - 1, gots)
                if t < bits:
                    gots = sum_launch(states, t)
        for n in range(steps, bits):
            states = sum_stage(states, n)
        finals.append(deliver(0, sum_end(states)))
    else:
        hidden = activate(parts, carried)
        state = ([hidden], [hidden])
        for t in range(1, steps + 1):
            gather_step(state, t)
    states = down_terms(state)
    for n in range(bits):
        states = sum_stage(states, n)
    finals.append(deliver(chunks - 1, sum_end(states)))
    final = swap_halves(jnp.concatenate(finals, axis=1))
    final = lax.dynamic_slice_in_dim(
        jnp.concatenate([final, final], axis=0), (planes - plane) % planes, planes, 0
    )
    layer_output = jnp.swapaxes(final, 0, 1).reshape(share, width)
    return (layer_output, kv_cache)


def solution(mesh):
    placed = (
        P("seq", None),
        P(),
        P(),
        P("seq", "mlp"),
        P("seq", None),
        P("seq", None),
        P("mlp", "seq"),
        P("seq", "mlp"),
        P("seq", "mlp"),
        P("mlp", "seq"),
        P("mlp"),
        P(),
        P(),
        P(),
        P(),
        P(),
    )
    return jax.shard_map(
        shards,
        mesh=mesh,
        in_specs=placed,
        out_specs=(P(("seq", "mlp"), None), P("seq", "mlp")),
        check_vma=False,
    )
```

```python
import math

import jax
import jax.numpy as jnp
from jax import lax
from jax.experimental import pallas as pl
from jax.experimental.pallas import tpu as pltpu
from jax.sharding import PartitionSpec as P

KVH = 8
HD = 128
PIECES_DEV = 2
CORES = 2

rope_base = 1000000.0
norm_eps = 1e-06
far_below = -1e30
start_top = -1e29
F32 = jnp.float32
BF16 = jnp.bfloat16


def rope_tables(position, head_dim):
    half_dim = head_dim // 2
    inverse_freq = jnp.power(
        jnp.float32(rope_base), -2.0 * jnp.arange(half_dim, dtype=jnp.float32) / head_dim
    )
    angles = position.astype(jnp.float32)[:, None] * inverse_freq[None, :]
    cosine, sine = jnp.cos(angles), jnp.sin(angles)
    return (jnp.concatenate([cosine, cosine], axis=1), jnp.concatenate([-sine, sine], axis=1))


def rotate_wide(values, cosine, sine):
    return values * cosine + pltpu.roll(values, HD // 2, 1) * sine


def lookup(small_table, indices):
    matches = indices[:, None] == jnp.arange(small_table.shape[0], dtype=jnp.int32)[None, :]
    return jnp.sum(jnp.where(matches, small_table[None, :], 0), axis=1)


def attend_kernel(
    count, active, piece_stream, own_ref, sib_ref, bias_ref, cos_ref, sin_ref, k_ref, v_ref, lo_ref, hi_ref, o_ref, acc_ref
):
    slot = pl.program_id(1)
    piece_len = k_ref.shape[0] // piece_stream.shape[0]
    rows, wide = own_ref.shape
    per_kv = wide // HD
    scale = 1.0 / math.sqrt(HD)
    cosine, sine = cos_ref[...], sin_ref[...]
    query = own_ref[...] + sib_ref[...] + bias_ref[...]
    q = jnp.concatenate(
        [
            rotate_wide(query[:, i * HD : (i + 1) * HD], cosine, sine).astype(BF16)
            for i in range(per_kv)
        ],
        axis=0,
    )
    lo = lo_ref[0]
    hi = hi_ref[0]
    acc_ref[...] = jnp.zeros_like(acc_ref)

    def step(i, carry):
        top, total = carry
        piece = active[slot, i]
        first = pl.multiple_of(piece * piece_len, piece_len)
        k = k_ref[pl.ds(first, piece_len), :]
        v = v_ref[pl.ds(first, piece_len), :]
        s = lax.dot_general(k, q, (((1,), (1,)), ((), ())), preferred_element_type=F32) * scale
        stream = piece_stream[piece] * piece_len + lax.broadcasted_iota(jnp.int32, s.shape, 0)
        s = jnp.where((stream >= lo) & (stream <= hi), s, far_below)
        new_top = jnp.maximum(top, jnp.max(s, axis=0, keepdims=True))
        w = jnp.exp(s - new_top)
        fade = jnp.exp(top - new_top)
        total = total * fade + jnp.sum(w, axis=0, keepdims=True)
        part = lax.dot_general(v, w.astype(BF16), (((0,), (0,)), ((), ())), preferred_element_type=F32)
        acc_ref[...] = acc_ref[...] * fade + part
        return (new_top, total)

    top = jnp.full((1, q.shape[0]), start_top, F32)
    total = jnp.zeros((1, q.shape[0]), F32)
    top, total = lax.fori_loop(0, count[slot], step, (top, total))
    out = (acc_ref[...] / total).T.astype(BF16)
    for i in range(per_kv):
        o_ref[:, i * HD : (i + 1) * HD] = out[i * rows : (i + 1) * rows]


def attend(query, query_sib, bias, cosine, sine, kv_rows, lo, hi, piece_stream, kv_heads):
    rows, width = query_sib.shape
    slots = PIECES_DEV
    lo, hi = lo.reshape(slots, -1), hi.reshape(slots, -1)
    per_kv = width // (kv_heads * HD)
    keys = kv_rows.shape[0]
    pieces = piece_stream.shape[0]
    piece_len = keys // pieces
    first = piece_stream[None, None, :] * piece_len
    touch = jnp.any(
        (lo[:, :, None] <= first + piece_len - 1) & (hi[:, :, None] >= first), axis=1
    ).astype(jnp.int32)
    place = jnp.cumsum(touch, axis=1) - 1
    ids = jnp.arange(pieces, dtype=jnp.int32)
    active = jnp.sum(
        jnp.where((touch[:, :, None] > 0) & (place[:, :, None] == ids), ids[None, :, None], 0), axis=1
    ).astype(jnp.int32)
    count = jnp.sum(touch, axis=1).astype(jnp.int32)
    lo_wide = jnp.tile(lo, (1, per_kv))[:, None, :]
    hi_wide = jnp.tile(hi, (1, per_kv))[:, None, :]
    tile = (piece_len, per_kv * HD)
    return pl.pallas_call(
        attend_kernel,
        grid_spec=pltpu.PrefetchScalarGridSpec(
            num_scalar_prefetch=3,
            grid=(kv_heads, slots),
            in_specs=[
                pl.BlockSpec(tile, lambda g, h, *_: (h, g)),
                pl.BlockSpec(tile, lambda g, h, *_: (h, g)),
                pl.BlockSpec((1, per_kv * HD), lambda g, h, *_: (0, g)),
                pl.BlockSpec((piece_len, HD), lambda g, h, *_: (h, 0)),
                pl.BlockSpec((piece_len, HD), lambda g, h, *_: (h, 0)),
                pl.BlockSpec((keys, HD), lambda g, h, *_: (0, 2 * g)),
                pl.BlockSpec((keys, HD), lambda g, h, *_: (0, 2 * g + 1)),
                pl.BlockSpec((1, 1, piece_len * per_kv), lambda g, h, *_: (h, 0, 0)),
                pl.BlockSpec((1, 1, piece_len * per_kv), lambda g, h, *_: (h, 0, 0)),
            ],
            out_specs=pl.BlockSpec(tile, lambda g, h, *_: (h, g)),
            scratch_shapes=[pltpu.VMEM((HD, piece_len * per_kv), F32)],
        ),
        out_shape=jax.ShapeDtypeStruct((rows, width), BF16),
        compiler_params=pltpu.CompilerParams(vmem_limit_bytes=32 * 2**20),
    )(count, active, piece_stream, query, query_sib, bias, cosine, sine, kv_rows, kv_rows, lo_wide, hi_wide)


def product_kernel(x_ref, w_ref, o_ref):
    o_ref[...] = jnp.dot(x_ref[...], w_ref[...], preferred_element_type=F32).astype(o_ref.dtype)


def product(x, w, out_type, first=0, cols=None):
    rows, inner = x.shape
    cols = w.shape[1] if cols is None else cols
    tile = next((t for t in (512, 384, 256) if cols % t == 0 and first % t == 0), cols)
    skip = first // tile
    return pl.pallas_call(
        product_kernel,
        grid=(cols // tile,),
        in_specs=[
            pl.BlockSpec((rows, inner), lambda n: (0, 0)),
            pl.BlockSpec((inner, tile), lambda n: (0, n + skip if skip else n)),
        ],
        out_specs=pl.BlockSpec((rows, tile), lambda n: (0, n)),
        out_shape=jax.ShapeDtypeStruct((rows, cols), out_type),
        cost_estimate=pl.CostEstimate(flops=0, transcendentals=0, bytes_accessed=0),
        compiler_params=pltpu.CompilerParams(vmem_limit_bytes=48 * 2**20),
    )(x, w)


def join_kernel(own_ref, sib_ref, bias_ref, cos_ref, sin_ref, o_ref):
    rows, wide = o_ref.shape
    heads = wide // (2 * HD)
    cosine, sine = cos_ref[...], sin_ref[...]
    kv = own_ref[:rows, :] + sib_ref[...] + bias_ref[...]
    for g in range(heads):
        key = rotate_wide(kv[:, g * HD : (g + 1) * HD], cosine, sine)
        o_ref[:, 2 * g * HD : (2 * g + 1) * HD] = key.astype(BF16)
        value = kv[:, (heads + g) * HD : (heads + g + 1) * HD]
        o_ref[:, (2 * g + 1) * HD : (2 * g + 2) * HD] = value.astype(BF16)


def shards(
    layer_input,
    attention_gain,
    feedforward_gain,
    query_weight,
    key_weight,
    value_weight,
    out_weight,
    gate_weight,
    up_weight,
    down_weight,
    query_bias,
    key_bias,
    value_bias,
    doc_lengths,
    piece_order,
    cache_page,
):
    seq_count = lax.axis_size("seq")
    mlp_count = lax.axis_size("mlp")
    seq_rank = lax.axis_index("seq")
    mlp_rank = lax.axis_index("mlp")
    planes = seq_count // CORES
    plane = seq_rank // CORES
    core = seq_rank % CORES
    rows, width = layer_input.shape
    dz = width // planes
    ds = width // seq_count
    share = rows // mlp_count
    chunks = 2 if share % 32 == 0 and planes > 3 else 1
    sub = share // chunks
    crows = mlp_count * sub
    piece_len = rows // PIECES_DEV
    bits = mlp_count.bit_length() - 1

    def move(x, pairs):
        return lax.ppermute(
            x, "seq", [(a * CORES + e, b * CORES + e) for a, b in pairs for e in range(CORES)]
        )

    def sibling(x):
        return lax.ppermute(
            x, "seq", [(a * CORES + e, a * CORES + 1 - e) for a in range(planes) for e in range(CORES)]
        )

    def partner(x, bit):
        return lax.ppermute(x, "mlp", [(a, a ^ bit) for a in range(mlp_count)])

    def after(x, dep):
        return lax.optimization_barrier((x, dep))

    def add(a, b):
        return (a.astype(F32) + b.astype(F32)).astype(BF16)

    def gather_step(state, t):
        ups, downs = state
        ups.append(move(ups[-1], [(i, i + 1) for i in range(t - 1, planes - 1)]))
        downs.append(move(downs[-1], [(i, i - 1) for i in range(1, planes - t + 1)]))

    def gather_slots(state):
        ups, downs = state
        return [ups[0]] + [ups[k] + downs[planes - k] for k in range(1, planes)]

    def scatter_step(parts, carried, t, held=()):
        send_up, send_down = parts[t], parts[planes - t]
        if carried is not None:
            send_up, send_down = add(send_up, carried[0]), add(send_down, carried[1])
        send_up, send_down, held = lax.optimization_barrier((send_up, send_down, held))
        up = move(send_up, [(i, i + 1) for i in range(0, min(t, planes - 1))])
        down = move(send_down, [(i, i - 1) for i in range(max(1, planes - t), planes)])
        return (up, down), held

    half = max(1, planes // 2)
    orders = [list(range(bits)), [(b + bits // 2) % bits for b in range(bits)]]

    def sum_begin(x):
        return [{j: part[:, j] for j in range(mlp_count)} for part in (x[:half], x[half:])]

    def sum_sent(states, n):
        return [[j for j in sorted(v) if j & (1 << o[n])] for v, o in zip(states, orders)]

    def sum_launch(states, n):
        sends = [
            jnp.stack([v[j].astype(BF16) for j in w], axis=0) for v, w in zip(states, sum_sent(states, n))
        ]
        sends = lax.optimization_barrier(sends)
        return [partner(send, 1 << o[n]) for send, o in zip(sends, orders)]

    def sum_land(states, n, gots):
        return [
            {j ^ (1 << o[n]): v[j ^ (1 << o[n])].astype(F32) + got[i].astype(F32) for i, j in enumerate(w)}
            for v, w, o, got in zip(states, sum_sent(states, n), orders, gots)
        ]

    def sum_stage(states, n):
        return sum_land(states, n, sum_launch(states, n))

    def sum_end(states):
        return jnp.concatenate([v[0] for v in states], axis=0)

    def spread_begin(x):
        return [{0: x[:half]}, {0: x[half:]}]

    def spread_launch(states, n):
        sends = [jnp.stack([v[j] for j in sorted(v)], axis=0) for v in states]
        sends = lax.optimization_barrier(sends)
        return [partner(send, 1 << o[bits - 1 - n]) for send, o in zip(sends, orders)]

    def spread_land(states, n, gots):
        return [
            v | {j | (1 << o[bits - 1 - n]): got[i] for i, j in enumerate(sorted(v))}
            for v, o, got in zip(states, orders, gots)
        ]

    def spread_stage(states, n):
        return spread_land(states, n, spread_launch(states, n))

    def spread_end(states):
        return [jnp.stack([v[j] for j in range(mlp_count)], axis=1) for v in states]

    lines = [[z * CORES + e for z in range(planes)] for e in range(CORES)]

    def line_collect(x):
        return lax.all_gather(x, "seq", axis=0, tiled=True, axis_index_groups=lines)

    def swap_halves(x):
        return jnp.where(core == 0, x, jnp.concatenate([x[..., ds:], x[..., :ds]], axis=-1))

    order = []
    for k in range(1, planes // 2 + 1):
        order += [k] if 2 * k == planes else [k, planes - k]
    order.append(0)

    kv_cols = max(HD, KVH * HD // mlp_count)
    kv_first = mlp_rank * KVH // mlp_count * HD
    kv_weight = jnp.concatenate(
        [
            lax.dynamic_slice_in_dim(key_weight, kv_first, kv_cols, 1),
            lax.dynamic_slice_in_dim(value_weight, kv_first, kv_cols, 1),
            query_weight,
        ],
        axis=1,
    )
    kv_bias = jnp.concatenate(
        [
            lax.dynamic_slice_in_dim(key_bias, kv_first, kv_cols, 0),
            lax.dynamic_slice_in_dim(value_bias, kv_first, kv_cols, 0),
        ]
    ).astype(F32)
    kv_weight, (gate_weight, up_weight, out_weight, down_weight, layer_input) = after(
        kv_weight, (gate_weight, up_weight, out_weight, down_weight, layer_input)
    )
    qkv_weight = line_collect(kv_weight)

    x = layer_input.astype(F32)
    mean_sq = jnp.mean(x * x, axis=-1, keepdims=True)
    normed = (x * lax.rsqrt(mean_sq + norm_eps) * attention_gain.astype(F32)).astype(BF16)
    even = jnp.concatenate([normed[:, CORES * z * ds : (CORES * z + 1) * ds] for z in range(planes)], axis=1)
    odd = jnp.concatenate([normed[:, (CORES * z + 1) * ds : CORES * (z + 1) * ds] for z in range(planes)], axis=1)
    mine = jnp.where(core == 0, even, odd)
    theirs = sibling(jnp.where(core == 0, odd, even))
    both = jnp.concatenate([mine, theirs], axis=0)

    units = gate_weight.shape[1]
    whole = units // HD * HD
    glu_own = jnp.concatenate(
        [gate_weight[:, :whole], up_weight[:, :whole], gate_weight[:, whole:], up_weight[:, whole:]],
        axis=1,
    )
    glu_own = lax.optimization_barrier(glu_own)
    glu_weight = jnp.concatenate(
        [
            jnp.pad(jnp.concatenate([glu_own, sibling(glu_own)], axis=0), ((0, 0), (0, HD))),
            jnp.pad(jnp.eye(HD, dtype=BF16), ((0, 0), (2 * units, 0))),
        ],
        axis=0,
    )
    out_wide = jnp.concatenate([out_weight, sibling(out_weight)], axis=1)
    down_wide = jnp.concatenate([down_weight, sibling(down_weight)], axis=1)

    own_share = lax.dynamic_slice_in_dim(layer_input, mlp_rank * share, share, 0)
    lane_sends = [lax.dynamic_slice_in_dim(own_share, (plane + k) % planes * dz, dz, 1) for k in order]
    gain_lane = swap_halves(lax.dynamic_slice_in_dim(feedforward_gain, plane * dz, dz, 0)).astype(F32)
    both, glu_weight, out_wide, down_wide, lane_sends = lax.optimization_barrier(
        (both, glu_weight, out_wide, down_wide, lane_sends)
    )

    row_ids = seq_rank * rows + jnp.arange(rows, dtype=jnp.int32)
    stream = lookup(piece_order, row_ids // piece_len) * piece_len + row_ids % piece_len
    doc_ends = jnp.cumsum(doc_lengths)
    segment = jnp.sum((stream[:, None] >= doc_ends[None, :]).astype(jnp.int32), axis=1)
    doc_first = lookup(doc_ends - doc_lengths, segment)
    cosine, sine = rope_tables(stream - doc_first, HD)

    kv_heads = kv_cols // HD
    lane_sends, qkv_weight = after(lane_sends, qkv_weight)
    lane_parts = [
        move(v, [(i, (i + k) % planes) for i in range(planes)]) if k else v
        for k, v in zip(order, lane_sends)
    ]
    kv = product(both, qkv_weight, F32, 0, 2 * kv_cols)
    joined = pl.pallas_call(
        join_kernel, out_shape=jax.ShapeDtypeStruct((rows, 2 * kv_cols), BF16)
    )(kv, sibling(kv[rows:]), kv_bias[None, :], cosine, sine)
    state = ([joined], [joined])
    for t in range(1, planes):
        if t == planes - 1:
            (state[0][-1], state[1][-1]), lane_parts = after((state[0][-1], state[1][-1]), lane_parts)
        gather_step(state, t)
    core_rows = jnp.concatenate(gather_slots(state), axis=0)
    kv_rows = jnp.concatenate([core_rows, sibling(core_rows)], axis=0)
    offsets = (plane - jnp.arange(planes, dtype=jnp.int32)) % planes
    slots = jnp.concatenate([offsets * CORES + core, offsets * CORES + 1 - core])
    slots = (slots[:, None] * PIECES_DEV + jnp.arange(PIECES_DEV, dtype=jnp.int32)).reshape(-1)
    piece_stream = lookup(piece_order, slots)

    own_cols = KVH * HD // mlp_count
    cache_width = 2 * own_cols
    offset = mlp_rank % max(1, HD // own_cols) * cache_width
    pieces = jnp.arange(piece_order.shape[0], dtype=jnp.int32)
    pages = []
    for p in range(PIECES_DEV):
        stream_piece = jnp.sum(jnp.where(cache_page == seq_rank * PIECES_DEV + p, pieces, 0))
        source = jnp.sum(jnp.where(piece_stream == stream_piece, pieces, 0))
        pages.append(lax.dynamic_slice(kv_rows, (source * piece_len, offset), (piece_len, cache_width)))
    kv_cache = jnp.concatenate(pages, axis=0)

    query = product(both, qkv_weight, F32, 2 * kv_cols, query_weight.shape[1])
    query_sib = sibling(query[rows:])
    lane_input = swap_halves(jnp.stack(lane_parts, axis=0)).reshape(planes, chunks, sub, dz)
    mixed = attend(
        query, query_sib, query_bias.astype(F32)[None, :], cosine, sine, kv_rows, doc_first, stream, piece_stream, kv_heads
    )
    chunked = [
        jnp.concatenate(
            [
                lax.dynamic_slice_in_dim(mixed, (mlp_rank ^ j) * share + h * sub, sub, 0)
                for j in range(mlp_count)
            ],
            axis=0,
        )
        for h in range(chunks)
    ]

    collected = [line_collect(v) for v in chunked]

    def attn_terms(h):
        heads = jnp.concatenate(
            [
                lax.dynamic_slice_in_dim(collected[h], (plane - k) % planes * crows, crows, 0)
                for k in order
            ],
            axis=0,
        )
        return sum_begin(product(heads, out_wide, BF16).reshape(planes, mlp_count, sub, dz))

    def attn_end(h, states):
        return lane_input[:, h].astype(F32) + sum_end(states)

    def lane_terms(residual):
        square = residual * residual
        square = sum(square[..., i : i + HD] for i in range(0, dz, HD))
        lane = jnp.concatenate([(residual * gain_lane).astype(BF16), square.astype(BF16)], axis=-1)
        return spread_begin(lane)

    def contract_half(lane):
        part = product(lane.reshape(-1, dz + HD), glu_weight, BF16).reshape(-1, crows, 2 * units + HD)
        return [part[i] for i in range(part.shape[0])]

    def contract(lanes):
        first = contract_half(lanes[0])
        last, first[0] = after(lanes[1], first[0])
        return dict(zip(order, first + contract_half(last)))

    def activate(part, carried):
        act = part[0].astype(F32) + carried[0].astype(F32) + carried[1].astype(F32)
        square = jnp.sum(act[:, 2 * units :], axis=1, keepdims=True)
        act = act * lax.rsqrt(square / width + norm_eps)
        hidden = jax.nn.silu(act[:, :whole]) * act[:, whole : 2 * whole]
        if units > whole:
            last = act[:, 2 * whole : 2 * units]
            edge = units - whole
            hidden = jnp.concatenate(
                [hidden, jax.nn.silu(last[:, :edge]) * last[:, edge:]], axis=1
            )
        return hidden.astype(BF16)

    def deliver(h, down):
        final = (residuals[h] + down).astype(BF16)
        found = {
            k: move(final[i], [(p, (p - k) % planes) for p in range(planes)]) if k else final[i]
            for i, k in enumerate(order)
        }
        return jnp.stack([found[k] for k in range(planes)])

    def down_terms(state):
        slots = gather_slots(state)
        hidden = jnp.concatenate([slots[k] for k in order], axis=0)
        return sum_begin(product(hidden, down_wide, BF16).reshape(planes, mlp_count, sub, dz))

    steps = planes - 1
    states = attn_terms(0)
    for n in range(bits):
        states = sum_stage(states, n)
    residuals = [attn_end(0, states)]
    states = lane_terms(residuals[0])
    for n in range(bits):
        states = spread_stage(states, n)
    lanes = lax.optimization_barrier(spread_end(states))
    first = contract_half(lanes[0])
    carried, last = scatter_step(dict(zip(order, first)), None, 1, lanes[1])
    parts = dict(zip(order, first + contract_half(last)))
    following = None
    if chunks > 1:
        collected[1], parts[0] = after(collected[1], parts[0])
        states = attn_terms(1)
        gots = sum_launch(states, 0)
    for t in range(2, steps + 1):
        if chunks > 1 and t == 2:
            carried, gots = scatter_step(parts, carried, t, gots)
            states = sum_land(states, 0, gots)
            for n in range(1, bits):
                states = sum_stage(states, n)
            residuals.append(attn_end(1, states))
            states = lane_terms(residuals[1])
            gots = spread_launch(states, 0)
        elif chunks > 1 and t == 3:
            carried, gots = scatter_step(parts, carried, t, gots)
            states = spread_land(states, 0, gots)
            for n in range(1, bits):
                states = spread_stage(states, n)
            following = contract(spread_end(states))
        else:
            carried, _ = scatter_step(parts, carried, t)
    finals = []
    if following is not None:
        ahead, carried = scatter_step(following, None, 1, carried)
        hidden = activate(parts, carried)
        state = ([hidden], [hidden])
        gather_step(state, 1)
        gather_step(state, 2)
        for t in range(2, steps + 1):
            ahead, (state[0][-1], state[1][-1]) = scatter_step(
                following, ahead, t, (state[0][-1], state[1][-1])
            )
            if t < steps:
                gather_step(state, t + 1)
        states = down_terms(state)
        gots = sum_launch(states, 0)
        hidden = activate(following, ahead)
        state = ([hidden], [hidden])
        for t in range(1, steps + 1):
            gather_step(state, t)
            if t <= bits:
                (state[0][-1], state[1][-1]), gots = after((state[0][-1], state[1][-1]), gots)
                states = sum_land(states, t - 1, gots)
                if t < bits:
                    gots = sum_launch(states, t)
        for n in range(steps, bits):
            states = sum_stage(states, n)
        finals.append(deliver(0, sum_end(states)))
    else:
        hidden = activate(parts, carried)
        state = ([hidden], [hidden])
        for t in range(1, steps + 1):
            gather_step(state, t)
    states = down_terms(state)
    for n in range(bits):
        states = sum_stage(states, n)
    finals.append(deliver(chunks - 1, sum_end(states)))
    final = swap_halves(jnp.concatenate(finals, axis=1))
    final = lax.dynamic_slice_in_dim(
        jnp.concatenate([final, final], axis=0), (planes - plane) % planes, planes, 0
    )
    layer_output = jnp.swapaxes(final, 0, 1).reshape(share, width)
    return (layer_output, kv_cache)


def solution(mesh):
    placed = (
        P("seq", None),
        P(),
        P(),
        P("seq", "mlp"),
        P("seq", None),
        P("seq", None),
        P("mlp", "seq"),
        P("seq", "mlp"),
        P("seq", "mlp"),
        P("mlp", "seq"),
        P("mlp"),
        P(),
        P(),
        P(),
        P(),
        P(),
    )
    return jax.shard_map(
        shards,
        mesh=mesh,
        in_specs=placed,
        out_specs=(P(("seq", "mlp"), None), P("seq", "mlp")),
        check_vma=False,
    )
```

```python
import math

import jax
import jax.numpy as jnp
from jax import lax
from jax.experimental import pallas as pl
from jax.experimental.pallas import tpu as pltpu
from jax.sharding import PartitionSpec as P

KVH = 8
HD = 128
PIECES_DEV = 2
CORES = 2

rope_base = 1000000.0
norm_eps = 1e-06
far_below = -1e30
start_top = -1e29
F32 = jnp.float32
BF16 = jnp.bfloat16


def rope_tables(position, head_dim):
    half_dim = head_dim // 2
    inverse_freq = jnp.power(
        jnp.float32(rope_base), -2.0 * jnp.arange(half_dim, dtype=jnp.float32) / head_dim
    )
    angles = position.astype(jnp.float32)[:, None] * inverse_freq[None, :]
    cosine, sine = jnp.cos(angles), jnp.sin(angles)
    return (jnp.concatenate([cosine, cosine], axis=1), jnp.concatenate([-sine, sine], axis=1))


def rotate_wide(values, cosine, sine):
    return values * cosine + pltpu.roll(values, HD // 2, 1) * sine


def lookup(small_table, indices):
    matches = indices[:, None] == jnp.arange(small_table.shape[0], dtype=jnp.int32)[None, :]
    return jnp.sum(jnp.where(matches, small_table[None, :], 0), axis=1)


def attend_kernel(
    count, active, piece_stream, own_ref, sib_ref, bias_ref, cos_ref, sin_ref, k_ref, v_ref, lo_ref, hi_ref, o_ref, acc_ref
):
    slot = pl.program_id(1)
    piece_len = k_ref.shape[0] // piece_stream.shape[0]
    rows, wide = own_ref.shape
    per_kv = wide // HD
    scale = 1.0 / math.sqrt(HD)
    cosine, sine = cos_ref[...], sin_ref[...]
    query = own_ref[...] + sib_ref[...] + bias_ref[...]
    q = jnp.concatenate(
        [
            rotate_wide(query[:, i * HD : (i + 1) * HD], cosine, sine).astype(BF16)
            for i in range(per_kv)
        ],
        axis=0,
    )
    lo = lo_ref[0]
    hi = hi_ref[0]
    acc_ref[...] = jnp.zeros_like(acc_ref)

    def step(i, carry):
        top, total = carry
        piece = active[slot, i]
        first = pl.multiple_of(piece * piece_len, piece_len)
        k = k_ref[pl.ds(first, piece_len), :]
        v = v_ref[pl.ds(first, piece_len), :]
        s = lax.dot_general(k, q, (((1,), (1,)), ((), ())), preferred_element_type=F32) * scale
        stream = piece_stream[piece] * piece_len + lax.broadcasted_iota(jnp.int32, s.shape, 0)
        s = jnp.where((stream >= lo) & (stream <= hi), s, far_below)
        new_top = jnp.maximum(top, jnp.max(s, axis=0, keepdims=True))
        w = jnp.exp(s - new_top)
        fade = jnp.exp(top - new_top)
        total = total * fade + jnp.sum(w, axis=0, keepdims=True)
        part = lax.dot_general(v, w.astype(BF16), (((0,), (0,)), ((), ())), preferred_element_type=F32)
        acc_ref[...] = acc_ref[...] * fade + part
        return (new_top, total)

    top = jnp.full((1, q.shape[0]), start_top, F32)
    total = jnp.zeros((1, q.shape[0]), F32)
    top, total = lax.fori_loop(0, count[slot], step, (top, total))
    out = (acc_ref[...] / total).T.astype(BF16)
    for i in range(per_kv):
        o_ref[:, i * HD : (i + 1) * HD] = out[i * rows : (i + 1) * rows]


def attend(query, query_sib, bias, cosine, sine, kv_rows, lo, hi, piece_stream, kv_heads):
    rows, width = query_sib.shape
    slots = PIECES_DEV
    lo, hi = lo.reshape(slots, -1), hi.reshape(slots, -1)
    per_kv = width // (kv_heads * HD)
    keys = kv_rows.shape[0]
    pieces = piece_stream.shape[0]
    piece_len = keys // pieces
    first = piece_stream[None, None, :] * piece_len
    touch = jnp.any(
        (lo[:, :, None] <= first + piece_len - 1) & (hi[:, :, None] >= first), axis=1
    ).astype(jnp.int32)
    place = jnp.cumsum(touch, axis=1) - 1
    ids = jnp.arange(pieces, dtype=jnp.int32)
    active = jnp.sum(
        jnp.where((touch[:, :, None] > 0) & (place[:, :, None] == ids), ids[None, :, None], 0), axis=1
    ).astype(jnp.int32)
    count = jnp.sum(touch, axis=1).astype(jnp.int32)
    lo_wide = jnp.tile(lo, (1, per_kv))[:, None, :]
    hi_wide = jnp.tile(hi, (1, per_kv))[:, None, :]
    tile = (piece_len, per_kv * HD)
    return pl.pallas_call(
        attend_kernel,
        grid_spec=pltpu.PrefetchScalarGridSpec(
            num_scalar_prefetch=3,
            grid=(kv_heads, slots),
            in_specs=[
                pl.BlockSpec(tile, lambda g, h, *_: (h, g)),
                pl.BlockSpec(tile, lambda g, h, *_: (h, g)),
                pl.BlockSpec((1, per_kv * HD), lambda g, h, *_: (0, g)),
                pl.BlockSpec((piece_len, HD), lambda g, h, *_: (h, 0)),
                pl.BlockSpec((piece_len, HD), lambda g, h, *_: (h, 0)),
                pl.BlockSpec((keys, HD), lambda g, h, *_: (0, 2 * g)),
                pl.BlockSpec((keys, HD), lambda g, h, *_: (0, 2 * g + 1)),
                pl.BlockSpec((1, 1, piece_len * per_kv), lambda g, h, *_: (h, 0, 0)),
                pl.BlockSpec((1, 1, piece_len * per_kv), lambda g, h, *_: (h, 0, 0)),
            ],
            out_specs=pl.BlockSpec(tile, lambda g, h, *_: (h, g)),
            scratch_shapes=[pltpu.VMEM((HD, piece_len * per_kv), F32)],
        ),
        out_shape=jax.ShapeDtypeStruct((rows, width), BF16),
        compiler_params=pltpu.CompilerParams(vmem_limit_bytes=32 * 2**20),
    )(count, active, piece_stream, query, query_sib, bias, cosine, sine, kv_rows, kv_rows, lo_wide, hi_wide)


def product_kernel(x_ref, w_ref, o_ref):
    o_ref[...] = jnp.dot(x_ref[...], w_ref[...], preferred_element_type=F32).astype(o_ref.dtype)


def product(x, w, out_type):
    rows, inner = x.shape
    cols = w.shape[1]
    tile = next((t for t in (512, 384, 256) if cols % t == 0), cols)
    return pl.pallas_call(
        product_kernel,
        grid=(cols // tile,),
        in_specs=[
            pl.BlockSpec((rows, inner), lambda n: (0, 0)),
            pl.BlockSpec((inner, tile), lambda n: (0, n)),
        ],
        out_specs=pl.BlockSpec((rows, tile), lambda n: (0, n)),
        out_shape=jax.ShapeDtypeStruct((rows, cols), out_type),
        cost_estimate=pl.CostEstimate(flops=0, transcendentals=0, bytes_accessed=0),
        compiler_params=pltpu.CompilerParams(vmem_limit_bytes=48 * 2**20),
    )(x, w)


def join_kernel(own_ref, sib_ref, bias_ref, cos_ref, sin_ref, o_ref):
    rows, wide = o_ref.shape
    heads = wide // (2 * HD)
    cosine, sine = cos_ref[...], sin_ref[...]
    kv = own_ref[:rows, :] + sib_ref[...] + bias_ref[...]
    for g in range(heads):
        key = rotate_wide(kv[:, g * HD : (g + 1) * HD], cosine, sine)
        o_ref[:, 2 * g * HD : (2 * g + 1) * HD] = key.astype(BF16)
        value = kv[:, (heads + g) * HD : (heads + g + 1) * HD]
        o_ref[:, (2 * g + 1) * HD : (2 * g + 2) * HD] = value.astype(BF16)


def shards(
    layer_input,
    attention_gain,
    feedforward_gain,
    query_weight,
    key_weight,
    value_weight,
    out_weight,
    gate_weight,
    up_weight,
    down_weight,
    query_bias,
    key_bias,
    value_bias,
    doc_lengths,
    piece_order,
    cache_page,
):
    seq_count = lax.axis_size("seq")
    mlp_count = lax.axis_size("mlp")
    seq_rank = lax.axis_index("seq")
    mlp_rank = lax.axis_index("mlp")
    planes = seq_count // CORES
    plane = seq_rank // CORES
    core = seq_rank % CORES
    rows, width = layer_input.shape
    dz = width // planes
    ds = width // seq_count
    share = rows // mlp_count
    chunks = 2 if share % 32 == 0 and planes > 3 else 1
    sub = share // chunks
    crows = mlp_count * sub
    piece_len = rows // PIECES_DEV
    bits = mlp_count.bit_length() - 1

    def move(x, pairs):
        return lax.ppermute(
            x, "seq", [(a * CORES + e, b * CORES + e) for a, b in pairs for e in range(CORES)]
        )

    def sibling(x):
        return lax.ppermute(
            x, "seq", [(a * CORES + e, a * CORES + 1 - e) for a in range(planes) for e in range(CORES)]
        )

    def partner(x, bit):
        return lax.ppermute(x, "mlp", [(a, a ^ bit) for a in range(mlp_count)])

    def after(x, dep):
        return lax.optimization_barrier((x, dep))

    def add(a, b):
        return (a.astype(F32) + b.astype(F32)).astype(BF16)

    def gather_step(state, t):
        ups, downs = state
        ups.append(move(ups[-1], [(i, i + 1) for i in range(t - 1, planes - 1)]))
        downs.append(move(downs[-1], [(i, i - 1) for i in range(1, planes - t + 1)]))

    def gather_slots(state):
        ups, downs = state
        return [ups[0]] + [ups[k] + downs[planes - k] for k in range(1, planes)]

    def line_gather(x):
        state = ([x], [x])
        for t in range(1, planes):
            gather_step(state, t)
        return gather_slots(state)

    def scatter_step(parts, carried, t, held=()):
        send_up, send_down = parts[t], parts[planes - t]
        if carried is not None:
            send_up, send_down = add(send_up, carried[0]), add(send_down, carried[1])
        send_up, send_down, held = lax.optimization_barrier((send_up, send_down, held))
        up = move(send_up, [(i, i + 1) for i in range(0, min(t, planes - 1))])
        down = move(send_down, [(i, i - 1) for i in range(max(1, planes - t), planes)])
        return (up, down), held

    half = max(1, planes // 2)
    orders = [list(range(bits)), [(b + bits // 2) % bits for b in range(bits)]]

    def sum_begin(x):
        return [{j: part[:, j] for j in range(mlp_count)} for part in (x[:half], x[half:])]

    def sum_sent(states, n):
        return [[j for j in sorted(v) if j & (1 << o[n])] for v, o in zip(states, orders)]

    def sum_launch(states, n):
        sends = [
            jnp.stack([v[j].astype(BF16) for j in w], axis=0) for v, w in zip(states, sum_sent(states, n))
        ]
        sends = lax.optimization_barrier(sends)
        return [partner(send, 1 << o[n]) for send, o in zip(sends, orders)]

    def sum_land(states, n, gots):
        return [
            {j ^ (1 << o[n]): v[j ^ (1 << o[n])].astype(F32) + got[i].astype(F32) for i, j in enumerate(w)}
            for v, w, o, got in zip(states, sum_sent(states, n), orders, gots)
        ]

    def sum_stage(states, n):
        return sum_land(states, n, sum_launch(states, n))

    def sum_end(states):
        return jnp.concatenate([v[0] for v in states], axis=0)

    def spread_begin(x):
        return [{0: x[:half]}, {0: x[half:]}]

    def spread_launch(states, n):
        sends = [jnp.stack([v[j] for j in sorted(v)], axis=0) for v in states]
        sends = lax.optimization_barrier(sends)
        return [partner(send, 1 << o[bits - 1 - n]) for send, o in zip(sends, orders)]

    def spread_land(states, n, gots):
        return [
            v | {j | (1 << o[bits - 1 - n]): got[i] for i, j in enumerate(sorted(v))}
            for v, o, got in zip(states, orders, gots)
        ]

    def spread_stage(states, n):
        return spread_land(states, n, spread_launch(states, n))

    def spread_end(states):
        return [jnp.stack([v[j] for j in range(mlp_count)], axis=1) for v in states]

    lines = [[z * CORES + e for z in range(planes)] for e in range(CORES)]

    def line_collect(x):
        return lax.all_gather(x, "seq", axis=0, tiled=True, axis_index_groups=lines)

    def swap_halves(x):
        return jnp.where(core == 0, x, jnp.concatenate([x[..., ds:], x[..., :ds]], axis=-1))

    order = []
    for k in range(1, planes // 2 + 1):
        order += [k] if 2 * k == planes else [k, planes - k]
    order.append(0)

    kv_cols = max(HD, KVH * HD // mlp_count)
    kv_first = mlp_rank * KVH // mlp_count * HD
    kv_weight = jnp.concatenate(
        [
            lax.dynamic_slice_in_dim(key_weight, kv_first, kv_cols, 1),
            lax.dynamic_slice_in_dim(value_weight, kv_first, kv_cols, 1),
        ],
        axis=1,
    )
    kv_bias = jnp.concatenate(
        [
            lax.dynamic_slice_in_dim(key_bias, kv_first, kv_cols, 0),
            lax.dynamic_slice_in_dim(value_bias, kv_first, kv_cols, 0),
        ]
    ).astype(F32)
    q_weight = line_collect(query_weight)
    kv_state = ([kv_weight], [kv_weight])
    gather_step(kv_state, 1)
    if planes > 3:
        ends, (gate_weight, up_weight) = after(
            (kv_state[0][-1], kv_state[1][-1]), (gate_weight, up_weight)
        )
        kv_state[0][-1], kv_state[1][-1] = ends
    for t in range(2, planes):
        gather_step(kv_state, t)
        if t == 2 and planes > 3:
            ends, (out_weight, down_weight) = after(
                (kv_state[0][-1], kv_state[1][-1]), (out_weight, down_weight)
            )
            kv_state[0][-1], kv_state[1][-1] = ends
    kv_slots = jnp.stack(gather_slots(kv_state), axis=0)
    kv_weight = jnp.concatenate(
        [lax.dynamic_index_in_dim(kv_slots, (plane - z) % planes, 0, False) for z in range(planes)], axis=0
    )

    x = layer_input.astype(F32)
    mean_sq = jnp.mean(x * x, axis=-1, keepdims=True)
    normed = (x * lax.rsqrt(mean_sq + norm_eps) * attention_gain.astype(F32)).astype(BF16)
    even = jnp.concatenate([normed[:, CORES * z * ds : (CORES * z + 1) * ds] for z in range(planes)], axis=1)
    odd = jnp.concatenate([normed[:, (CORES * z + 1) * ds : CORES * (z + 1) * ds] for z in range(planes)], axis=1)
    mine = jnp.where(core == 0, even, odd)
    theirs = sibling(jnp.where(core == 0, odd, even))
    both = jnp.concatenate([mine, theirs], axis=0)

    units = gate_weight.shape[1]
    whole = units // HD * HD
    glu_own = jnp.concatenate(
        [gate_weight[:, :whole], up_weight[:, :whole], gate_weight[:, whole:], up_weight[:, whole:]],
        axis=1,
    )
    glu_own = lax.optimization_barrier(glu_own)
    glu_weight = jnp.concatenate(
        [
            jnp.pad(jnp.concatenate([glu_own, sibling(glu_own)], axis=0), ((0, 0), (0, HD))),
            jnp.pad(jnp.eye(HD, dtype=BF16), ((0, 0), (2 * units, 0))),
        ],
        axis=0,
    )
    out_wide = jnp.concatenate([out_weight, sibling(out_weight)], axis=1)
    down_wide = jnp.concatenate([down_weight, sibling(down_weight)], axis=1)

    own_share = lax.dynamic_slice_in_dim(layer_input, mlp_rank * share, share, 0)
    lane_sends = [lax.dynamic_slice_in_dim(own_share, (plane + k) % planes * dz, dz, 1) for k in order]
    gain_lane = swap_halves(lax.dynamic_slice_in_dim(feedforward_gain, plane * dz, dz, 0)).astype(F32)
    both, glu_weight, out_wide, down_wide, lane_sends = lax.optimization_barrier(
        (both, glu_weight, out_wide, down_wide, lane_sends)
    )

    row_ids = seq_rank * rows + jnp.arange(rows, dtype=jnp.int32)
    stream = lookup(piece_order, row_ids // piece_len) * piece_len + row_ids % piece_len
    doc_ends = jnp.cumsum(doc_lengths)
    segment = jnp.sum((stream[:, None] >= doc_ends[None, :]).astype(jnp.int32), axis=1)
    doc_first = lookup(doc_ends - doc_lengths, segment)
    cosine, sine = rope_tables(stream - doc_first, HD)

    kv_heads = kv_cols // HD
    kv = product(both, kv_weight, F32)
    joined = pl.pallas_call(
        join_kernel, out_shape=jax.ShapeDtypeStruct((rows, 2 * kv_cols), BF16)
    )(kv, sibling(kv[rows:]), kv_bias[None, :], cosine, sine)
    core_rows = jnp.concatenate(line_gather(joined), axis=0)
    kv_rows = jnp.concatenate([core_rows, sibling(core_rows)], axis=0)
    offsets = (plane - jnp.arange(planes, dtype=jnp.int32)) % planes
    slots = jnp.concatenate([offsets * CORES + core, offsets * CORES + 1 - core])
    slots = (slots[:, None] * PIECES_DEV + jnp.arange(PIECES_DEV, dtype=jnp.int32)).reshape(-1)
    piece_stream = lookup(piece_order, slots)

    own_cols = KVH * HD // mlp_count
    cache_width = 2 * own_cols
    offset = mlp_rank % max(1, HD // own_cols) * cache_width
    pieces = jnp.arange(piece_order.shape[0], dtype=jnp.int32)
    pages = []
    for p in range(PIECES_DEV):
        stream_piece = jnp.sum(jnp.where(cache_page == seq_rank * PIECES_DEV + p, pieces, 0))
        source = jnp.sum(jnp.where(piece_stream == stream_piece, pieces, 0))
        pages.append(lax.dynamic_slice(kv_rows, (source * piece_len, offset), (piece_len, cache_width)))
    kv_cache = jnp.concatenate(pages, axis=0)

    lane_sends, q_weight = after(lane_sends, q_weight)
    lane_parts = [
        move(v, [(i, (i + k) % planes) for i in range(planes)]) if k else v
        for k, v in zip(order, lane_sends)
    ]
    query = product(both, q_weight, F32)
    query_sib, lane_parts = after(sibling(query[rows:]), lane_parts)
    lane_input = swap_halves(jnp.stack(lane_parts, axis=0)).reshape(planes, chunks, sub, dz)
    mixed = attend(
        query, query_sib, query_bias.astype(F32)[None, :], cosine, sine, kv_rows, doc_first, stream, piece_stream, kv_heads
    )
    chunked = [
        jnp.concatenate(
            [
                lax.dynamic_slice_in_dim(mixed, ((mlp_rank ^ j) if h == 0 else j) * share + h * sub, sub, 0)
                for j in range(mlp_count)
            ],
            axis=0,
        )
        for h in range(chunks)
    ]

    collected = [line_collect(v) for v in chunked]

    def heads_of(h):
        return jnp.concatenate(
            [
                lax.dynamic_slice_in_dim(collected[h], (plane - k) % planes * crows, crows, 0)
                for k in order
            ],
            axis=0,
        )

    def attn_terms(h):
        return sum_begin(product(heads_of(h), out_wide, BF16).reshape(planes, mlp_count, sub, dz))

    def share_first(x):
        return jnp.swapaxes(x.reshape(planes, mlp_count, sub, -1), 0, 1).reshape(x.shape)

    def attn_end(h, summed):
        return lane_input[:, h].astype(F32) + summed

    def lane_of(residual):
        square = residual * residual
        square = sum(square[..., i : i + HD] for i in range(0, dz, HD))
        return jnp.concatenate([(residual * gain_lane).astype(BF16), square.astype(BF16)], axis=-1)

    def contract_half(lane):
        part = product(lane.reshape(-1, dz + HD), glu_weight, BF16).reshape(-1, crows, 2 * units + HD)
        return [part[i] for i in range(part.shape[0])]

    def contract(lanes):
        first = contract_half(lanes[0])
        last, first[0] = after(lanes[1], first[0])
        return dict(zip(order, first + contract_half(last)))

    def activate(part, carried):
        act = part[0].astype(F32) + carried[0].astype(F32) + carried[1].astype(F32)
        square = jnp.sum(act[:, 2 * units :], axis=1, keepdims=True)
        act = act * lax.rsqrt(square / width + norm_eps)
        hidden = jax.nn.silu(act[:, :whole]) * act[:, whole : 2 * whole]
        if units > whole:
            last = act[:, 2 * whole : 2 * units]
            edge = units - whole
            hidden = jnp.concatenate(
                [hidden, jax.nn.silu(last[:, :edge]) * last[:, edge:]], axis=1
            )
        return hidden.astype(BF16)

    def deliver(h, down):
        final = (residuals[h] + down).astype(BF16)
        found = {
            k: move(final[i], [(p, (p - k) % planes) for p in range(planes)]) if k else final[i]
            for i, k in enumerate(order)
        }
        return jnp.stack([found[k] for k in range(planes)])

    def down_terms(state):
        slots = gather_slots(state)
        hidden = jnp.concatenate([slots[k] for k in order], axis=0)
        return sum_begin(product(hidden, down_wide, BF16).reshape(planes, mlp_count, sub, dz))

    steps = planes - 1
    states = attn_terms(0)
    for n in range(bits):
        states = sum_stage(states, n)
    residuals = [attn_end(0, sum_end(states))]
    states = spread_begin(lane_of(residuals[0]))
    for n in range(bits):
        states = spread_stage(states, n)
    lanes = lax.optimization_barrier(spread_end(states))
    first = contract_half(lanes[0])
    carried, last = scatter_step(dict(zip(order, first)), None, 1, lanes[1])
    parts = dict(zip(order, first + contract_half(last)))
    following = None
    if chunks > 1:
        collected[1], parts[0] = after(collected[1], parts[0])
        terms = product(share_first(heads_of(1)), out_wide, BF16)
        _, carried = after(terms, carried)
        terms = lax.psum_scatter(terms, "mlp", scatter_dimension=0, tiled=True)
    for t in range(2, steps + 1):
        carried, _ = scatter_step(parts, carried, t)
        if chunks > 1 and t == 2:
            terms, _ = after(terms, carried)
            residuals.append(attn_end(1, terms.astype(F32).reshape(planes, sub, dz)))
            lane = lane_of(residuals[1]).reshape(planes * sub, dz + HD)
            lane = lax.all_gather(lane, "mlp", axis=0, tiled=True)
            lane = lane.reshape(mlp_count, planes, sub, dz + HD)
    if chunks > 1:
        following = contract([jnp.swapaxes(v, 0, 1) for v in (lane[:, :half], lane[:, half:])])
    finals = []
    if following is not None:
        ahead, carried = scatter_step(following, None, 1, carried)
        hidden = activate(parts, carried)
        state = ([hidden], [hidden])
        gather_step(state, 1)
        gather_step(state, 2)
        for t in range(2, steps + 1):
            ahead, (state[0][-1], state[1][-1]) = scatter_step(
                following, ahead, t, (state[0][-1], state[1][-1])
            )
            if t < steps:
                gather_step(state, t + 1)
        states = down_terms(state)
        gots = sum_launch(states, 0)
        hidden = activate(following, ahead)
        hidden = jnp.concatenate(
            [
                lax.dynamic_slice_in_dim(hidden, (mlp_rank ^ j) * sub, sub, 0)
                for j in range(mlp_count)
            ],
            axis=0,
        )
        state = ([hidden], [hidden])
        for t in range(1, steps + 1):
            gather_step(state, t)
            if t <= bits:
                (state[0][-1], state[1][-1]), gots = after((state[0][-1], state[1][-1]), gots)
                states = sum_land(states, t - 1, gots)
                if t < bits:
                    gots = sum_launch(states, t)
        for n in range(steps, bits):
            states = sum_stage(states, n)
        finals.append(deliver(0, sum_end(states)))
    else:
        hidden = activate(parts, carried)
        state = ([hidden], [hidden])
        for t in range(1, steps + 1):
            gather_step(state, t)
    states = down_terms(state)
    for n in range(bits):
        states = sum_stage(states, n)
    finals.append(deliver(chunks - 1, sum_end(states)))
    final = swap_halves(jnp.concatenate(finals, axis=1))
    final = lax.dynamic_slice_in_dim(
        jnp.concatenate([final, final], axis=0), (planes - plane) % planes, planes, 0
    )
    layer_output = jnp.swapaxes(final, 0, 1).reshape(share, width)
    return (layer_output, kv_cache)


def solution(mesh):
    placed = (
        P("seq", None),
        P(),
        P(),
        P("seq", "mlp"),
        P("seq", None),
        P("seq", None),
        P("mlp", "seq"),
        P("seq", "mlp"),
        P("seq", "mlp"),
        P("mlp", "seq"),
        P("mlp"),
        P(),
        P(),
        P(),
        P(),
        P(),
    )
    return jax.shard_map(
        shards,
        mesh=mesh,
        in_specs=placed,
        out_specs=(P(("seq", "mlp"), None), P("seq", "mlp")),
        check_vma=False,
    )
```

```python
import math

import jax
import jax.numpy as jnp
from jax import lax
from jax.experimental import pallas as pl
from jax.experimental.pallas import tpu as pltpu
from jax.sharding import PartitionSpec as P

KVH = 8
HD = 128
PIECES_DEV = 2
CORES = 2
CHUNKS = 3

rope_base = 1000000.0
norm_eps = 1e-06
far_below = -1e30
start_top = -1e29
F32 = jnp.float32
BF16 = jnp.bfloat16


def rope_tables(position, head_dim):
    half_dim = head_dim // 2
    inverse_freq = jnp.power(
        jnp.float32(rope_base), -2.0 * jnp.arange(half_dim, dtype=jnp.float32) / head_dim
    )
    angles = position.astype(jnp.float32)[:, None] * inverse_freq[None, :]
    cosine, sine = jnp.cos(angles), jnp.sin(angles)
    return (jnp.concatenate([cosine, cosine], axis=1), jnp.concatenate([-sine, sine], axis=1))


def rotate_wide(values, cosine, sine):
    return values * cosine + pltpu.roll(values, HD // 2, 1) * sine


def lookup(small_table, indices):
    matches = indices[:, None] == jnp.arange(small_table.shape[0], dtype=jnp.int32)[None, :]
    return jnp.sum(jnp.where(matches, small_table[None, :], 0), axis=1)


def attend_kernel(
    count, active, piece_stream, own_ref, sib_ref, bias_ref, cos_ref, sin_ref, k_ref, v_ref, lo_ref, hi_ref, o_ref, acc_ref
):
    slot = pl.program_id(1)
    piece_len = k_ref.shape[0] // piece_stream.shape[0]
    rows, wide = own_ref.shape
    per_kv = wide // HD
    scale = 1.0 / math.sqrt(HD)
    cosine, sine = cos_ref[...], sin_ref[...]
    query = own_ref[...] + sib_ref[...] + bias_ref[...]
    q = jnp.concatenate(
        [
            rotate_wide(query[:, i * HD : (i + 1) * HD], cosine, sine).astype(BF16)
            for i in range(per_kv)
        ],
        axis=0,
    )
    lo = lo_ref[0]
    hi = hi_ref[0]
    acc_ref[...] = jnp.zeros_like(acc_ref)

    def step(i, carry):
        top, total = carry
        piece = active[slot, i]
        first = pl.multiple_of(piece * piece_len, piece_len)
        k = k_ref[pl.ds(first, piece_len), :]
        v = v_ref[pl.ds(first, piece_len), :]
        s = lax.dot_general(k, q, (((1,), (1,)), ((), ())), preferred_element_type=F32) * scale
        stream = piece_stream[piece] * piece_len + lax.broadcasted_iota(jnp.int32, s.shape, 0)
        s = jnp.where((stream >= lo) & (stream <= hi), s, far_below)
        new_top = jnp.maximum(top, jnp.max(s, axis=0, keepdims=True))
        w = jnp.exp(s - new_top)
        fade = jnp.exp(top - new_top)
        total = total * fade + jnp.sum(w, axis=0, keepdims=True)
        part = lax.dot_general(v, w.astype(BF16), (((0,), (0,)), ((), ())), preferred_element_type=F32)
        acc_ref[...] = acc_ref[...] * fade + part
        return (new_top, total)

    top = jnp.full((1, q.shape[0]), start_top, F32)
    total = jnp.zeros((1, q.shape[0]), F32)
    top, total = lax.fori_loop(0, count[slot], step, (top, total))
    out = (acc_ref[...] / total).T.astype(BF16)
    for i in range(per_kv):
        o_ref[:, i * HD : (i + 1) * HD] = out[i * rows : (i + 1) * rows]


def attend(query, query_sib, bias, cosine, sine, kv_rows, lo, hi, piece_stream, kv_heads):
    rows, width = query_sib.shape
    slots = PIECES_DEV
    lo, hi = lo.reshape(slots, -1), hi.reshape(slots, -1)
    per_kv = width // (kv_heads * HD)
    keys = kv_rows.shape[0]
    pieces = piece_stream.shape[0]
    piece_len = keys // pieces
    first = piece_stream[None, None, :] * piece_len
    touch = jnp.any(
        (lo[:, :, None] <= first + piece_len - 1) & (hi[:, :, None] >= first), axis=1
    ).astype(jnp.int32)
    place = jnp.cumsum(touch, axis=1) - 1
    ids = jnp.arange(pieces, dtype=jnp.int32)
    active = jnp.sum(
        jnp.where((touch[:, :, None] > 0) & (place[:, :, None] == ids), ids[None, :, None], 0), axis=1
    ).astype(jnp.int32)
    count = jnp.sum(touch, axis=1).astype(jnp.int32)
    lo_wide = jnp.tile(lo, (1, per_kv))[:, None, :]
    hi_wide = jnp.tile(hi, (1, per_kv))[:, None, :]
    tile = (piece_len, per_kv * HD)
    return pl.pallas_call(
        attend_kernel,
        grid_spec=pltpu.PrefetchScalarGridSpec(
            num_scalar_prefetch=3,
            grid=(kv_heads, slots),
            in_specs=[
                pl.BlockSpec(tile, lambda g, h, *_: (h, g)),
                pl.BlockSpec(tile, lambda g, h, *_: (h, g)),
                pl.BlockSpec((1, per_kv * HD), lambda g, h, *_: (0, g)),
                pl.BlockSpec((piece_len, HD), lambda g, h, *_: (h, 0)),
                pl.BlockSpec((piece_len, HD), lambda g, h, *_: (h, 0)),
                pl.BlockSpec((keys, HD), lambda g, h, *_: (0, 2 * g)),
                pl.BlockSpec((keys, HD), lambda g, h, *_: (0, 2 * g + 1)),
                pl.BlockSpec((1, 1, piece_len * per_kv), lambda g, h, *_: (h, 0, 0)),
                pl.BlockSpec((1, 1, piece_len * per_kv), lambda g, h, *_: (h, 0, 0)),
            ],
            out_specs=pl.BlockSpec(tile, lambda g, h, *_: (h, g)),
            scratch_shapes=[pltpu.VMEM((HD, piece_len * per_kv), F32)],
        ),
        out_shape=jax.ShapeDtypeStruct((rows, width), BF16),
        compiler_params=pltpu.CompilerParams(vmem_limit_bytes=32 * 2**20),
    )(count, active, piece_stream, query, query_sib, bias, cosine, sine, kv_rows, kv_rows, lo_wide, hi_wide)


def product_kernel(x_ref, w_ref, o_ref):
    o_ref[...] = jnp.dot(x_ref[...], w_ref[...], preferred_element_type=F32).astype(o_ref.dtype)


def product(x, w, out_type):
    rows, inner = x.shape
    cols = w.shape[1]
    tile = next((t for t in (512, 384, 256) if cols % t == 0), cols)
    return pl.pallas_call(
        product_kernel,
        grid=(cols // tile,),
        in_specs=[
            pl.BlockSpec((rows, inner), lambda n: (0, 0)),
            pl.BlockSpec((inner, tile), lambda n: (0, n)),
        ],
        out_specs=pl.BlockSpec((rows, tile), lambda n: (0, n)),
        out_shape=jax.ShapeDtypeStruct((rows, cols), out_type),
        cost_estimate=pl.CostEstimate(flops=0, transcendentals=0, bytes_accessed=0),
        compiler_params=pltpu.CompilerParams(vmem_limit_bytes=48 * 2**20),
    )(x, w)


def join_kernel(own_ref, sib_ref, bias_ref, cos_ref, sin_ref, o_ref):
    rows, wide = o_ref.shape
    heads = wide // (2 * HD)
    cosine, sine = cos_ref[...], sin_ref[...]
    kv = own_ref[:rows, :] + sib_ref[...] + bias_ref[...]
    for g in range(heads):
        key = rotate_wide(kv[:, g * HD : (g + 1) * HD], cosine, sine)
        o_ref[:, 2 * g * HD : (2 * g + 1) * HD] = key.astype(BF16)
        value = kv[:, (heads + g) * HD : (heads + g + 1) * HD]
        o_ref[:, (2 * g + 1) * HD : (2 * g + 2) * HD] = value.astype(BF16)


def shards(
    layer_input,
    attention_gain,
    feedforward_gain,
    query_weight,
    key_weight,
    value_weight,
    out_weight,
    gate_weight,
    up_weight,
    down_weight,
    query_bias,
    key_bias,
    value_bias,
    doc_lengths,
    piece_order,
    cache_page,
):
    seq_count = lax.axis_size("seq")
    mlp_count = lax.axis_size("mlp")
    seq_rank = lax.axis_index("seq")
    mlp_rank = lax.axis_index("mlp")
    planes = seq_count // CORES
    plane = seq_rank // CORES
    core = seq_rank % CORES
    rows, width = layer_input.shape
    dz = width // planes
    ds = width // seq_count
    share = rows // mlp_count
    chunks = CHUNKS if share % (16 * CHUNKS) == 0 and planes > 3 else 1
    sub = share // chunks
    crows = mlp_count * sub
    piece_len = rows // PIECES_DEV
    bits = mlp_count.bit_length() - 1

    def move(x, pairs):
        return lax.ppermute(
            x, "seq", [(a * CORES + e, b * CORES + e) for a, b in pairs for e in range(CORES)]
        )

    def sibling(x):
        return lax.ppermute(
            x, "seq", [(a * CORES + e, a * CORES + 1 - e) for a in range(planes) for e in range(CORES)]
        )

    def partner(x, bit):
        return lax.ppermute(x, "mlp", [(a, a ^ bit) for a in range(mlp_count)])

    def after(x, dep):
        return lax.optimization_barrier((x, dep))

    def add(a, b):
        return (a.astype(F32) + b.astype(F32)).astype(BF16)

    def gather_step(state, t):
        ups, downs = state
        ups.append(move(ups[-1], [(i, i + 1) for i in range(t - 1, planes - 1)]))
        downs.append(move(downs[-1], [(i, i - 1) for i in range(1, planes - t + 1)]))

    def gather_slots(state):
        ups, downs = state
        return [ups[0]] + [ups[k] + downs[planes - k] for k in range(1, planes)]

    def line_gather(x):
        state = ([x], [x])
        for t in range(1, planes):
            gather_step(state, t)
        return gather_slots(state)

    def scatter_step(parts, carried, t, held=()):
        send_up, send_down = parts[t], parts[planes - t]
        if carried is not None:
            send_up, send_down = add(send_up, carried[0]), add(send_down, carried[1])
        send_up, send_down, held = lax.optimization_barrier((send_up, send_down, held))
        up = move(send_up, [(i, i + 1) for i in range(0, min(t, planes - 1))])
        down = move(send_down, [(i, i - 1) for i in range(max(1, planes - t), planes)])
        return (up, down), held

    half = max(1, planes // 2)
    orders = [list(range(bits)), [(b + bits // 2) % bits for b in range(bits)]]

    def sum_begin(x):
        return [{j: part[:, j] for j in range(mlp_count)} for part in (x[:half], x[half:])]

    def sum_sent(states, n):
        return [[j for j in sorted(v) if j & (1 << o[n])] for v, o in zip(states, orders)]

    def sum_launch(states, n):
        sends = [
            jnp.stack([v[j].astype(BF16) for j in w], axis=0) for v, w in zip(states, sum_sent(states, n))
        ]
        sends = lax.optimization_barrier(sends)
        return [partner(send, 1 << o[n]) for send, o in zip(sends, orders)]

    def sum_land(states, n, gots):
        return [
            {j ^ (1 << o[n]): v[j ^ (1 << o[n])].astype(F32) + got[i].astype(F32) for i, j in enumerate(w)}
            for v, w, o, got in zip(states, sum_sent(states, n), orders, gots)
        ]

    def sum_stage(states, n):
        return sum_land(states, n, sum_launch(states, n))

    def sum_end(states):
        return jnp.concatenate([v[0] for v in states], axis=0)

    def spread_begin(x):
        return [{0: x[:half]}, {0: x[half:]}]

    def spread_launch(states, n):
        sends = [jnp.stack([v[j] for j in sorted(v)], axis=0) for v in states]
        sends = lax.optimization_barrier(sends)
        return [partner(send, 1 << o[bits - 1 - n]) for send, o in zip(sends, orders)]

    def spread_land(states, n, gots):
        return [
            v | {j | (1 << o[bits - 1 - n]): got[i] for i, j in enumerate(sorted(v))}
            for v, o, got in zip(states, orders, gots)
        ]

    def spread_stage(states, n):
        return spread_land(states, n, spread_launch(states, n))

    def spread_end(states):
        return [jnp.stack([v[j] for j in range(mlp_count)], axis=1) for v in states]

    lines = [[z * CORES + e for z in range(planes)] for e in range(CORES)]

    def line_collect(x):
        return lax.all_gather(x, "seq", axis=0, tiled=True, axis_index_groups=lines)

    def swap_halves(x):
        return jnp.where(core == 0, x, jnp.concatenate([x[..., ds:], x[..., :ds]], axis=-1))

    order = []
    for k in range(1, planes // 2 + 1):
        order += [k] if 2 * k == planes else [k, planes - k]
    order.append(0)

    kv_cols = max(HD, KVH * HD // mlp_count)
    kv_first = mlp_rank * KVH // mlp_count * HD
    kv_weight = jnp.concatenate(
        [
            lax.dynamic_slice_in_dim(key_weight, kv_first, kv_cols, 1),
            lax.dynamic_slice_in_dim(value_weight, kv_first, kv_cols, 1),
        ],
        axis=1,
    )
    kv_bias = jnp.concatenate(
        [
            lax.dynamic_slice_in_dim(key_bias, kv_first, kv_cols, 0),
            lax.dynamic_slice_in_dim(value_bias, kv_first, kv_cols, 0),
        ]
    ).astype(F32)
    kv_weight, (gate_weight, up_weight, out_weight, down_weight, layer_input) = after(
        kv_weight, (gate_weight, up_weight, out_weight, down_weight, layer_input)
    )
    kv_weight = line_collect(kv_weight)
    q_weight = line_collect(query_weight)

    x = layer_input.astype(F32)
    mean_sq = jnp.mean(x * x, axis=-1, keepdims=True)
    normed = (x * lax.rsqrt(mean_sq + norm_eps) * attention_gain.astype(F32)).astype(BF16)
    even = jnp.concatenate([normed[:, CORES * z * ds : (CORES * z + 1) * ds] for z in range(planes)], axis=1)
    odd = jnp.concatenate([normed[:, (CORES * z + 1) * ds : CORES * (z + 1) * ds] for z in range(planes)], axis=1)
    mine = jnp.where(core == 0, even, odd)
    theirs = sibling(jnp.where(core == 0, odd, even))
    both = jnp.concatenate([mine, theirs], axis=0)

    units = gate_weight.shape[1]
    whole = units // HD * HD
    glu_own = jnp.concatenate(
        [gate_weight[:, :whole], up_weight[:, :whole], gate_weight[:, whole:], up_weight[:, whole:]],
        axis=1,
    )
    glu_own = lax.optimization_barrier(glu_own)
    glu_weight = jnp.concatenate(
        [
            jnp.pad(jnp.concatenate([glu_own, sibling(glu_own)], axis=0), ((0, 0), (0, HD))),
            jnp.pad(jnp.eye(HD, dtype=BF16), ((0, 0), (2 * units, 0))),
        ],
        axis=0,
    )
    out_wide = jnp.concatenate([out_weight, sibling(out_weight)], axis=1)
    down_wide = jnp.concatenate([down_weight, sibling(down_weight)], axis=1)

    own_share = lax.dynamic_slice_in_dim(layer_input, mlp_rank * share, share, 0)
    lane_sends = [lax.dynamic_slice_in_dim(own_share, (plane + k) % planes * dz, dz, 1) for k in order]
    gain_lane = swap_halves(lax.dynamic_slice_in_dim(feedforward_gain, plane * dz, dz, 0)).astype(F32)
    both, glu_weight, out_wide, down_wide, lane_sends = lax.optimization_barrier(
        (both, glu_weight, out_wide, down_wide, lane_sends)
    )

    row_ids = seq_rank * rows + jnp.arange(rows, dtype=jnp.int32)
    stream = lookup(piece_order, row_ids // piece_len) * piece_len + row_ids % piece_len
    doc_ends = jnp.cumsum(doc_lengths)
    segment = jnp.sum((stream[:, None] >= doc_ends[None, :]).astype(jnp.int32), axis=1)
    doc_first = lookup(doc_ends - doc_lengths, segment)
    cosine, sine = rope_tables(stream - doc_first, HD)

    kv_heads = kv_cols // HD
    kv = product(both, kv_weight, F32)
    joined = pl.pallas_call(
        join_kernel, out_shape=jax.ShapeDtypeStruct((rows, 2 * kv_cols), BF16)
    )(kv, sibling(kv[rows:]), kv_bias[None, :], cosine, sine)
    core_rows = jnp.concatenate(line_gather(joined), axis=0)
    kv_rows = jnp.concatenate([core_rows, sibling(core_rows)], axis=0)
    offsets = (plane - jnp.arange(planes, dtype=jnp.int32)) % planes
    slots = jnp.concatenate([offsets * CORES + core, offsets * CORES + 1 - core])
    slots = (slots[:, None] * PIECES_DEV + jnp.arange(PIECES_DEV, dtype=jnp.int32)).reshape(-1)
    piece_stream = lookup(piece_order, slots)

    own_cols = KVH * HD // mlp_count
    cache_width = 2 * own_cols
    offset = mlp_rank % max(1, HD // own_cols) * cache_width
    pieces = jnp.arange(piece_order.shape[0], dtype=jnp.int32)
    pages = []
    for p in range(PIECES_DEV):
        stream_piece = jnp.sum(jnp.where(cache_page == seq_rank * PIECES_DEV + p, pieces, 0))
        source = jnp.sum(jnp.where(piece_stream == stream_piece, pieces, 0))
        pages.append(lax.dynamic_slice(kv_rows, (source * piece_len, offset), (piece_len, cache_width)))
    kv_cache = jnp.concatenate(pages, axis=0)

    lane_sends, q_weight = after(lane_sends, q_weight)
    lane_parts = [
        move(v, [(i, (i + k) % planes) for i in range(planes)]) if k else v
        for k, v in zip(order, lane_sends)
    ]
    query = product(both, q_weight, F32)
    query_sib = sibling(query[rows:])
    mixed = attend(
        query, query_sib, query_bias.astype(F32)[None, :], cosine, sine, kv_rows, doc_first, stream, piece_stream, kv_heads
    )
    mixed, lane_parts = after(mixed, lane_parts)
    lane_input = swap_halves(jnp.stack(lane_parts, axis=0)).reshape(planes, chunks, sub, dz)
    chunked = [
        jnp.concatenate(
            [
                lax.dynamic_slice_in_dim(mixed, (mlp_rank ^ j) * share + h * sub, sub, 0)
                for j in range(mlp_count)
            ],
            axis=0,
        )
        for h in range(chunks)
    ]

    collected = [line_collect(v) for v in chunked]

    def attn_terms(h):
        heads = jnp.concatenate(
            [
                lax.dynamic_slice_in_dim(collected[h], (plane - k) % planes * crows, crows, 0)
                for k in order
            ],
            axis=0,
        )
        return sum_begin(product(heads, out_wide, BF16).reshape(planes, mlp_count, sub, dz))

    def attn_end(h, states):
        return lane_input[:, h].astype(F32) + sum_end(states)

    def lane_terms(residual):
        square = residual * residual
        square = sum(square[..., i : i + HD] for i in range(0, dz, HD))
        lane = jnp.concatenate([(residual * gain_lane).astype(BF16), square.astype(BF16)], axis=-1)
        return spread_begin(lane)

    def contract_half(lane):
        part = product(lane.reshape(-1, dz + HD), glu_weight, BF16).reshape(-1, crows, 2 * units + HD)
        return [part[i] for i in range(part.shape[0])]

    def contract(lanes):
        first = contract_half(lanes[0])
        last, first[0] = after(lanes[1], first[0])
        return dict(zip(order, first + contract_half(last)))

    def activate(part, carried):
        act = part[0].astype(F32) + carried[0].astype(F32) + carried[1].astype(F32)
        square = jnp.sum(act[:, 2 * units :], axis=1, keepdims=True)
        act = act * lax.rsqrt(square / width + norm_eps)
        hidden = jax.nn.silu(act[:, :whole]) * act[:, whole : 2 * whole]
        if units > whole:
            last = act[:, 2 * whole : 2 * units]
            edge = units - whole
            hidden = jnp.concatenate(
                [hidden, jax.nn.silu(last[:, :edge]) * last[:, edge:]], axis=1
            )
        return hidden.astype(BF16)

    def deliver(h, down):
        final = (residuals[h] + down).astype(BF16)
        found = {
            k: move(final[i], [(p, (p - k) % planes) for p in range(planes)]) if k else final[i]
            for i, k in enumerate(order)
        }
        return jnp.stack([found[k] for k in range(planes)])

    def down_terms(state):
        slots = gather_slots(state)
        hidden = jnp.concatenate([slots[k] for k in order], axis=0)
        return sum_begin(product(hidden, down_wide, BF16).reshape(planes, mlp_count, sub, dz))

    steps = planes - 1
    states = attn_terms(0)
    for n in range(bits):
        states = sum_stage(states, n)
    residuals = [attn_end(0, states)]
    states = lane_terms(residuals[0])
    for n in range(bits):
        states = spread_stage(states, n)
    lanes = lax.optimization_barrier(spread_end(states))
    first = contract_half(lanes[0])
    carried, last = scatter_step(dict(zip(order, first)), None, 1, lanes[1])
    parts = dict(zip(order, first + contract_half(last)))
    finals = [None] * chunks
    before, summing, following = None, None, None
    for h in range(chunks):
        flight = {}
        for t in range(1, steps + 1):
            if t > 1:
                if before is not None:
                    flight["state"] = (state[0][-1], state[1][-1])
                carried, flight = scatter_step(parts, carried, t, flight)
                if before is not None:
                    state[0][-1], state[1][-1] = flight.pop("state")
            if summing is not None:
                who, n, terms, gots = summing
                gots = flight.pop("down", gots)
                terms = sum_land(terms, n, gots)
                if n + 1 < bits:
                    flight["down"] = sum_launch(terms, n + 1)
                    summing = (who, n + 1, terms, None)
                else:
                    finals[who] = deliver(who, sum_end(terms))
                    summing = None
            if before is not None:
                if t == 1:
                    hidden = activate(*before)
                    state = ([hidden], [hidden])
                    gather_step(state, 1)
                    gather_step(state, 2)
                elif t < steps:
                    gather_step(state, t + 1)
                else:
                    terms = down_terms(state)
                    summing = (h - 1, 0, terms, sum_launch(terms, 0))
            if h + 1 < chunks:
                if t == 1:
                    collected[h + 1], parts[0] = after(collected[h + 1], parts[0])
                    states = attn_terms(h + 1)
                    flight["lead"] = sum_launch(states, 0)
                elif t == 2:
                    states = sum_land(states, 0, flight.pop("lead"))
                    for n in range(1, bits):
                        states = sum_stage(states, n)
                    residuals.append(attn_end(h + 1, states))
                    states = lane_terms(residuals[h + 1])
                    flight["lead"] = spread_launch(states, 0)
                elif t == 3:
                    states = spread_land(states, 0, flight.pop("lead"))
                    for n in range(1, bits):
                        states = spread_stage(states, n)
                    following = contract(spread_end(states))
        before = (parts, carried)
        if h + 1 < chunks:
            gots = summing[3] if summing is not None else ()
            carried, (behind, gots) = scatter_step(following, None, 1, (carried, gots))
            if summing is not None:
                summing = summing[:3] + (gots,)
            before = (parts, behind)
            parts = following
    hidden = activate(*before)
    state = ([hidden], [hidden])
    for t in range(1, steps + 1):
        gather_step(state, t)
        if summing is not None:
            who, n, terms, gots = summing
            (state[0][-1], state[1][-1]), gots = after((state[0][-1], state[1][-1]), gots)
            terms = sum_land(terms, n, gots)
            if n + 1 < bits:
                summing = (who, n + 1, terms, sum_launch(terms, n + 1))
            else:
                finals[who] = deliver(who, sum_end(terms))
                summing = None
    if chunks > 1:
        (state[0][-1], state[1][-1]), finals[:-1] = after((state[0][-1], state[1][-1]), finals[:-1])
    states = down_terms(state)
    for n in range(bits):
        states = sum_stage(states, n)
    finals[chunks - 1] = deliver(chunks - 1, sum_end(states))
    final = swap_halves(jnp.concatenate(finals, axis=1))
    final = lax.dynamic_slice_in_dim(
        jnp.concatenate([final, final], axis=0), (planes - plane) % planes, planes, 0
    )
    layer_output = jnp.swapaxes(final, 0, 1).reshape(share, width)
    return (layer_output, kv_cache)


def solution(mesh):
    placed = (
        P("seq", None),
        P(),
        P(),
        P("seq", "mlp"),
        P("seq", None),
        P("seq", None),
        P("mlp", "seq"),
        P("seq", "mlp"),
        P("seq", "mlp"),
        P("mlp", "seq"),
        P("mlp"),
        P(),
        P(),
        P(),
        P(),
        P(),
    )
    return jax.shard_map(
        shards,
        mesh=mesh,
        in_specs=placed,
        out_specs=(P(("seq", "mlp"), None), P("seq", "mlp")),
        check_vma=False,
    )
```

```python
import math

import jax
import jax.numpy as jnp
from jax import lax
from jax.experimental import pallas as pl
from jax.experimental.pallas import tpu as pltpu
from jax.sharding import PartitionSpec as P

KVH = 8
HD = 128
PIECES_DEV = 2
CORES = 2
CHUNKS = 2

rope_base = 1000000.0
norm_eps = 1e-06
far_below = -1e30
start_top = -1e29
F32 = jnp.float32
BF16 = jnp.bfloat16


def rope_tables(position, head_dim):
    half_dim = head_dim // 2
    inverse_freq = jnp.power(
        jnp.float32(rope_base), -2.0 * jnp.arange(half_dim, dtype=jnp.float32) / head_dim
    )
    angles = position.astype(jnp.float32)[:, None] * inverse_freq[None, :]
    cosine, sine = jnp.cos(angles), jnp.sin(angles)
    return (jnp.concatenate([cosine, cosine], axis=1), jnp.concatenate([-sine, sine], axis=1))


def rotate_wide(values, cosine, sine):
    return values * cosine + pltpu.roll(values, HD // 2, 1) * sine


def lookup(small_table, indices):
    matches = indices[:, None] == jnp.arange(small_table.shape[0], dtype=jnp.int32)[None, :]
    return jnp.sum(jnp.where(matches, small_table[None, :], 0), axis=1)


def attend_kernel(
    count, active, piece_stream, own_ref, sib_ref, bias_ref, cos_ref, sin_ref, k_ref, v_ref, lo_ref, hi_ref, o_ref, acc_ref
):
    slot = pl.program_id(1)
    piece_len = k_ref.shape[0] // piece_stream.shape[0]
    rows, wide = own_ref.shape
    per_kv = wide // HD
    scale = 1.0 / math.sqrt(HD)
    cosine, sine = cos_ref[...], sin_ref[...]
    query = own_ref[...] + sib_ref[...] + bias_ref[...]
    q = jnp.concatenate(
        [
            rotate_wide(query[:, i * HD : (i + 1) * HD], cosine, sine).astype(BF16)
            for i in range(per_kv)
        ],
        axis=0,
    )
    lo = lo_ref[0]
    hi = hi_ref[0]
    acc_ref[...] = jnp.zeros_like(acc_ref)

    def step(i, carry):
        top, total = carry
        piece = active[slot, i]
        first = pl.multiple_of(piece * piece_len, piece_len)
        k = k_ref[pl.ds(first, piece_len), :]
        v = v_ref[pl.ds(first, piece_len), :]
        s = lax.dot_general(k, q, (((1,), (1,)), ((), ())), preferred_element_type=F32) * scale
        stream = piece_stream[piece] * piece_len + lax.broadcasted_iota(jnp.int32, s.shape, 0)
        s = jnp.where((stream >= lo) & (stream <= hi), s, far_below)
        new_top = jnp.maximum(top, jnp.max(s, axis=0, keepdims=True))
        w = jnp.exp(s - new_top)
        fade = jnp.exp(top - new_top)
        total = total * fade + jnp.sum(w, axis=0, keepdims=True)
        part = lax.dot_general(v, w.astype(BF16), (((0,), (0,)), ((), ())), preferred_element_type=F32)
        acc_ref[...] = acc_ref[...] * fade + part
        return (new_top, total)

    top = jnp.full((1, q.shape[0]), start_top, F32)
    total = jnp.zeros((1, q.shape[0]), F32)
    top, total = lax.fori_loop(0, count[slot], step, (top, total))
    out = (acc_ref[...] / total).T.astype(BF16)
    for i in range(per_kv):
        o_ref[:, i * HD : (i + 1) * HD] = out[i * rows : (i + 1) * rows]


def attend(query, query_sib, bias, cosine, sine, kv_rows, lo, hi, piece_stream, kv_heads):
    rows, width = query_sib.shape
    slots = PIECES_DEV
    lo, hi = lo.reshape(slots, -1), hi.reshape(slots, -1)
    per_kv = width // (kv_heads * HD)
    keys = kv_rows.shape[0]
    pieces = piece_stream.shape[0]
    piece_len = keys // pieces
    first = piece_stream[None, None, :] * piece_len
    touch = jnp.any(
        (lo[:, :, None] <= first + piece_len - 1) & (hi[:, :, None] >= first), axis=1
    ).astype(jnp.int32)
    place = jnp.cumsum(touch, axis=1) - 1
    ids = jnp.arange(pieces, dtype=jnp.int32)
    active = jnp.sum(
        jnp.where((touch[:, :, None] > 0) & (place[:, :, None] == ids), ids[None, :, None], 0), axis=1
    ).astype(jnp.int32)
    count = jnp.sum(touch, axis=1).astype(jnp.int32)
    lo_wide = jnp.tile(lo, (1, per_kv))[:, None, :]
    hi_wide = jnp.tile(hi, (1, per_kv))[:, None, :]
    tile = (piece_len, per_kv * HD)
    return pl.pallas_call(
        attend_kernel,
        grid_spec=pltpu.PrefetchScalarGridSpec(
            num_scalar_prefetch=3,
            grid=(kv_heads, slots),
            in_specs=[
                pl.BlockSpec(tile, lambda g, h, *_: (h, g)),
                pl.BlockSpec(tile, lambda g, h, *_: (h, g)),
                pl.BlockSpec((1, per_kv * HD), lambda g, h, *_: (0, g)),
                pl.BlockSpec((piece_len, HD), lambda g, h, *_: (h, 0)),
                pl.BlockSpec((piece_len, HD), lambda g, h, *_: (h, 0)),
                pl.BlockSpec((keys, HD), lambda g, h, *_: (0, 2 * g)),
                pl.BlockSpec((keys, HD), lambda g, h, *_: (0, 2 * g + 1)),
                pl.BlockSpec((1, 1, piece_len * per_kv), lambda g, h, *_: (h, 0, 0)),
                pl.BlockSpec((1, 1, piece_len * per_kv), lambda g, h, *_: (h, 0, 0)),
            ],
            out_specs=pl.BlockSpec(tile, lambda g, h, *_: (h, g)),
            scratch_shapes=[pltpu.VMEM((HD, piece_len * per_kv), F32)],
        ),
        out_shape=jax.ShapeDtypeStruct((rows, width), BF16),
        compiler_params=pltpu.CompilerParams(vmem_limit_bytes=32 * 2**20),
    )(count, active, piece_stream, query, query_sib, bias, cosine, sine, kv_rows, kv_rows, lo_wide, hi_wide)


def product_kernel(x_ref, w_ref, o_ref):
    o_ref[...] = jnp.dot(x_ref[...], w_ref[...], preferred_element_type=F32).astype(o_ref.dtype)


def product(x, w, out_type):
    rows, inner = x.shape
    cols = w.shape[1]
    tile = next((t for t in (512, 384, 256) if cols % t == 0), cols)
    return pl.pallas_call(
        product_kernel,
        grid=(cols // tile,),
        in_specs=[
            pl.BlockSpec((rows, inner), lambda n: (0, 0)),
            pl.BlockSpec((inner, tile), lambda n: (0, n)),
        ],
        out_specs=pl.BlockSpec((rows, tile), lambda n: (0, n)),
        out_shape=jax.ShapeDtypeStruct((rows, cols), out_type),
        cost_estimate=pl.CostEstimate(flops=0, transcendentals=0, bytes_accessed=0),
        compiler_params=pltpu.CompilerParams(vmem_limit_bytes=48 * 2**20),
    )(x, w)


def join_kernel(own_ref, sib_ref, bias_ref, cos_ref, sin_ref, o_ref):
    rows, wide = o_ref.shape
    heads = wide // (2 * HD)
    cosine, sine = cos_ref[...], sin_ref[...]
    kv = own_ref[:rows, :] + sib_ref[...] + bias_ref[...]
    for g in range(heads):
        key = rotate_wide(kv[:, g * HD : (g + 1) * HD], cosine, sine)
        o_ref[:, 2 * g * HD : (2 * g + 1) * HD] = key.astype(BF16)
        value = kv[:, (heads + g) * HD : (heads + g + 1) * HD]
        o_ref[:, (2 * g + 1) * HD : (2 * g + 2) * HD] = value.astype(BF16)


def shards(
    layer_input,
    attention_gain,
    feedforward_gain,
    query_weight,
    key_weight,
    value_weight,
    out_weight,
    gate_weight,
    up_weight,
    down_weight,
    query_bias,
    key_bias,
    value_bias,
    doc_lengths,
    piece_order,
    cache_page,
):
    seq_count = lax.axis_size("seq")
    mlp_count = lax.axis_size("mlp")
    seq_rank = lax.axis_index("seq")
    mlp_rank = lax.axis_index("mlp")
    planes = seq_count // CORES
    plane = seq_rank // CORES
    core = seq_rank % CORES
    rows, width = layer_input.shape
    dz = width // planes
    ds = width // seq_count
    share = rows // mlp_count
    chunks = CHUNKS if share % (16 * CHUNKS) == 0 and planes > 3 else 1
    sub = share // chunks
    crows = mlp_count * sub
    piece_len = rows // PIECES_DEV
    bits = mlp_count.bit_length() - 1

    def move(x, pairs):
        return lax.ppermute(
            x, "seq", [(a * CORES + e, b * CORES + e) for a, b in pairs for e in range(CORES)]
        )

    def sibling(x):
        return lax.ppermute(
            x, "seq", [(a * CORES + e, a * CORES + 1 - e) for a in range(planes) for e in range(CORES)]
        )

    def partner(x, bit):
        return lax.ppermute(x, "mlp", [(a, a ^ bit) for a in range(mlp_count)])

    def after(x, dep):
        return lax.optimization_barrier((x, dep))

    def add(a, b):
        return (a.astype(F32) + b.astype(F32)).astype(BF16)

    def gather_step(state, t):
        ups, downs = state
        ups.append(move(ups[-1], [(i, i + 1) for i in range(t - 1, planes - 1)]))
        downs.append(move(downs[-1], [(i, i - 1) for i in range(1, planes - t + 1)]))

    def gather_slots(state):
        ups, downs = state
        return [ups[0]] + [ups[k] + downs[planes - k] for k in range(1, planes)]

    def line_gather(x):
        state = ([x], [x])
        for t in range(1, planes):
            gather_step(state, t)
        return gather_slots(state)

    def scatter_step(parts, carried, t, held=()):
        send_up, send_down = parts[t], parts[planes - t]
        if carried is not None:
            send_up, send_down = add(send_up, carried[0]), add(send_down, carried[1])
        send_up, send_down, held = lax.optimization_barrier((send_up, send_down, held))
        up = move(send_up, [(i, i + 1) for i in range(0, min(t, planes - 1))])
        down = move(send_down, [(i, i - 1) for i in range(max(1, planes - t), planes)])
        return (up, down), held

    half = max(1, planes // 2)
    orders = [list(range(bits)), [(b + bits // 2) % bits for b in range(bits)]]

    def sum_begin(x):
        return [{j: part[:, j] for j in range(mlp_count)} for part in (x[:half], x[half:])]

    def sum_sent(states, n):
        return [[j for j in sorted(v) if j & (1 << o[n])] for v, o in zip(states, orders)]

    def sum_launch(states, n):
        sends = [
            jnp.stack([v[j].astype(BF16) for j in w], axis=0) for v, w in zip(states, sum_sent(states, n))
        ]
        sends = lax.optimization_barrier(sends)
        return [partner(send, 1 << o[n]) for send, o in zip(sends, orders)]

    def sum_land(states, n, gots):
        return [
            {j ^ (1 << o[n]): v[j ^ (1 << o[n])].astype(F32) + got[i].astype(F32) for i, j in enumerate(w)}
            for v, w, o, got in zip(states, sum_sent(states, n), orders, gots)
        ]

    def sum_stage(states, n):
        return sum_land(states, n, sum_launch(states, n))

    def sum_end(states):
        return jnp.concatenate([v[0] for v in states], axis=0)

    def spread_begin(x):
        return [{0: x[:half]}, {0: x[half:]}]

    def spread_launch(states, n):
        sends = [jnp.stack([v[j] for j in sorted(v)], axis=0) for v in states]
        sends = lax.optimization_barrier(sends)
        return [partner(send, 1 << o[bits - 1 - n]) for send, o in zip(sends, orders)]

    def spread_land(states, n, gots):
        return [
            v | {j | (1 << o[bits - 1 - n]): got[i] for i, j in enumerate(sorted(v))}
            for v, o, got in zip(states, orders, gots)
        ]

    def spread_stage(states, n):
        return spread_land(states, n, spread_launch(states, n))

    def spread_end(states):
        return [jnp.stack([v[j] for j in range(mlp_count)], axis=1) for v in states]

    lines = [[z * CORES + e for z in range(planes)] for e in range(CORES)]

    def line_collect(x):
        return lax.all_gather(x, "seq", axis=0, tiled=True, axis_index_groups=lines)

    def swap_halves(x):
        return jnp.where(core == 0, x, jnp.concatenate([x[..., ds:], x[..., :ds]], axis=-1))

    order = []
    for k in range(1, planes // 2 + 1):
        order += [k] if 2 * k == planes else [k, planes - k]
    order.append(0)

    kv_cols = max(HD, KVH * HD // mlp_count)
    kv_first = mlp_rank * KVH // mlp_count * HD
    kv_weight = jnp.concatenate(
        [
            lax.dynamic_slice_in_dim(key_weight, kv_first, kv_cols, 1),
            lax.dynamic_slice_in_dim(value_weight, kv_first, kv_cols, 1),
        ],
        axis=1,
    )
    kv_bias = jnp.concatenate(
        [
            lax.dynamic_slice_in_dim(key_bias, kv_first, kv_cols, 0),
            lax.dynamic_slice_in_dim(value_bias, kv_first, kv_cols, 0),
        ]
    ).astype(F32)
    kv_weight, (gate_weight, up_weight, out_weight, down_weight, layer_input) = after(
        kv_weight, (gate_weight, up_weight, out_weight, down_weight, layer_input)
    )
    kv_weight = line_collect(kv_weight)
    q_weight = line_collect(query_weight)

    x = layer_input.astype(F32)
    mean_sq = jnp.mean(x * x, axis=-1, keepdims=True)
    normed = (x * lax.rsqrt(mean_sq + norm_eps) * attention_gain.astype(F32)).astype(BF16)
    even = jnp.concatenate([normed[:, CORES * z * ds : (CORES * z + 1) * ds] for z in range(planes)], axis=1)
    odd = jnp.concatenate([normed[:, (CORES * z + 1) * ds : CORES * (z + 1) * ds] for z in range(planes)], axis=1)
    mine = jnp.where(core == 0, even, odd)
    theirs = sibling(jnp.where(core == 0, odd, even))
    both = jnp.concatenate([mine, theirs], axis=0)

    units = gate_weight.shape[1]
    whole = units // HD * HD
    glu_own = jnp.concatenate(
        [gate_weight[:, :whole], up_weight[:, :whole], gate_weight[:, whole:], up_weight[:, whole:]],
        axis=1,
    )
    glu_own = lax.optimization_barrier(glu_own)
    glu_weight = jnp.concatenate(
        [
            jnp.pad(jnp.concatenate([glu_own, sibling(glu_own)], axis=0), ((0, 0), (0, HD))),
            jnp.pad(jnp.eye(HD, dtype=BF16), ((0, 0), (2 * units, 0))),
        ],
        axis=0,
    )
    out_wide = jnp.concatenate([out_weight, sibling(out_weight)], axis=1)
    down_wide = jnp.concatenate([down_weight, sibling(down_weight)], axis=1)

    own_share = lax.dynamic_slice_in_dim(layer_input, mlp_rank * share, share, 0)
    lane_sends = [lax.dynamic_slice_in_dim(own_share, (plane + k) % planes * dz, dz, 1) for k in order]
    gain_lane = swap_halves(lax.dynamic_slice_in_dim(feedforward_gain, plane * dz, dz, 0)).astype(F32)
    both, glu_weight, out_wide, down_wide, lane_sends = lax.optimization_barrier(
        (both, glu_weight, out_wide, down_wide, lane_sends)
    )

    row_ids = seq_rank * rows + jnp.arange(rows, dtype=jnp.int32)
    stream = lookup(piece_order, row_ids // piece_len) * piece_len + row_ids % piece_len
    doc_ends = jnp.cumsum(doc_lengths)
    segment = jnp.sum((stream[:, None] >= doc_ends[None, :]).astype(jnp.int32), axis=1)
    doc_first = lookup(doc_ends - doc_lengths, segment)
    cosine, sine = rope_tables(stream - doc_first, HD)

    kv_heads = kv_cols // HD
    kv = product(both, kv_weight, F32)
    joined = pl.pallas_call(
        join_kernel, out_shape=jax.ShapeDtypeStruct((rows, 2 * kv_cols), BF16)
    )(kv, sibling(kv[rows:]), kv_bias[None, :], cosine, sine)
    core_rows = jnp.concatenate(line_gather(joined), axis=0)
    kv_rows = jnp.concatenate([core_rows, sibling(core_rows)], axis=0)
    offsets = (plane - jnp.arange(planes, dtype=jnp.int32)) % planes
    slots = jnp.concatenate([offsets * CORES + core, offsets * CORES + 1 - core])
    slots = (slots[:, None] * PIECES_DEV + jnp.arange(PIECES_DEV, dtype=jnp.int32)).reshape(-1)
    piece_stream = lookup(piece_order, slots)

    own_cols = KVH * HD // mlp_count
    cache_width = 2 * own_cols
    offset = mlp_rank % max(1, HD // own_cols) * cache_width
    pieces = jnp.arange(piece_order.shape[0], dtype=jnp.int32)
    pages = []
    for p in range(PIECES_DEV):
        stream_piece = jnp.sum(jnp.where(cache_page == seq_rank * PIECES_DEV + p, pieces, 0))
        source = jnp.sum(jnp.where(piece_stream == stream_piece, pieces, 0))
        pages.append(lax.dynamic_slice(kv_rows, (source * piece_len, offset), (piece_len, cache_width)))
    kv_cache = jnp.concatenate(pages, axis=0)

    lane_sends, q_weight = after(lane_sends, q_weight)
    lane_parts = [
        move(v, [(i, (i + k) % planes) for i in range(planes)]) if k else v
        for k, v in zip(order, lane_sends)
    ]
    query = product(both, q_weight, F32)
    query_sib = sibling(query[rows:])
    mixed = attend(
        query, query_sib, query_bias.astype(F32)[None, :], cosine, sine, kv_rows, doc_first, stream, piece_stream, kv_heads
    )
    mixed, lane_parts = after(mixed, lane_parts)
    lane_input = swap_halves(jnp.stack(lane_parts, axis=0)).reshape(planes, chunks, sub, dz)
    chunked = [
        jnp.concatenate(
            [
                lax.dynamic_slice_in_dim(mixed, (mlp_rank ^ j) * share + h * sub, sub, 0)
                for j in range(mlp_count)
            ],
            axis=0,
        )
        for h in range(chunks)
    ]

    collected = [line_collect(v) for v in chunked]

    def attn_terms(h):
        heads = jnp.concatenate(
            [
                lax.dynamic_slice_in_dim(collected[h], (plane - k) % planes * crows, crows, 0)
                for k in order
            ],
            axis=0,
        )
        return sum_begin(product(heads, out_wide, BF16).reshape(planes, mlp_count, sub, dz))

    def attn_end(h, states):
        return lane_input[:, h].astype(F32) + sum_end(states)

    def lane_terms(residual):
        square = residual * residual
        square = sum(square[..., i : i + HD] for i in range(0, dz, HD))
        lane = jnp.concatenate([(residual * gain_lane).astype(BF16), square.astype(BF16)], axis=-1)
        return spread_begin(lane)

    def contract_half(lane):
        part = product(lane.reshape(-1, dz + HD), glu_weight, BF16).reshape(-1, crows, 2 * units + HD)
        return [part[i] for i in range(part.shape[0])]

    def contract(lanes):
        first = contract_half(lanes[0])
        last, first[0] = after(lanes[1], first[0])
        return dict(zip(order, first + contract_half(last)))

    def activate(part, carried):
        act = part[0].astype(F32) + carried[0].astype(F32) + carried[1].astype(F32)
        square = jnp.sum(act[:, 2 * units :], axis=1, keepdims=True)
        act = act * lax.rsqrt(square / width + norm_eps)
        hidden = jax.nn.silu(act[:, :whole]) * act[:, whole : 2 * whole]
        if units > whole:
            last = act[:, 2 * whole : 2 * units]
            edge = units - whole
            hidden = jnp.concatenate(
                [hidden, jax.nn.silu(last[:, :edge]) * last[:, edge:]], axis=1
            )
        return hidden.astype(BF16)

    def deliver(h, down):
        final = (residuals[h] + down).astype(BF16)
        found = {
            k: move(final[i], [(p, (p - k) % planes) for p in range(planes)]) if k else final[i]
            for i, k in enumerate(order)
        }
        return jnp.stack([found[k] for k in range(planes)])

    def down_terms(state):
        slots = gather_slots(state)
        hidden = jnp.concatenate([slots[k] for k in order], axis=0)
        return sum_begin(product(hidden, down_wide, BF16).reshape(planes, mlp_count, sub, dz))

    steps = planes - 1
    states = attn_terms(0)
    for n in range(bits):
        states = sum_stage(states, n)
    residuals = [attn_end(0, states)]
    states = lane_terms(residuals[0])
    for n in range(bits):
        states = spread_stage(states, n)
    lanes = lax.optimization_barrier(spread_end(states))
    first = contract_half(lanes[0])
    carried, last = scatter_step(dict(zip(order, first)), None, 1, lanes[1])
    parts = dict(zip(order, first + contract_half(last)))
    finals = [None] * chunks
    before, summing, following = None, None, None
    for h in range(chunks):
        flight = {}
        for t in range(1, steps + 1):
            if t > 1:
                if before is not None:
                    flight["state"] = (state[0][-1], state[1][-1])
                carried, flight = scatter_step(parts, carried, t, flight)
                if before is not None:
                    state[0][-1], state[1][-1] = flight.pop("state")
            if summing is not None:
                who, n, terms, gots = summing
                gots = flight.pop("down", gots)
                terms = sum_land(terms, n, gots)
                if n + 1 < bits:
                    flight["down"] = sum_launch(terms, n + 1)
                    summing = (who, n + 1, terms, None)
                else:
                    finals[who] = deliver(who, sum_end(terms))
                    summing = None
            if before is not None:
                if t == 1:
                    hidden = activate(*before)
                    state = ([hidden], [hidden])
                    gather_step(state, 1)
                    gather_step(state, 2)
                elif t < steps:
                    gather_step(state, t + 1)
                else:
                    terms = down_terms(state)
                    summing = (h - 1, 0, terms, sum_launch(terms, 0))
            if h + 1 < chunks:
                if t == 1:
                    collected[h + 1], parts[0] = after(collected[h + 1], parts[0])
                    states = attn_terms(h + 1)
                    flight["lead"] = sum_launch(states, 0)
                elif t == 2:
                    states = sum_land(states, 0, flight.pop("lead"))
                    for n in range(1, bits):
                        states = sum_stage(states, n)
                    residuals.append(attn_end(h + 1, states))
                    states = lane_terms(residuals[h + 1])
                    flight["lead"] = spread_launch(states, 0)
                elif t == 3:
                    states = spread_land(states, 0, flight.pop("lead"))
                    for n in range(1, bits):
                        states = spread_stage(states, n)
                    following = contract(spread_end(states))
        before = (parts, carried)
        if h + 1 < chunks:
            gots = summing[3] if summing is not None else ()
            carried, (behind, gots) = scatter_step(following, None, 1, (carried, gots))
            if summing is not None:
                summing = summing[:3] + (gots,)
            before = (parts, behind)
            parts = following
    hidden = activate(*before)
    state = ([hidden], [hidden])
    for t in range(1, steps + 1):
        gather_step(state, t)
        if summing is not None:
            who, n, terms, gots = summing
            (state[0][-1], state[1][-1]), gots = after((state[0][-1], state[1][-1]), gots)
            terms = sum_land(terms, n, gots)
            if n + 1 < bits:
                summing = (who, n + 1, terms, sum_launch(terms, n + 1))
            else:
                finals[who] = deliver(who, sum_end(terms))
                summing = None
    if chunks > 1:
        (state[0][-1], state[1][-1]), finals[:-1] = after((state[0][-1], state[1][-1]), finals[:-1])
    states = down_terms(state)
    for n in range(bits):
        states = sum_stage(states, n)
    finals[chunks - 1] = deliver(chunks - 1, sum_end(states))
    final = swap_halves(jnp.concatenate(finals, axis=1))
    final = lax.dynamic_slice_in_dim(
        jnp.concatenate([final, final], axis=0), (planes - plane) % planes, planes, 0
    )
    layer_output = jnp.swapaxes(final, 0, 1).reshape(share, width)
    return (layer_output, kv_cache)


def solution(mesh):
    placed = (
        P("seq", None),
        P(),
        P(),
        P("seq", "mlp"),
        P("seq", None),
        P("seq", None),
        P("mlp", "seq"),
        P("seq", "mlp"),
        P("seq", "mlp"),
        P("mlp", "seq"),
        P("mlp"),
        P(),
        P(),
        P(),
        P(),
        P(),
    )
    return jax.shard_map(
        shards,
        mesh=mesh,
        in_specs=placed,
        out_specs=(P(("seq", "mlp"), None), P("seq", "mlp")),
        check_vma=False,
    )
```

```python
import math

import jax
import jax.numpy as jnp
from jax import lax
from jax.experimental import pallas as pl
from jax.experimental.pallas import tpu as pltpu
from jax.sharding import PartitionSpec as P

KVH = 8
HD = 128
PIECES_DEV = 2
CORES = 2
CHUNKS = 2

rope_base = 1000000.0
norm_eps = 1e-06
far_below = -1e30
start_top = -1e29
F32 = jnp.float32
BF16 = jnp.bfloat16


def rope_tables(position, head_dim):
    half_dim = head_dim // 2
    inverse_freq = jnp.power(
        jnp.float32(rope_base), -2.0 * jnp.arange(half_dim, dtype=jnp.float32) / head_dim
    )
    angles = position.astype(jnp.float32)[:, None] * inverse_freq[None, :]
    cosine, sine = jnp.cos(angles), jnp.sin(angles)
    return (jnp.concatenate([cosine, cosine], axis=1), jnp.concatenate([-sine, sine], axis=1))


def rotate_wide(values, cosine, sine):
    return values * cosine + pltpu.roll(values, HD // 2, 1) * sine


def lookup(small_table, indices):
    matches = indices[:, None] == jnp.arange(small_table.shape[0], dtype=jnp.int32)[None, :]
    return jnp.sum(jnp.where(matches, small_table[None, :], 0), axis=1)


def attend_kernel(
    count, active, piece_stream, own_ref, sib_ref, bias_ref, cos_ref, sin_ref, k_ref, v_ref, lo_ref, hi_ref, o_ref, acc_ref
):
    slot = pl.program_id(1)
    piece_len = k_ref.shape[0] // piece_stream.shape[0]
    rows, wide = own_ref.shape
    per_kv = wide // HD
    scale = 1.0 / math.sqrt(HD)
    cosine, sine = cos_ref[...], sin_ref[...]
    query = own_ref[...] + sib_ref[...] + bias_ref[...]
    q = jnp.concatenate(
        [
            rotate_wide(query[:, i * HD : (i + 1) * HD], cosine, sine).astype(BF16)
            for i in range(per_kv)
        ],
        axis=0,
    )
    lo = lo_ref[0]
    hi = hi_ref[0]
    acc_ref[...] = jnp.zeros_like(acc_ref)

    def step(i, carry):
        top, total = carry
        piece = active[slot, i]
        first = pl.multiple_of(piece * piece_len, piece_len)
        k = k_ref[pl.ds(first, piece_len), :]
        v = v_ref[pl.ds(first, piece_len), :]
        s = lax.dot_general(k, q, (((1,), (1,)), ((), ())), preferred_element_type=F32) * scale
        stream = piece_stream[piece] * piece_len + lax.broadcasted_iota(jnp.int32, s.shape, 0)
        s = jnp.where((stream >= lo) & (stream <= hi), s, far_below)
        new_top = jnp.maximum(top, jnp.max(s, axis=0, keepdims=True))
        w = jnp.exp(s - new_top)
        fade = jnp.exp(top - new_top)
        total = total * fade + jnp.sum(w, axis=0, keepdims=True)
        part = lax.dot_general(v, w.astype(BF16), (((0,), (0,)), ((), ())), preferred_element_type=F32)
        acc_ref[...] = acc_ref[...] * fade + part
        return (new_top, total)

    top = jnp.full((1, q.shape[0]), start_top, F32)
    total = jnp.zeros((1, q.shape[0]), F32)
    top, total = lax.fori_loop(0, count[slot], step, (top, total))
    out = (acc_ref[...] / total).T.astype(BF16)
    for i in range(per_kv):
        o_ref[:, i * HD : (i + 1) * HD] = out[i * rows : (i + 1) * rows]


def attend(query, query_sib, bias, cosine, sine, kv_rows, lo, hi, piece_stream, kv_heads):
    rows, width = query_sib.shape
    slots = PIECES_DEV
    lo, hi = lo.reshape(slots, -1), hi.reshape(slots, -1)
    per_kv = width // (kv_heads * HD)
    keys = kv_rows.shape[0]
    pieces = piece_stream.shape[0]
    piece_len = keys // pieces
    first = piece_stream[None, None, :] * piece_len
    touch = jnp.any(
        (lo[:, :, None] <= first + piece_len - 1) & (hi[:, :, None] >= first), axis=1
    ).astype(jnp.int32)
    place = jnp.cumsum(touch, axis=1) - 1
    ids = jnp.arange(pieces, dtype=jnp.int32)
    active = jnp.sum(
        jnp.where((touch[:, :, None] > 0) & (place[:, :, None] == ids), ids[None, :, None], 0), axis=1
    ).astype(jnp.int32)
    count = jnp.sum(touch, axis=1).astype(jnp.int32)
    lo_wide = jnp.tile(lo, (1, per_kv))[:, None, :]
    hi_wide = jnp.tile(hi, (1, per_kv))[:, None, :]
    tile = (piece_len, per_kv * HD)
    return pl.pallas_call(
        attend_kernel,
        grid_spec=pltpu.PrefetchScalarGridSpec(
            num_scalar_prefetch=3,
            grid=(kv_heads, slots),
            in_specs=[
                pl.BlockSpec(tile, lambda g, h, *_: (h, g)),
                pl.BlockSpec(tile, lambda g, h, *_: (h, g)),
                pl.BlockSpec((1, per_kv * HD), lambda g, h, *_: (0, g)),
                pl.BlockSpec((piece_len, HD), lambda g, h, *_: (h, 0)),
                pl.BlockSpec((piece_len, HD), lambda g, h, *_: (h, 0)),
                pl.BlockSpec((keys, HD), lambda g, h, *_: (0, 2 * g)),
                pl.BlockSpec((keys, HD), lambda g, h, *_: (0, 2 * g + 1)),
                pl.BlockSpec((1, 1, piece_len * per_kv), lambda g, h, *_: (h, 0, 0)),
                pl.BlockSpec((1, 1, piece_len * per_kv), lambda g, h, *_: (h, 0, 0)),
            ],
            out_specs=pl.BlockSpec(tile, lambda g, h, *_: (h, g)),
            scratch_shapes=[pltpu.VMEM((HD, piece_len * per_kv), F32)],
        ),
        out_shape=jax.ShapeDtypeStruct((rows, width), BF16),
        compiler_params=pltpu.CompilerParams(vmem_limit_bytes=32 * 2**20),
    )(count, active, piece_stream, query, query_sib, bias, cosine, sine, kv_rows, kv_rows, lo_wide, hi_wide)


def product_kernel(x_ref, w_ref, o_ref):
    o_ref[...] = jnp.dot(x_ref[...], w_ref[...], preferred_element_type=F32).astype(o_ref.dtype)


def product(x, w, out_type):
    rows, inner = x.shape
    cols = w.shape[1]
    tile = next((t for t in (512, 384, 256) if cols % t == 0), cols)
    return pl.pallas_call(
        product_kernel,
        grid=(cols // tile,),
        in_specs=[
            pl.BlockSpec((rows, inner), lambda n: (0, 0)),
            pl.BlockSpec((inner, tile), lambda n: (0, n)),
        ],
        out_specs=pl.BlockSpec((rows, tile), lambda n: (0, n)),
        out_shape=jax.ShapeDtypeStruct((rows, cols), out_type),
        cost_estimate=pl.CostEstimate(flops=0, transcendentals=0, bytes_accessed=0),
        compiler_params=pltpu.CompilerParams(vmem_limit_bytes=48 * 2**20),
    )(x, w)


def join_kernel(own_ref, sib_ref, bias_ref, cos_ref, sin_ref, o_ref):
    rows, wide = o_ref.shape
    heads = wide // (2 * HD)
    cosine, sine = cos_ref[...], sin_ref[...]
    kv = own_ref[:rows, :] + sib_ref[...] + bias_ref[...]
    for g in range(heads):
        key = rotate_wide(kv[:, g * HD : (g + 1) * HD], cosine, sine)
        o_ref[:, 2 * g * HD : (2 * g + 1) * HD] = key.astype(BF16)
        value = kv[:, (heads + g) * HD : (heads + g + 1) * HD]
        o_ref[:, (2 * g + 1) * HD : (2 * g + 2) * HD] = value.astype(BF16)


def shards(
    layer_input,
    attention_gain,
    feedforward_gain,
    query_weight,
    key_weight,
    value_weight,
    out_weight,
    gate_weight,
    up_weight,
    down_weight,
    query_bias,
    key_bias,
    value_bias,
    doc_lengths,
    piece_order,
    cache_page,
):
    seq_count = lax.axis_size("seq")
    mlp_count = lax.axis_size("mlp")
    seq_rank = lax.axis_index("seq")
    mlp_rank = lax.axis_index("mlp")
    planes = seq_count // CORES
    plane = seq_rank // CORES
    core = seq_rank % CORES
    rows, width = layer_input.shape
    dz = width // planes
    ds = width // seq_count
    share = rows // mlp_count
    chunks = CHUNKS if share % (16 * CHUNKS) == 0 and planes > 3 else 1
    sub = share // chunks
    crows = mlp_count * sub
    piece_len = rows // PIECES_DEV
    bits = mlp_count.bit_length() - 1

    def move(x, pairs):
        return lax.ppermute(
            x, "seq", [(a * CORES + e, b * CORES + e) for a, b in pairs for e in range(CORES)]
        )

    def sibling(x):
        return lax.ppermute(
            x, "seq", [(a * CORES + e, a * CORES + 1 - e) for a in range(planes) for e in range(CORES)]
        )

    def partner(x, bit):
        return lax.ppermute(x, "mlp", [(a, a ^ bit) for a in range(mlp_count)])

    def after(x, dep):
        return lax.optimization_barrier((x, dep))

    def add(a, b):
        return (a.astype(F32) + b.astype(F32)).astype(BF16)

    def gather_step(state, t):
        ups, downs = state
        ups.append(move(ups[-1], [(i, i + 1) for i in range(t - 1, planes - 1)]))
        downs.append(move(downs[-1], [(i, i - 1) for i in range(1, planes - t + 1)]))

    def gather_slots(state):
        ups, downs = state
        return [ups[0]] + [ups[k] + downs[planes - k] for k in range(1, planes)]

    def line_gather(x):
        state = ([x], [x])
        for t in range(1, planes):
            gather_step(state, t)
        return gather_slots(state)

    def scatter_step(parts, carried, t, held=()):
        send_up, send_down = parts[t], parts[planes - t]
        if carried is not None:
            send_up, send_down = add(send_up, carried[0]), add(send_down, carried[1])
        send_up, send_down, held = lax.optimization_barrier((send_up, send_down, held))
        up = move(send_up, [(i, i + 1) for i in range(0, min(t, planes - 1))])
        down = move(send_down, [(i, i - 1) for i in range(max(1, planes - t), planes)])
        return (up, down), held

    half = max(1, planes // 2)
    orders = [list(range(bits)), [(b + bits // 2) % bits for b in range(bits)]]

    def sum_begin(x):
        return [{j: part[:, j] for j in range(mlp_count)} for part in (x[:half], x[half:])]

    def sum_sent(states, n):
        return [[j for j in sorted(v) if j & (1 << o[n])] for v, o in zip(states, orders)]

    def sum_launch(states, n):
        sends = [
            jnp.stack([v[j].astype(BF16) for j in w], axis=0) for v, w in zip(states, sum_sent(states, n))
        ]
        sends = lax.optimization_barrier(sends)
        return [partner(send, 1 << o[n]) for send, o in zip(sends, orders)]

    def sum_land(states, n, gots):
        return [
            {j ^ (1 << o[n]): v[j ^ (1 << o[n])].astype(F32) + got[i].astype(F32) for i, j in enumerate(w)}
            for v, w, o, got in zip(states, sum_sent(states, n), orders, gots)
        ]

    def sum_stage(states, n):
        return sum_land(states, n, sum_launch(states, n))

    def sum_end(states):
        return jnp.concatenate([v[0] for v in states], axis=0)

    def spread_begin(x):
        return [{0: x[:half]}, {0: x[half:]}]

    def spread_launch(states, n):
        sends = [jnp.stack([v[j] for j in sorted(v)], axis=0) for v in states]
        sends = lax.optimization_barrier(sends)
        return [partner(send, 1 << o[bits - 1 - n]) for send, o in zip(sends, orders)]

    def spread_land(states, n, gots):
        return [
            v | {j | (1 << o[bits - 1 - n]): got[i] for i, j in enumerate(sorted(v))}
            for v, o, got in zip(states, orders, gots)
        ]

    def spread_stage(states, n):
        return spread_land(states, n, spread_launch(states, n))

    def spread_end(states):
        return [jnp.stack([v[j] for j in range(mlp_count)], axis=1) for v in states]

    lines = [[z * CORES + e for z in range(planes)] for e in range(CORES)]

    def line_collect(x):
        return lax.all_gather(x, "seq", axis=0, tiled=True, axis_index_groups=lines)

    def swap_halves(x):
        return jnp.where(core == 0, x, jnp.concatenate([x[..., ds:], x[..., :ds]], axis=-1))

    order = []
    for k in range(1, planes // 2 + 1):
        order += [k] if 2 * k == planes else [k, planes - k]
    order.append(0)

    kv_cols = max(HD, KVH * HD // mlp_count)
    kv_first = mlp_rank * KVH // mlp_count * HD
    kv_weight = jnp.concatenate(
        [
            lax.dynamic_slice_in_dim(key_weight, kv_first, kv_cols, 1),
            lax.dynamic_slice_in_dim(value_weight, kv_first, kv_cols, 1),
        ],
        axis=1,
    )
    kv_bias = jnp.concatenate(
        [
            lax.dynamic_slice_in_dim(key_bias, kv_first, kv_cols, 0),
            lax.dynamic_slice_in_dim(value_bias, kv_first, kv_cols, 0),
        ]
    ).astype(F32)
    kv_weight, (gate_weight, up_weight, out_weight, down_weight, layer_input) = after(
        kv_weight, (gate_weight, up_weight, out_weight, down_weight, layer_input)
    )
    kv_weight = line_collect(kv_weight)
    q_weight = line_collect(query_weight)

    x = layer_input.astype(F32)
    mean_sq = jnp.mean(x * x, axis=-1, keepdims=True)
    normed = (x * lax.rsqrt(mean_sq + norm_eps) * attention_gain.astype(F32)).astype(BF16)
    even = jnp.concatenate([normed[:, CORES * z * ds : (CORES * z + 1) * ds] for z in range(planes)], axis=1)
    odd = jnp.concatenate([normed[:, (CORES * z + 1) * ds : CORES * (z + 1) * ds] for z in range(planes)], axis=1)
    mine = jnp.where(core == 0, even, odd)
    theirs = sibling(jnp.where(core == 0, odd, even))
    both = jnp.concatenate([mine, theirs], axis=0)

    units = gate_weight.shape[1]
    whole = units // HD * HD
    glu_own = jnp.concatenate(
        [gate_weight[:, :whole], up_weight[:, :whole], gate_weight[:, whole:], up_weight[:, whole:]],
        axis=1,
    )
    glu_own = lax.optimization_barrier(glu_own)
    glu_weight = jnp.concatenate(
        [
            jnp.pad(jnp.concatenate([glu_own, sibling(glu_own)], axis=0), ((0, 0), (0, HD))),
            jnp.pad(jnp.eye(HD, dtype=BF16), ((0, 0), (2 * units, 0))),
        ],
        axis=0,
    )
    out_wide = jnp.concatenate([out_weight, sibling(out_weight)], axis=1)
    down_wide = jnp.concatenate([down_weight, sibling(down_weight)], axis=1)

    own_share = lax.dynamic_slice_in_dim(layer_input, mlp_rank * share, share, 0)
    lane_sends = [lax.dynamic_slice_in_dim(own_share, (plane + k) % planes * dz, dz, 1) for k in order]
    gain_lane = swap_halves(lax.dynamic_slice_in_dim(feedforward_gain, plane * dz, dz, 0)).astype(F32)
    both, glu_weight, out_wide, down_wide, lane_sends = lax.optimization_barrier(
        (both, glu_weight, out_wide, down_wide, lane_sends)
    )

    row_ids = seq_rank * rows + jnp.arange(rows, dtype=jnp.int32)
    stream = lookup(piece_order, row_ids // piece_len) * piece_len + row_ids % piece_len
    doc_ends = jnp.cumsum(doc_lengths)
    segment = jnp.sum((stream[:, None] >= doc_ends[None, :]).astype(jnp.int32), axis=1)
    doc_first = lookup(doc_ends - doc_lengths, segment)
    cosine, sine = rope_tables(stream - doc_first, HD)

    kv_heads = kv_cols // HD
    kv = product(both, kv_weight, F32)
    joined = pl.pallas_call(
        join_kernel, out_shape=jax.ShapeDtypeStruct((rows, 2 * kv_cols), BF16)
    )(kv, sibling(kv[rows:]), kv_bias[None, :], cosine, sine)
    core_rows = jnp.concatenate(line_gather(joined), axis=0)
    kv_rows = jnp.concatenate([core_rows, sibling(core_rows)], axis=0)
    offsets = (plane - jnp.arange(planes, dtype=jnp.int32)) % planes
    slots = jnp.concatenate([offsets * CORES + core, offsets * CORES + 1 - core])
    slots = (slots[:, None] * PIECES_DEV + jnp.arange(PIECES_DEV, dtype=jnp.int32)).reshape(-1)
    piece_stream = lookup(piece_order, slots)

    own_cols = KVH * HD // mlp_count
    cache_width = 2 * own_cols
    offset = mlp_rank % max(1, HD // own_cols) * cache_width
    pieces = jnp.arange(piece_order.shape[0], dtype=jnp.int32)
    pages = []
    for p in range(PIECES_DEV):
        stream_piece = jnp.sum(jnp.where(cache_page == seq_rank * PIECES_DEV + p, pieces, 0))
        source = jnp.sum(jnp.where(piece_stream == stream_piece, pieces, 0))
        pages.append(lax.dynamic_slice(kv_rows, (source * piece_len, offset), (piece_len, cache_width)))
    kv_cache = jnp.concatenate(pages, axis=0)

    lane_sends, q_weight = after(lane_sends, q_weight)
    lane_parts = [
        move(v, [(i, (i + k) % planes) for i in range(planes)]) if k else v
        for k, v in zip(order, lane_sends)
    ]
    query = product(both, q_weight, F32)
    query_sib = sibling(query[rows:])
    mixed = attend(
        query, query_sib, query_bias.astype(F32)[None, :], cosine, sine, kv_rows, doc_first, stream, piece_stream, kv_heads
    )
    mixed, lane_parts = after(mixed, lane_parts)
    lane_input = swap_halves(jnp.stack(lane_parts, axis=0)).reshape(planes, chunks, sub, dz)
    chunked = [
        jnp.concatenate(
            [
                lax.dynamic_slice_in_dim(mixed, (mlp_rank ^ j) * share + h * sub, sub, 0)
                for j in range(mlp_count)
            ],
            axis=0,
        )
        for h in range(chunks)
    ]

    collected = [line_collect(v) for v in chunked]

    def attn_terms(h):
        heads = jnp.concatenate(
            [
                lax.dynamic_slice_in_dim(collected[h], (plane - k) % planes * crows, crows, 0)
                for k in order
            ],
            axis=0,
        )
        return sum_begin(product(heads, out_wide, BF16).reshape(planes, mlp_count, sub, dz))

    def attn_end(h, states):
        return lane_input[:, h].astype(F32) + sum_end(states)

    def lane_terms(residual):
        square = residual * residual
        square = sum(square[..., i : i + HD] for i in range(0, dz, HD))
        lane = jnp.concatenate([(residual * gain_lane).astype(BF16), square.astype(BF16)], axis=-1)
        return spread_begin(lane)

    def contract(lanes):
        lane = jnp.concatenate(lanes, axis=0).reshape(planes * crows, dz + HD)
        part = product(lane, glu_weight, BF16).reshape(planes, crows, 2 * units + HD)
        return {k: part[i] for i, k in enumerate(order)}

    def activate(part, carried):
        act = part[0].astype(F32) + carried[0].astype(F32) + carried[1].astype(F32)
        square = jnp.sum(act[:, 2 * units :], axis=1, keepdims=True)
        act = act * lax.rsqrt(square / width + norm_eps)
        hidden = jax.nn.silu(act[:, :whole]) * act[:, whole : 2 * whole]
        if units > whole:
            last = act[:, 2 * whole : 2 * units]
            edge = units - whole
            hidden = jnp.concatenate(
                [hidden, jax.nn.silu(last[:, :edge]) * last[:, edge:]], axis=1
            )
        return hidden.astype(BF16)

    def deliver(h, down):
        final = (residuals[h] + down).astype(BF16)
        found = {
            k: move(final[i], [(p, (p - k) % planes) for p in range(planes)]) if k else final[i]
            for i, k in enumerate(order)
        }
        return jnp.stack([found[k] for k in range(planes)])

    def down_terms(state):
        slots = gather_slots(state)
        hidden = jnp.concatenate([slots[k] for k in order], axis=0)
        return sum_begin(product(hidden, down_wide, BF16).reshape(planes, mlp_count, sub, dz))

    steps = planes - 1
    states = attn_terms(0)
    for n in range(bits):
        states = sum_stage(states, n)
    residuals = [attn_end(0, states)]
    states = lane_terms(residuals[0])
    for n in range(bits):
        states = spread_stage(states, n)
    parts = contract(spread_end(states))
    carried, _ = scatter_step(parts, None, 1)
    finals = [None] * chunks
    before, summing, following = None, None, None
    for h in range(chunks):
        flight = {}
        for t in range(1, steps + 1):
            if t > 1:
                if before is not None:
                    flight["state"] = (state[0][-1], state[1][-1])
                carried, flight = scatter_step(parts, carried, t, flight)
                if before is not None:
                    state[0][-1], state[1][-1] = flight.pop("state")
            if summing is not None:
                who, n, terms, gots = summing
                gots = flight.pop("down", gots)
                terms = sum_land(terms, n, gots)
                if n + 1 < bits:
                    flight["down"] = sum_launch(terms, n + 1)
                    summing = (who, n + 1, terms, None)
                else:
                    finals[who] = deliver(who, sum_end(terms))
                    summing = None
            if before is not None:
                if t == 1:
                    gather_step(state, 2)
                elif t < steps:
                    gather_step(state, t + 1)
                else:
                    terms = down_terms(state)
                    summing = (h - 1, 0, terms, sum_launch(terms, 0))
            if h + 1 < chunks:
                if t == 1:
                    collected[h + 1], parts[0] = after(collected[h + 1], parts[0])
                    states = attn_terms(h + 1)
                    flight["lead"] = sum_launch(states, 0)
                elif t == 2:
                    states = sum_land(states, 0, flight.pop("lead"))
                    for n in range(1, bits):
                        states = sum_stage(states, n)
                    residuals.append(attn_end(h + 1, states))
                    states = lane_terms(residuals[h + 1])
                    flight["lead"] = spread_launch(states, 0)
                elif t == 3:
                    states = spread_land(states, 0, flight.pop("lead"))
                    for n in range(1, bits):
                        states = spread_stage(states, n)
                    following = contract(spread_end(states))
        before = (parts, carried)
        if h + 1 < chunks:
            hidden = activate(*before)
            state = ([hidden], [hidden])
            gather_step(state, 1)
            gots = summing[3] if summing is not None else ()
            (state[0][-1], state[1][-1]), (parts, gots) = after((state[0][-1], state[1][-1]), (following, gots))
            if summing is not None:
                summing = summing[:3] + (gots,)
            carried, _ = scatter_step(parts, None, 1)
    hidden = activate(*before)
    state = ([hidden], [hidden])
    for t in range(1, steps + 1):
        gather_step(state, t)
        if summing is not None:
            who, n, terms, gots = summing
            (state[0][-1], state[1][-1]), gots = after((state[0][-1], state[1][-1]), gots)
            terms = sum_land(terms, n, gots)
            if n + 1 < bits:
                summing = (who, n + 1, terms, sum_launch(terms, n + 1))
            else:
                finals[who] = deliver(who, sum_end(terms))
                summing = None
    if chunks > 1:
        (state[0][-1], state[1][-1]), finals[:-1] = after((state[0][-1], state[1][-1]), finals[:-1])
    states = down_terms(state)
    for n in range(bits):
        states = sum_stage(states, n)
    finals[chunks - 1] = deliver(chunks - 1, sum_end(states))
    final = swap_halves(jnp.concatenate(finals, axis=1))
    final = lax.dynamic_slice_in_dim(
        jnp.concatenate([final, final], axis=0), (planes - plane) % planes, planes, 0
    )
    layer_output = jnp.swapaxes(final, 0, 1).reshape(share, width)
    return (layer_output, kv_cache)


def solution(mesh):
    placed = (
        P("seq", None),
        P(),
        P(),
        P("seq", "mlp"),
        P("seq", None),
        P("seq", None),
        P("mlp", "seq"),
        P("seq", "mlp"),
        P("seq", "mlp"),
        P("mlp", "seq"),
        P("mlp"),
        P(),
        P(),
        P(),
        P(),
        P(),
    )
    return jax.shard_map(
        shards,
        mesh=mesh,
        in_specs=placed,
        out_specs=(P(("seq", "mlp"), None), P("seq", "mlp")),
        check_vma=False,
    )
```

```python
import math

import jax
import jax.numpy as jnp
from jax import lax
from jax.experimental import pallas as pl
from jax.experimental.pallas import tpu as pltpu
from jax.sharding import PartitionSpec as P

KVH = 8
HD = 128
PIECES_DEV = 2
CORES = 2
CHUNKS = 2

rope_base = 1000000.0
norm_eps = 1e-06
far_below = -1e30
start_top = -1e29
F32 = jnp.float32
BF16 = jnp.bfloat16


def rope_tables(position, head_dim):
    half_dim = head_dim // 2
    inverse_freq = jnp.power(
        jnp.float32(rope_base), -2.0 * jnp.arange(half_dim, dtype=jnp.float32) / head_dim
    )
    angles = position.astype(jnp.float32)[:, None] * inverse_freq[None, :]
    cosine, sine = jnp.cos(angles), jnp.sin(angles)
    return (jnp.concatenate([cosine, cosine], axis=1), jnp.concatenate([-sine, sine], axis=1))


def rotate_wide(values, cosine, sine):
    return values * cosine + pltpu.roll(values, HD // 2, 1) * sine


def lookup(small_table, indices):
    matches = indices[:, None] == jnp.arange(small_table.shape[0], dtype=jnp.int32)[None, :]
    return jnp.sum(jnp.where(matches, small_table[None, :], 0), axis=1)


def attend_kernel(
    count, active, piece_stream, own_ref, sib_ref, bias_ref, cos_ref, sin_ref, k_ref, v_ref, lo_ref, hi_ref, o_ref, acc_ref
):
    slot = pl.program_id(1)
    piece_len = k_ref.shape[0] // piece_stream.shape[0]
    rows, wide = own_ref.shape
    per_kv = wide // HD
    scale = 1.0 / math.sqrt(HD)
    cosine, sine = cos_ref[...], sin_ref[...]
    query = own_ref[...] + sib_ref[...] + bias_ref[...]
    q = jnp.concatenate(
        [
            rotate_wide(query[:, i * HD : (i + 1) * HD], cosine, sine).astype(BF16)
            for i in range(per_kv)
        ],
        axis=0,
    )
    lo = lo_ref[0]
    hi = hi_ref[0]
    acc_ref[...] = jnp.zeros_like(acc_ref)

    def step(i, carry):
        top, total = carry
        piece = active[slot, i]
        first = pl.multiple_of(piece * piece_len, piece_len)
        k = k_ref[pl.ds(first, piece_len), :]
        v = v_ref[pl.ds(first, piece_len), :]
        s = lax.dot_general(k, q, (((1,), (1,)), ((), ())), preferred_element_type=F32) * scale
        stream = piece_stream[piece] * piece_len + lax.broadcasted_iota(jnp.int32, s.shape, 0)
        s = jnp.where((stream >= lo) & (stream <= hi), s, far_below)
        new_top = jnp.maximum(top, jnp.max(s, axis=0, keepdims=True))
        w = jnp.exp(s - new_top)
        fade = jnp.exp(top - new_top)
        total = total * fade + jnp.sum(w, axis=0, keepdims=True)
        part = lax.dot_general(v, w.astype(BF16), (((0,), (0,)), ((), ())), preferred_element_type=F32)
        acc_ref[...] = acc_ref[...] * fade + part
        return (new_top, total)

    top = jnp.full((1, q.shape[0]), start_top, F32)
    total = jnp.zeros((1, q.shape[0]), F32)
    top, total = lax.fori_loop(0, count[slot], step, (top, total))
    out = (acc_ref[...] / total).T.astype(BF16)
    for i in range(per_kv):
        o_ref[:, i * HD : (i + 1) * HD] = out[i * rows : (i + 1) * rows]


def attend(query, query_sib, bias, cosine, sine, kv_rows, lo, hi, piece_stream, kv_heads):
    rows, width = query_sib.shape
    slots = PIECES_DEV
    lo, hi = lo.reshape(slots, -1), hi.reshape(slots, -1)
    per_kv = width // (kv_heads * HD)
    keys = kv_rows.shape[0]
    pieces = piece_stream.shape[0]
    piece_len = keys // pieces
    first = piece_stream[None, None, :] * piece_len
    touch = jnp.any(
        (lo[:, :, None] <= first + piece_len - 1) & (hi[:, :, None] >= first), axis=1
    ).astype(jnp.int32)
    place = jnp.cumsum(touch, axis=1) - 1
    ids = jnp.arange(pieces, dtype=jnp.int32)
    active = jnp.sum(
        jnp.where((touch[:, :, None] > 0) & (place[:, :, None] == ids), ids[None, :, None], 0), axis=1
    ).astype(jnp.int32)
    count = jnp.sum(touch, axis=1).astype(jnp.int32)
    lo_wide = jnp.tile(lo, (1, per_kv))[:, None, :]
    hi_wide = jnp.tile(hi, (1, per_kv))[:, None, :]
    tile = (piece_len, per_kv * HD)
    return pl.pallas_call(
        attend_kernel,
        grid_spec=pltpu.PrefetchScalarGridSpec(
            num_scalar_prefetch=3,
            grid=(kv_heads, slots),
            in_specs=[
                pl.BlockSpec(tile, lambda g, h, *_: (h, g)),
                pl.BlockSpec(tile, lambda g, h, *_: (h, g)),
                pl.BlockSpec((1, per_kv * HD), lambda g, h, *_: (0, g)),
                pl.BlockSpec((piece_len, HD), lambda g, h, *_: (h, 0)),
                pl.BlockSpec((piece_len, HD), lambda g, h, *_: (h, 0)),
                pl.BlockSpec((keys, HD), lambda g, h, *_: (0, 2 * g)),
                pl.BlockSpec((keys, HD), lambda g, h, *_: (0, 2 * g + 1)),
                pl.BlockSpec((1, 1, piece_len * per_kv), lambda g, h, *_: (h, 0, 0)),
                pl.BlockSpec((1, 1, piece_len * per_kv), lambda g, h, *_: (h, 0, 0)),
            ],
            out_specs=pl.BlockSpec(tile, lambda g, h, *_: (h, g)),
            scratch_shapes=[pltpu.VMEM((HD, piece_len * per_kv), F32)],
        ),
        out_shape=jax.ShapeDtypeStruct((rows, width), BF16),
        compiler_params=pltpu.CompilerParams(vmem_limit_bytes=32 * 2**20),
    )(count, active, piece_stream, query, query_sib, bias, cosine, sine, kv_rows, kv_rows, lo_wide, hi_wide)


def product_kernel(x_ref, w_ref, *o_refs):
    found = jnp.dot(x_ref[...], w_ref[...], preferred_element_type=F32)
    rows = o_refs[0].shape[0]
    for i, o_ref in enumerate(o_refs):
        o_ref[...] = found[i * rows : (i + 1) * rows].astype(o_ref.dtype)


def product(x, w, out_type, pieces=1):
    rows, inner = x.shape
    cols = w.shape[1]
    tile = next((t for t in (512, 384, 256) if cols % t == 0), cols)
    return pl.pallas_call(
        product_kernel,
        grid=(cols // tile,),
        in_specs=[
            pl.BlockSpec((rows, inner), lambda n: (0, 0)),
            pl.BlockSpec((inner, tile), lambda n: (0, n)),
        ],
        out_specs=[pl.BlockSpec((rows // pieces, tile), lambda n: (0, n))] * pieces,
        out_shape=[jax.ShapeDtypeStruct((rows // pieces, cols), out_type)] * pieces,
        cost_estimate=pl.CostEstimate(flops=0, transcendentals=0, bytes_accessed=0),
        compiler_params=pltpu.CompilerParams(vmem_limit_bytes=48 * 2**20),
    )(x, w)


def join_kernel(own_ref, sib_ref, bias_ref, cos_ref, sin_ref, o_ref):
    rows, wide = o_ref.shape
    heads = wide // (2 * HD)
    cosine, sine = cos_ref[...], sin_ref[...]
    kv = own_ref[:rows, :] + sib_ref[...] + bias_ref[...]
    for g in range(heads):
        key = rotate_wide(kv[:, g * HD : (g + 1) * HD], cosine, sine)
        o_ref[:, 2 * g * HD : (2 * g + 1) * HD] = key.astype(BF16)
        value = kv[:, (heads + g) * HD : (heads + g + 1) * HD]
        o_ref[:, (2 * g + 1) * HD : (2 * g + 2) * HD] = value.astype(BF16)


def shards(
    layer_input,
    attention_gain,
    feedforward_gain,
    query_weight,
    key_weight,
    value_weight,
    out_weight,
    gate_weight,
    up_weight,
    down_weight,
    query_bias,
    key_bias,
    value_bias,
    doc_lengths,
    piece_order,
    cache_page,
):
    seq_count = lax.axis_size("seq")
    mlp_count = lax.axis_size("mlp")
    seq_rank = lax.axis_index("seq")
    mlp_rank = lax.axis_index("mlp")
    planes = seq_count // CORES
    plane = seq_rank // CORES
    core = seq_rank % CORES
    rows, width = layer_input.shape
    dz = width // planes
    ds = width // seq_count
    share = rows // mlp_count
    chunks = CHUNKS if share % (16 * CHUNKS) == 0 and planes > 3 else 1
    sub = share // chunks
    crows = mlp_count * sub
    piece_len = rows // PIECES_DEV
    bits = mlp_count.bit_length() - 1

    def move(x, pairs):
        return lax.ppermute(
            x, "seq", [(a * CORES + e, b * CORES + e) for a, b in pairs for e in range(CORES)]
        )

    def sibling(x):
        return lax.ppermute(
            x, "seq", [(a * CORES + e, a * CORES + 1 - e) for a in range(planes) for e in range(CORES)]
        )

    def partner(x, bit):
        return lax.ppermute(x, "mlp", [(a, a ^ bit) for a in range(mlp_count)])

    def after(x, dep):
        return lax.optimization_barrier((x, dep))

    def add(a, b):
        return (a.astype(F32) + b.astype(F32)).astype(BF16)

    def gather_step(state, t):
        ups, downs = state
        ups.append(move(ups[-1], [(i, i + 1) for i in range(t - 1, planes - 1)]))
        downs.append(move(downs[-1], [(i, i - 1) for i in range(1, planes - t + 1)]))

    def gather_slots(state):
        ups, downs = state
        return [ups[0]] + [ups[k] + downs[planes - k] for k in range(1, planes)]

    def line_gather(x):
        state = ([x], [x])
        for t in range(1, planes):
            gather_step(state, t)
        return gather_slots(state)

    def scatter_step(parts, carried, t, held=()):
        send_up, send_down = parts[t], parts[planes - t]
        if carried is not None:
            send_up, send_down = add(send_up, carried[0]), add(send_down, carried[1])
        send_up, send_down, held = lax.optimization_barrier((send_up, send_down, held))
        up = move(send_up, [(i, i + 1) for i in range(0, min(t, planes - 1))])
        down = move(send_down, [(i, i - 1) for i in range(max(1, planes - t), planes)])
        return (up, down), held

    half = max(1, planes // 2)
    orders = [list(range(bits)), [(b + bits // 2) % bits for b in range(bits)]]

    def sum_begin(x):
        return [{j: part[:, j] for j in range(mlp_count)} for part in (x[:half], x[half:])]

    def sum_sent(states, n):
        return [[j for j in sorted(v) if j & (1 << o[n])] for v, o in zip(states, orders)]

    def sum_launch(states, n):
        sends = [
            jnp.stack([v[j].astype(BF16) for j in w], axis=0) for v, w in zip(states, sum_sent(states, n))
        ]
        sends = lax.optimization_barrier(sends)
        return [partner(send, 1 << o[n]) for send, o in zip(sends, orders)]

    def sum_land(states, n, gots):
        return [
            {j ^ (1 << o[n]): v[j ^ (1 << o[n])].astype(F32) + got[i].astype(F32) for i, j in enumerate(w)}
            for v, w, o, got in zip(states, sum_sent(states, n), orders, gots)
        ]

    def sum_stage(states, n):
        return sum_land(states, n, sum_launch(states, n))

    def sum_end(states):
        return jnp.concatenate([v[0] for v in states], axis=0)

    def spread_begin(x):
        return [{0: x[:half]}, {0: x[half:]}]

    def spread_launch(states, n):
        sends = [jnp.stack([v[j] for j in sorted(v)], axis=0) for v in states]
        sends = lax.optimization_barrier(sends)
        return [partner(send, 1 << o[bits - 1 - n]) for send, o in zip(sends, orders)]

    def spread_land(states, n, gots):
        return [
            v | {j | (1 << o[bits - 1 - n]): got[i] for i, j in enumerate(sorted(v))}
            for v, o, got in zip(states, orders, gots)
        ]

    def spread_stage(states, n):
        return spread_land(states, n, spread_launch(states, n))

    def spread_end(states):
        return [jnp.stack([v[j] for j in range(mlp_count)], axis=1) for v in states]

    lines = [[z * CORES + e for z in range(planes)] for e in range(CORES)]

    def line_collect(x):
        return lax.all_gather(x, "seq", axis=0, tiled=True, axis_index_groups=lines)

    def swap_halves(x):
        return jnp.where(core == 0, x, jnp.concatenate([x[..., ds:], x[..., :ds]], axis=-1))

    order = []
    for k in range(1, planes // 2 + 1):
        order += [k] if 2 * k == planes else [k, planes - k]
    order.append(0)

    kv_cols = max(HD, KVH * HD // mlp_count)
    kv_first = mlp_rank * KVH // mlp_count * HD
    kv_weight = jnp.concatenate(
        [
            lax.dynamic_slice_in_dim(key_weight, kv_first, kv_cols, 1),
            lax.dynamic_slice_in_dim(value_weight, kv_first, kv_cols, 1),
        ],
        axis=1,
    )
    kv_bias = jnp.concatenate(
        [
            lax.dynamic_slice_in_dim(key_bias, kv_first, kv_cols, 0),
            lax.dynamic_slice_in_dim(value_bias, kv_first, kv_cols, 0),
        ]
    ).astype(F32)
    kv_weight, (gate_weight, up_weight, out_weight, down_weight, layer_input) = after(
        kv_weight, (gate_weight, up_weight, out_weight, down_weight, layer_input)
    )
    kv_weight = line_collect(kv_weight)
    q_weight = line_collect(query_weight)

    x = layer_input.astype(F32)
    mean_sq = jnp.mean(x * x, axis=-1, keepdims=True)
    normed = (x * lax.rsqrt(mean_sq + norm_eps) * attention_gain.astype(F32)).astype(BF16)
    even = jnp.concatenate([normed[:, CORES * z * ds : (CORES * z + 1) * ds] for z in range(planes)], axis=1)
    odd = jnp.concatenate([normed[:, (CORES * z + 1) * ds : CORES * (z + 1) * ds] for z in range(planes)], axis=1)
    mine = jnp.where(core == 0, even, odd)
    theirs = sibling(jnp.where(core == 0, odd, even))
    both = jnp.concatenate([mine, theirs], axis=0)

    units = gate_weight.shape[1]
    whole = units // HD * HD
    glu_own = jnp.concatenate(
        [gate_weight[:, :whole], up_weight[:, :whole], gate_weight[:, whole:], up_weight[:, whole:]],
        axis=1,
    )
    glu_own = lax.optimization_barrier(glu_own)
    glu_weight = jnp.concatenate(
        [
            jnp.pad(jnp.concatenate([glu_own, sibling(glu_own)], axis=0), ((0, 0), (0, HD))),
            jnp.pad(jnp.eye(HD, dtype=BF16), ((0, 0), (2 * units, 0))),
        ],
        axis=0,
    )
    out_wide = jnp.concatenate([out_weight, sibling(out_weight)], axis=1)
    down_wide = jnp.concatenate([down_weight, sibling(down_weight)], axis=1)

    own_share = lax.dynamic_slice_in_dim(layer_input, mlp_rank * share, share, 0)
    lane_sends = [lax.dynamic_slice_in_dim(own_share, (plane + k) % planes * dz, dz, 1) for k in order]
    gain_lane = swap_halves(lax.dynamic_slice_in_dim(feedforward_gain, plane * dz, dz, 0)).astype(F32)
    both, glu_weight, out_wide, down_wide, lane_sends = lax.optimization_barrier(
        (both, glu_weight, out_wide, down_wide, lane_sends)
    )

    row_ids = seq_rank * rows + jnp.arange(rows, dtype=jnp.int32)
    stream = lookup(piece_order, row_ids // piece_len) * piece_len + row_ids % piece_len
    doc_ends = jnp.cumsum(doc_lengths)
    segment = jnp.sum((stream[:, None] >= doc_ends[None, :]).astype(jnp.int32), axis=1)
    doc_first = lookup(doc_ends - doc_lengths, segment)
    cosine, sine = rope_tables(stream - doc_first, HD)

    kv_heads = kv_cols // HD
    kv, kv_theirs = product(both, kv_weight, F32, 2)
    joined = pl.pallas_call(
        join_kernel, out_shape=jax.ShapeDtypeStruct((rows, 2 * kv_cols), BF16)
    )(kv, sibling(kv_theirs), kv_bias[None, :], cosine, sine)
    core_rows = jnp.concatenate(line_gather(joined), axis=0)
    kv_rows = jnp.concatenate([core_rows, sibling(core_rows)], axis=0)
    offsets = (plane - jnp.arange(planes, dtype=jnp.int32)) % planes
    slots = jnp.concatenate([offsets * CORES + core, offsets * CORES + 1 - core])
    slots = (slots[:, None] * PIECES_DEV + jnp.arange(PIECES_DEV, dtype=jnp.int32)).reshape(-1)
    piece_stream = lookup(piece_order, slots)

    own_cols = KVH * HD // mlp_count
    cache_width = 2 * own_cols
    offset = mlp_rank % max(1, HD // own_cols) * cache_width
    pieces = jnp.arange(piece_order.shape[0], dtype=jnp.int32)
    pages = []
    for p in range(PIECES_DEV):
        stream_piece = jnp.sum(jnp.where(cache_page == seq_rank * PIECES_DEV + p, pieces, 0))
        source = jnp.sum(jnp.where(piece_stream == stream_piece, pieces, 0))
        pages.append(lax.dynamic_slice(kv_rows, (source * piece_len, offset), (piece_len, cache_width)))
    kv_cache = jnp.concatenate(pages, axis=0)

    lane_sends, q_weight = after(lane_sends, q_weight)
    lane_parts = [
        move(v, [(i, (i + k) % planes) for i in range(planes)]) if k else v
        for k, v in zip(order, lane_sends)
    ]
    query, query_theirs = product(both, q_weight, F32, 2)
    query_sib = sibling(query_theirs)
    mixed = attend(
        query, query_sib, query_bias.astype(F32)[None, :], cosine, sine, kv_rows, doc_first, stream, piece_stream, kv_heads
    )
    mixed, lane_parts = after(mixed, lane_parts)
    lane_input = swap_halves(jnp.stack(lane_parts, axis=0)).reshape(planes, chunks, sub, dz)
    chunked = [
        jnp.concatenate(
            [
                lax.dynamic_slice_in_dim(mixed, (mlp_rank ^ j) * share + h * sub, sub, 0)
                for j in range(mlp_count)
            ],
            axis=0,
        )
        for h in range(chunks)
    ]

    collected = [line_collect(v) for v in chunked]

    def attn_terms(h):
        heads = jnp.concatenate(
            [
                lax.dynamic_slice_in_dim(collected[h], (plane - k) % planes * crows, crows, 0)
                for k in order
            ],
            axis=0,
        )
        return sum_begin(product(heads, out_wide, BF16)[0].reshape(planes, mlp_count, sub, dz))

    def attn_end(h, states):
        return lane_input[:, h].astype(F32) + sum_end(states)

    def lane_terms(residual):
        square = residual * residual
        square = sum(square[..., i : i + HD] for i in range(0, dz, HD))
        lane = jnp.concatenate([(residual * gain_lane).astype(BF16), square.astype(BF16)], axis=-1)
        return spread_begin(lane)

    def contract(lanes):
        lane = jnp.concatenate(lanes, axis=0).reshape(planes * crows, dz + HD)
        return dict(zip(order, product(lane, glu_weight, BF16, planes)))

    def activate(part, carried):
        act = part[0].astype(F32) + carried[0].astype(F32) + carried[1].astype(F32)
        square = jnp.sum(act[:, 2 * units :], axis=1, keepdims=True)
        act = act * lax.rsqrt(square / width + norm_eps)
        hidden = jax.nn.silu(act[:, :whole]) * act[:, whole : 2 * whole]
        if units > whole:
            last = act[:, 2 * whole : 2 * units]
            edge = units - whole
            hidden = jnp.concatenate(
                [hidden, jax.nn.silu(last[:, :edge]) * last[:, edge:]], axis=1
            )
        return hidden.astype(BF16)

    def deliver(h, down):
        final = (residuals[h] + down).astype(BF16)
        found = {
            k: move(final[i], [(p, (p - k) % planes) for p in range(planes)]) if k else final[i]
            for i, k in enumerate(order)
        }
        return jnp.stack([found[k] for k in range(planes)])

    def down_terms(state):
        slots = gather_slots(state)
        hidden = jnp.concatenate([slots[k] for k in order], axis=0)
        return sum_begin(product(hidden, down_wide, BF16)[0].reshape(planes, mlp_count, sub, dz))

    steps = planes - 1
    states = attn_terms(0)
    for n in range(bits):
        states = sum_stage(states, n)
    residuals = [attn_end(0, states)]
    states = lane_terms(residuals[0])
    for n in range(bits):
        states = spread_stage(states, n)
    parts = contract(spread_end(states))
    carried, _ = scatter_step(parts, None, 1)
    finals = [None] * chunks
    before, summing, following = None, None, None
    for h in range(chunks):
        flight = {}
        for t in range(1, steps + 1):
            if t > 1:
                if before is not None:
                    flight["state"] = (state[0][-1], state[1][-1])
                carried, flight = scatter_step(parts, carried, t, flight)
                if before is not None:
                    state[0][-1], state[1][-1] = flight.pop("state")
            if summing is not None:
                who, n, terms, gots = summing
                gots = flight.pop("down", gots)
                terms = sum_land(terms, n, gots)
                if n + 1 < bits:
                    flight["down"] = sum_launch(terms, n + 1)
                    summing = (who, n + 1, terms, None)
                else:
                    finals[who] = deliver(who, sum_end(terms))
                    summing = None
            if before is not None:
                if t == 1:
                    gather_step(state, 2)
                elif t < steps:
                    gather_step(state, t + 1)
                else:
                    terms = down_terms(state)
                    summing = (h - 1, 0, terms, sum_launch(terms, 0))
            if h + 1 < chunks:
                if t == 1:
                    collected[h + 1], parts[0] = after(collected[h + 1], parts[0])
                    states = attn_terms(h + 1)
                    flight["lead"] = sum_launch(states, 0)
                elif t == 2:
                    states = sum_land(states, 0, flight.pop("lead"))
                    for n in range(1, bits):
                        states = sum_stage(states, n)
                    residuals.append(attn_end(h + 1, states))
                    states = lane_terms(residuals[h + 1])
                    flight["lead"] = spread_launch(states, 0)
                elif t == 3:
                    states = spread_land(states, 0, flight.pop("lead"))
                    for n in range(1, bits):
                        states = spread_stage(states, n)
                    following = contract(spread_end(states))
        before = (parts, carried)
        if h + 1 < chunks:
            hidden = activate(*before)
            state = ([hidden], [hidden])
            gather_step(state, 1)
            gots = summing[3] if summing is not None else ()
            (state[0][-1], state[1][-1]), (parts, gots) = after((state[0][-1], state[1][-1]), (following, gots))
            if summing is not None:
                summing = summing[:3] + (gots,)
            carried, _ = scatter_step(parts, None, 1)
    hidden = activate(*before)
    state = ([hidden], [hidden])
    for t in range(1, steps + 1):
        gather_step(state, t)
        if summing is not None:
            who, n, terms, gots = summing
            (state[0][-1], state[1][-1]), gots = after((state[0][-1], state[1][-1]), gots)
            terms = sum_land(terms, n, gots)
            if n + 1 < bits:
                summing = (who, n + 1, terms, sum_launch(terms, n + 1))
            else:
                finals[who] = deliver(who, sum_end(terms))
                summing = None
    if chunks > 1:
        (state[0][-1], state[1][-1]), finals[:-1] = after((state[0][-1], state[1][-1]), finals[:-1])
    states = down_terms(state)
    for n in range(bits):
        states = sum_stage(states, n)
    finals[chunks - 1] = deliver(chunks - 1, sum_end(states))
    final = swap_halves(jnp.concatenate(finals, axis=1))
    final = lax.dynamic_slice_in_dim(
        jnp.concatenate([final, final], axis=0), (planes - plane) % planes, planes, 0
    )
    layer_output = jnp.swapaxes(final, 0, 1).reshape(share, width)
    return (layer_output, kv_cache)


def solution(mesh):
    placed = (
        P("seq", None),
        P(),
        P(),
        P("seq", "mlp"),
        P("seq", None),
        P("seq", None),
        P("mlp", "seq"),
        P("seq", "mlp"),
        P("seq", "mlp"),
        P("mlp", "seq"),
        P("mlp"),
        P(),
        P(),
        P(),
        P(),
        P(),
    )
    return jax.shard_map(
        shards,
        mesh=mesh,
        in_specs=placed,
        out_specs=(P(("seq", "mlp"), None), P("seq", "mlp")),
        check_vma=False,
    )
```
